1024 devices in a mesh: gx: 64 (over z, core), gy: 16 (over x, y).
Axes of the slice: x: 4, y: 4, z: 32, core: 2. Of those that a mesh axis runs over, the one named last changes fastest.
Arguments:
- density: float32 [256, 128, 128], P('gx', 'gy'), may hold values from 0.9 to 1.1
- velocity: float32 [3, 256, 128, 128], P(None, 'gx', 'gy'), may hold values from -0.625 to 0.625
- fluid_mask: int32 [256, 128, 128], P('gx', 'gy'), may hold values 0 or 1
- unit_of_column: int32 [256, 128], P('gx', 'gy'), may hold values from 0 to 127
- radius_base: float32 [8192], P(('gx', 'gy')), may hold values from 0.5 to 2
Outputs:
- density_out: float32 [256, 128, 128], P('gx', 'gy')
- velocity_out: float32 [3, 256, 128, 128], P(None, 'gx', 'gy')
- radius_out: float32 [8192], P(('gx', 'gy'))
The draws below stay inside these ranges and needn't reach their ends.
All inputs are finite; a program needn't handle non-finite values. No bound on the sum of `fluid_mask` on one device may be relied on, other than what follows from the above.
Results may differ from the reference program's by a relative error of at most 0.0003.
Values sent between devices are 32-bit elements; how exact they have to be, the bound alone decides.
No kernel may reach another device: no remote copies, remote signals or barrier semaphores. Data moves between devices by JAX's collectives and lax.ppermute only.
A program may use at most 32 MiB of HBM per device.

```python
import math
import jax
import jax.numpy as jnp

CX = 4
NZ = 128
STEPS = 6
UNIT_DEV = 8
NX = 256
NY = 128
UNITS = 8192
N_GY = 16


def set_ends(values, rng, least, largest):
    dims = values.shape
    place = [jax.random.randint(jax.random.fold_in(rng, axis), (), 0, dims[axis]) for axis in range(len(dims))]
    values = values.at[tuple(place)].set(least)
    longest = dims.index(max(dims))
    place[longest] = (place[longest] + 1) % dims[longest]
    return values.at[tuple(place)].set(largest)


def levels(stream_key, shape, split, smallest, largest):
    level = 1.0
    for axis_at, blocks in split:
        steps = jax.random.uniform(jax.random.fold_in(jax.random.fold_in(stream_key, 6), axis_at), (blocks,), jnp.float32, smallest / len(split), largest / len(split))
        level = level * jnp.repeat(jnp.exp(steps), shape[axis_at] // blocks).reshape((-1,) + (1,) * (len(shape) - 1 - axis_at))
    return level


def gaussian(key, extent, spread, most, shards=(), held_as=jnp.bfloat16):
    drawn = spread * jax.random.normal(key, extent, jnp.float32)
    if shards:
        drawn = drawn * levels(key, extent, shards, -0.22, 0.18)
    return jnp.clip(drawn, -most, most).astype(held_as)


def setup_inputs(seed: int = 0) -> dict:
    keys = jax.random.split(jax.random.key(seed), 6)
    return {
        "density": jnp.clip(0.9 + 0.20000005 * jax.random.uniform(keys[0], (NX, NY, NZ), jnp.float32) ** levels(keys[0], (NX, NY, NZ), ((0, 64), (1, 16)), -0.2, 0.2), 0.9, 1.1),
        "velocity": gaussian(keys[1], (3, NX, NY, NZ), 0.04, 0.625, ((1, 64), (2, 16)), jnp.float32),
        "fluid_mask": set_ends((jax.random.randint(keys[2], (NX, NY, NZ), 0, 4) < 3).astype(jnp.int32), jax.random.fold_in(keys[2], 1), 0, 1),
        "unit_of_column": set_ends(jax.random.randint(keys[3], (NX, NY), 0, UNIT_DEV * N_GY), jax.random.fold_in(keys[3], 1), 0, (UNIT_DEV * N_GY) - 1).astype(jnp.int32),
        "radius_base": jnp.clip(jnp.exp(math.log(2.0) - 1.3862944 * jax.random.uniform(keys[4], (UNITS,), jnp.float32) ** levels(keys[4], (UNITS,), ((0, 1024),), -0.2, 0.2)), 0.5, 2.0),
    }


LATTICE = ((0, 0, 0), (1, 0, 0), (-1, 0, 0), (0, 1, 0), (0, -1, 0), (0, 0, 1), (0, 0, -1), (1, 1, 0), (-1, -1, 0), (1, -1, 0), (-1, 1, 0), (1, 0, 1), (-1, 0, -1), (1, 0, -1), (-1, 0, 1), (0, 1, 1), (0, -1, -1), (0, 1, -1), (0, -1, 1))
WEIGHTS = (1.0 / 3.0,) + (1.0 / 18.0,) * 6 + (1.0 / 36.0,) * 12
RELAX_RATE = 1.25
DRIVE_SCALE = 0.002


def reverse_of(direction):
    if direction == 0:
        return 0
    return direction + 1 if direction % 2 == 1 else direction - 1


def moments(populations, fluid_share):
    density_now = populations[0]
    momentum = [jnp.zeros_like(density_now) for component in range(3)]
    for direction in range(1, 19):
        density_now = density_now + populations[direction]
        for component in range(3):
            if LATTICE[direction][component] != 0:
                momentum[component] = momentum[component] + LATTICE[direction][component] * populations[direction]
    inverse = 1.0 / (density_now + 1.0 - fluid_share)
    return density_now, [moment * inverse for moment in momentum]


def equilibrium(density_now, velocity_now):
    speed_sq = velocity_now[0] * velocity_now[0] + velocity_now[1] * velocity_now[1] + velocity_now[2] * velocity_now[2]
    balance_terms = []
    for direction in range(19):
        projected = jnp.zeros_like(density_now)
        for component in range(3):
            if LATTICE[direction][component] != 0:
                projected = projected + LATTICE[direction][component] * velocity_now[component]
        balance_terms.append(WEIGHTS[direction] * density_now * (1.0 + 3.0 * projected + 4.5 * projected * projected - 1.5 * speed_sq))
    return jnp.stack(balance_terms)


def collide(populations, density_now, velocity_now, drive_field):
    balance = equilibrium(density_now, velocity_now)
    forcing = jnp.stack([3.0 * WEIGHTS[direction] * LATTICE[direction][2] * drive_field * density_now for direction in range(19)])
    return populations - RELAX_RATE * (populations - balance) + forcing


def stream(padded, mask_padded, collided, fluid_share):
    size_x, size_y, size_z = collided.shape[1:]
    read = []
    for direction in range(19):
        step_x, step_y, step_z = LATTICE[direction]
        source = padded[direction, 1 - step_x:1 - step_x + size_x, 1 - step_y:1 - step_y + size_y, 1 - step_z:1 - step_z + size_z]
        open_site = mask_padded[1 - step_x:1 - step_x + size_x, 1 - step_y:1 - step_y + size_y, 1 - step_z:1 - step_z + size_z]
        read.append(jnp.where(open_site > 0, source, collided[reverse_of(direction)]))
    return jnp.stack(read) * fluid_share


def wall_count(mask_padded, fluid_share):
    size_x, size_y, size_z = fluid_share.shape
    link_total = jnp.zeros_like(fluid_share)
    for direction in range(1, 19):
        step_x, step_y, step_z = LATTICE[direction]
        neighbour = mask_padded[1 + step_x:1 + step_x + size_x, 1 + step_y:1 + step_y + size_y, 1 + step_z:1 + step_z + size_z]
        link_total = link_total + (neighbour == 0).astype(jnp.float32)
    return link_total * fluid_share


def respond(base_radius, shear_sum, link_sum):
    return base_radius * (0.6 + 0.8 * jnp.tanh(100.0 * shear_sum / jnp.maximum(link_sum, 1.0)))


def reference(density, velocity, fluid_mask, unit_of_column, radius_base):
    fluid_share = fluid_mask.astype(jnp.float32)
    mask_padded = jnp.pad(fluid_mask, 1)
    link_count = wall_count(mask_padded, fluid_share)
    populations = equilibrium(density, [velocity[0], velocity[1], velocity[2]]) * fluid_share
    unit_global = ((jnp.arange(NX, dtype=jnp.int32) // CX)[:, None] * (UNIT_DEV * N_GY) + unit_of_column).astype(jnp.int32)
    radius_now = radius_base
    for step_index in range(STEPS):
        density_now, velocity_now = moments(populations, fluid_share)
        speed_sq = velocity_now[0] * velocity_now[0] + velocity_now[1] * velocity_now[1] + velocity_now[2] * velocity_now[2]
        shear_term = jnp.sum(link_count * speed_sq, axis=2)
        link_term = jnp.sum(link_count, axis=2)
        shear_sum = jax.ops.segment_sum(shear_term.reshape(-1), unit_global.reshape(-1), num_segments=UNITS)
        link_sum = jax.ops.segment_sum(link_term.reshape(-1), unit_global.reshape(-1), num_segments=UNITS)
        radius_site = radius_now[unit_global]
        drive_field = (DRIVE_SCALE * radius_site * radius_site)[:, :, None]
        collided = collide(populations, density_now, velocity_now, drive_field)
        padded = jnp.pad(collided, ((0, 0), (1, 1), (1, 1), (1, 1)))
        populations = stream(padded, mask_padded, collided, fluid_share)
        radius_now = respond(radius_base, shear_sum, link_sum)
    density_now, velocity_now = moments(populations, fluid_share)
    return density_now, jnp.stack(velocity_now), radius_now
```

```python
import functools

import jax
import jax.numpy as jnp
from jax import lax
from jax.experimental import pallas as pl
from jax.experimental.pallas import tpu as pltpu
from jax.sharding import Mesh
from jax.sharding import PartitionSpec as P

UNIT_DEV = 8
GX_GY = ("gx", "gy_0", "gy_1")
GY = ("gy_0", "gy_1")

LATTICE = (
    (0, 0, 0),
    (1, 0, 0),
    (-1, 0, 0),
    (0, 1, 0),
    (0, -1, 0),
    (0, 0, 1),
    (0, 0, -1),
    (1, 1, 0),
    (-1, -1, 0),
    (1, -1, 0),
    (-1, 1, 0),
    (1, 0, 1),
    (-1, 0, -1),
    (1, 0, -1),
    (-1, 0, 1),
    (0, 1, 1),
    (0, -1, -1),
    (0, 1, -1),
    (0, -1, 1),
)
PAIRS = tuple(range(1, 19, 2))
WEIGHTS = (1.0 / 3.0,) + (1.0 / 18.0,) * 6 + (1.0 / 36.0,) * 12
RELAX_RATE = 1.25
DRIVE_SCALE = 0.002
F32 = jnp.float32

TILE = 8
LANES = 128
PAD = 8
WIDE = 24
MID = 16


def opposite(direction):
    if direction == 0:
        return 0
    return direction + 1 if direction % 2 == 1 else direction - 1


def dot_c(direction, vector):
    total = None
    for c, v in zip(LATTICE[direction], vector):
        if c != 0:
            term = v if c > 0 else -v
            total = term if total is None else total + term
    return total


def moments(f, fluid):
    rho = f[0]
    momentum = [None, None, None]
    for i in PAIRS:
        rho = rho + (f[i] + f[i + 1])
        diff = f[i] - f[i + 1]
        for k in range(3):
            c = LATTICE[i][k]
            if c != 0:
                term = diff if c > 0 else -diff
                momentum[k] = term if momentum[k] is None else momentum[k] + term
    inverse = jnp.where(fluid, 1.0 / rho, 0.0)
    return jnp.where(fluid, rho, 0.0), [m * inverse for m in momentum]


def square(u):
    return u[0] * u[0] + u[1] * u[1] + u[2] * u[2]


def relaxed(f, rho, u, speed_sq, drive):
    rate = 1.0 if f is None else RELAX_RATE
    scaled = rate * rho
    even_base = scaled * (1.0 - 1.5 * speed_sq)
    force = drive * rho
    post = [None] * 19
    rest = WEIGHTS[0] * even_base
    post[0] = rest if f is None else rest + (1.0 - RELAX_RATE) * f[0]
    per_weight = {}
    for w in (WEIGHTS[1], WEIGHTS[7]):
        per_weight[w] = (w * even_base, (4.5 * w) * scaled, (3.0 * w) * scaled, (3.0 * w) * force)
    for i in PAIRS:
        base, quadratic, linear, push = per_weight[WEIGHTS[i]]
        cu = dot_c(i, u)
        even = base + quadratic * (cu * cu)
        odd = linear * cu
        if LATTICE[i][2] > 0:
            odd = odd + push
        elif LATTICE[i][2] < 0:
            odd = odd - push
        post[i] = even + odd
        post[i + 1] = even - odd
        if f is not None:
            post[i] = post[i] + (1.0 - RELAX_RATE) * f[i]
            post[i + 1] = post[i + 1] + (1.0 - RELAX_RATE) * f[i + 1]
    return post


def rolled(x, step):
    if step == 0:
        return x
    return pltpu.roll(x, step % LANES, axis=1)


def pulled(post_ref, column, row, bits):
    f = [post_ref[0, column, pl.ds(row, TILE), :]]
    for i in range(1, 19):
        cx, cy, cz = LATTICE[i]
        source = rolled(post_ref[i, column - cx, pl.ds(row - cy, TILE), :], cz)
        bounced = post_ref[opposite(i), column, pl.ds(row, TILE), :]
        f.append(jnp.where((bits & (1 << i)) != 0, source, bounced))
    return f


def drive_of(radius_row, unit):
    radius = jnp.take_along_axis(radius_row, unit.astype(jnp.int32), axis=1)
    return DRIVE_SCALE * radius * radius


def shear(links, speed_sq):
    return jnp.where(links > 0.0, links * speed_sq, 0.0)


def by_unit(column_values, unit):
    total = jnp.sum(column_values, axis=1, keepdims=True)
    lane = lax.broadcasted_iota(jnp.int32, (TILE, LANES), 1)
    return jnp.where(unit.astype(jnp.int32) == lane, total, 0.0)


def sublane_total(x):
    return jnp.broadcast_to(jnp.sum(x, axis=0, keepdims=True), (TILE, LANES))


def row_pick(rows):
    sub = lax.broadcasted_iota(jnp.int32, (TILE, LANES), 0)
    out = jnp.zeros((TILE, LANES), F32)
    for k, value in enumerate(rows):
        out = jnp.where(sub == k, value, out)
    return out


def every(tile, k):
    return jnp.broadcast_to(tile[k : k + 1, :], (TILE, LANES))


def send_all(ref, tile):
    for j in range(ref.shape[0]):
        ref[j] = tile


def sum_of(ref):
    parts = [ref[j] for j in range(ref.shape[0])]
    while len(parts) > 1:
        parts = [a + b for a, b in zip(parts[::2], parts[1::2])] + (
            [parts[-1]] if len(parts) % 2 else []
        )
    return parts[0]


def gather_kernel(density, velocity, mask, unit, out):
    for x in range(4):
        out[0, x] = jnp.where(mask[x] != 0, density[x], 0.0)
        for k in range(3):
            out[1 + k, x] = velocity[k, x]
        out[4, x] = unit[x]


def rows_kernel(low, own, high, left_out, right_out):
    for half, out in ((0, left_out), (1, right_out)):
        for k in range(5):
            for x in range(2):
                for part, ref in enumerate((low, own, high)):
                    out[k, x, pl.ds(part * TILE, TILE), :] = ref[k, 2 * half + x]


def base_kernel(own, left, right, out):
    sub = lax.broadcasted_iota(jnp.int32, (TILE, LANES), 0)
    tile = jnp.where(sub == 0, own[...], jnp.where(sub == 1, left[...], right[...]))
    send_all(out, jnp.where(sub < 3, tile, 0.0))


def first_kernel(
    edge_ref, halo_l, left, right, halo_r, base_in, f_l, f_r, bits_out, links_out, send, base_out, post, open_
):
    fields = (halo_l, left, right, halo_r)
    base = sum_of(base_in)
    base_out[...] = base
    radius = [every(base, 1), every(base, 0), every(base, 0), every(base, 2)]
    lane = lax.broadcasted_iota(jnp.int32, (TILE, LANES), 1)
    for part in range(4):
        inside = None
        if part == 0:
            inside = edge_ref[0]
        elif part == 3:
            inside = edge_ref[1]
        for x in range(2):
            column = 2 * part + x
            zero = jnp.zeros((TILE, LANES), jnp.int32)
            for k in range(3):
                open_[k, column, pl.ds(0, TILE), :] = zero
                open_[k, column, pl.ds(PAD + WIDE, TILE), :] = zero
            for t in range(WIDE // TILE):
                here = (fields[part][0, x, pl.ds(t * TILE, TILE), :] > 0.0).astype(jnp.int32)
                if inside is not None:
                    here = here * inside
                rows = pl.ds(PAD + t * TILE, TILE)
                open_[0, column, rows, :] = here
                open_[1, column, rows, :] = jnp.where(lane == 0, 0, pltpu.roll(here, 1, axis=1))
                open_[2, column, rows, :] = jnp.where(
                    lane == LANES - 1, 0, pltpu.roll(here, LANES - 1, axis=1)
                )
    for column in range(1, 7):
        part, x = divmod(column, 2)
        for t in range(WIDE // TILE):
            rows = pl.ds(t * TILE, TILE)
            rho = fields[part][0, x, rows, :]
            u = [fields[part][1 + k, x, rows, :] for k in range(3)]
            drive = drive_of(radius[part], fields[part][4, x, rows, :])
            values = relaxed(None, rho, u, square(u), drive)
            for i in range(19):
                post[i, column, pl.ds(PAD + t * TILE, TILE), :] = values[i]
    link_sum = shear_0 = shear_1 = jnp.zeros((TILE, LANES), F32)
    for column in range(1, 7):
        part, x = divmod(column, 2)
        for t in range(WIDE // TILE):
            row = PAD + t * TILE
            rows = pl.ds(t * TILE, TILE)
            bits = jnp.zeros((TILE, LANES), jnp.int32)
            count = jnp.zeros((TILE, LANES), jnp.int32)
            for i in range(1, 19):
                cx, cy, cz = LATTICE[i]
                seen = open_[cz % 3, column - cx, pl.ds(row - cy, TILE), :]
                count = count + seen
                bits = bits | (seen << i)
            bits_out[column - 1, rows, :] = bits
            if part not in (1, 2):
                continue
            f = pulled(post, column, row, bits)
            out = f_l if part == 1 else f_r
            for i in range(19):
                out[i, x, rows, :] = f[i]
            if t != 1:
                links_out[column - 2, rows, :] = jnp.zeros((TILE, LANES), F32)
                continue
            fluid = fields[part][0, x, rows, :] > 0.0
            links = jnp.where(fluid, (18 - count).astype(F32), 0.0)
            links_out[column - 2, rows, :] = links
            unit = fields[part][4, x, rows, :]
            u = [fields[part][1 + k, x, rows, :] for k in range(3)]
            link_sum = link_sum + by_unit(links, unit)
            shear_0 = shear_0 + by_unit(links * square(u), unit)
            _, u = moments(f, fluid)
            shear_1 = shear_1 + by_unit(links * square(u), unit)
    send_all(send, row_pick([sublane_total(s) for s in (shear_0, shear_1, link_sum)]))


def response_kernel(gathered, base, links_in, radius_out, links_out, *, first):
    totals = sum_of(gathered)
    links = every(totals, 2) if first else links_in[...]
    links_out[...] = links
    mean = 100.0 * totals / jnp.maximum(links, 1.0)
    radius_out[...] = every(base[...], 0) * (0.6 + 0.8 * jnp.tanh(mean))


def collide_from(parts, fields, radius, row_in_fields, columns, n_rows, post):
    for column in columns:
        part, x = divmod(column, 2)
        for t in range(n_rows // TILE):
            rows = pl.ds(t * TILE, TILE)
            near = pl.ds(row_in_fields + t * TILE, TILE)
            f = [parts[part][i, x, rows, :] for i in range(19)]
            rho, u = moments(f, fields[part][0, x, near, :] > 0.0)
            drive = drive_of(radius[part], fields[part][4, x, near, :])
            values = relaxed(f, rho, u, square(u), drive)
            for i in range(19):
                post[i, column, pl.ds(PAD + t * TILE, TILE), :] = values[i]


def two_steps_kernel(
    h_l, a, b, h_r, g_hl, g_a, g_b, g_hr, bits_in, links_in, rad, rad_l, rad_r, f_l, f_r, send, post_a, post_b, *, n_rows
):
    parts, fields = (h_l, a, b, h_r), (g_hl, g_a, g_b, g_hr)
    top = (WIDE - n_rows) // 2
    first = [every(r[...], 0) for r in (rad_l, rad, rad, rad_r)]
    second = [every(r[...], 1) for r in (rad_l, rad, rad, rad_r)]
    collide_from(parts, fields, first, top, range(8), n_rows, post_a)
    shear_a = shear_b = jnp.zeros((TILE, LANES), F32)
    skip = (n_rows - MID) // 2
    for column in range(1, 7):
        part, x = divmod(column, 2)
        for t in range(MID // TILE):
            near = pl.ds((WIDE - MID) // 2 + t * TILE, TILE)
            f = pulled(post_a, column, PAD + skip + t * TILE, bits_in[column - 1, near, :])
            rho, u = moments(f, fields[part][0, x, near, :] > 0.0)
            speed_sq = square(u)
            unit = fields[part][4, x, near, :]
            if part in (1, 2):
                shear_a = shear_a + by_unit(shear(links_in[column - 2, near, :], speed_sq), unit)
            values = relaxed(f, rho, u, speed_sq, drive_of(second[part], unit))
            for i in range(19):
                post_b[i, column, pl.ds(PAD + t * TILE, TILE), :] = values[i]
    for column in range(2, 6):
        part, x = divmod(column, 2)
        out = f_l if part == 1 else f_r
        for t in range(MID // TILE):
            near = pl.ds((WIDE - MID) // 2 + t * TILE, TILE)
            f = pulled(post_b, column, PAD + t * TILE, bits_in[column - 1, near, :])
            for i in range(19):
                out[i, x, pl.ds(t * TILE, TILE), :] = f[i]
            _, u = moments(f, fields[part][0, x, near, :] > 0.0)
            shear_b = shear_b + by_unit(
                shear(links_in[column - 2, near, :], square(u)), fields[part][4, x, near, :]
            )
    send_all(send, row_pick([sublane_total(s) for s in (shear_a, shear_b)]))


def last_kernel(
    h_l, a, b, h_r, g_hl, g_a, g_b, g_hr, bits_in, rad, rad_l, rad_r, density, velocity, post
):
    parts, fields = (h_l, a, b, h_r), (g_hl, g_a, g_b, g_hr)
    radius = [every(r[...], 0) for r in (rad_l, rad, rad, rad_r)]
    collide_from(parts, fields, radius, (WIDE - MID) // 2, range(1, 7), MID, post)
    own = pl.ds(TILE, TILE)
    for column in range(2, 6):
        part, x = divmod(column, 2)
        f = pulled(post, column, PAD + (MID - TILE) // 2, bits_in[column - 1, own, :])
        rho, u = moments(f, fields[part][0, x, own, :] > 0.0)
        density[column - 2] = rho
        for k in range(3):
            velocity[k, column - 2] = u[k]


def call(kernel, outs, scratch=(), scalars=0, mib=1):
    vmem = pl.BlockSpec(memory_space=pltpu.VMEM)
    smem = pl.BlockSpec(memory_space=pltpu.SMEM)

    def run(*args):
        args = args[:scalars] + tuple(
            pltpu.with_memory_space_constraint(a, pltpu.VMEM) for a in args[scalars:]
        )
        return pl.pallas_call(
            kernel,
            out_shape=[pltpu.VMEM(shape, dtype) for shape, dtype in outs],
            in_specs=[smem] * scalars + [vmem] * (len(args) - scalars),
            out_specs=[vmem] * len(outs),
            scratch_shapes=[pltpu.VMEM(shape, dtype) for shape, dtype in scratch],
            compiler_params=pltpu.CompilerParams(vmem_limit_bytes=mib << 20),
        )(*args)

    return run


def ring(low, high):
    count = lax.axis_size("gx")
    up = [(i, (i + 1) % count) for i in range(count)]
    down = [(target, source) for source, target in up]
    return lax.ppermute(high, "gx", up), lax.ppermute(low, "gx", down)


def per_device(density, velocity, fluid_mask, unit_of_column, radius_base):
    count = lax.axis_size(GY)
    place = lax.axis_index(GY)
    at_x = lax.axis_index("gx")
    edge = jnp.stack([at_x > 0, at_x < lax.axis_size("gx") - 1]).astype(jnp.int32)

    lane = lax.broadcasted_iota(jnp.int32, (TILE, LANES), 1)
    repeated = jnp.tile(radius_base, LANES // UNIT_DEV)[None, :]
    placed = jnp.where(lane // UNIT_DEV == place, repeated, 0.0)
    base_l, base_r = ring(placed, placed)
    (base_send,) = call(base_kernel, [((count, TILE, LANES), F32)])(placed, base_l, base_r)
    exchange = functools.partial(
        lax.all_to_all, axis_name=GY, split_axis=0, concat_axis=0, tiled=True
    )
    base_in = exchange(base_send)

    unit = jnp.broadcast_to(unit_of_column.astype(F32)[:, :, None], (4, TILE, LANES))
    (own,) = call(gather_kernel, [((5, 4, TILE, LANES), F32)])(density, velocity, fluid_mask, unit)
    forward = [(i, i + 1) for i in range(count - 1)]
    backward = [(target, source) for source, target in forward]
    low = lax.ppermute(own, GY, forward)
    high = lax.ppermute(own, GY, backward)
    pair = ((5, 2, WIDE, LANES), F32)
    g_l, g_r = call(rows_kernel, [pair, pair])(low, own, high)
    g_hl, g_hr = ring(g_l, g_r)
    fields = (g_hl, g_l, g_r, g_hr)

    def populations(rows):
        return ((19, 2, rows, LANES), F32)

    tile = ((TILE, LANES), F32)
    sends = ((count, TILE, LANES), F32)
    f_l, f_r, bits, links, send, base = call(
        first_kernel,
        [
            populations(WIDE),
            populations(WIDE),
            ((6, WIDE, LANES), jnp.int32),
            ((4, WIDE, LANES), F32),
            sends,
            tile,
        ],
        [((19, 8, WIDE + 2 * PAD, LANES), F32), ((3, 8, WIDE + 2 * PAD, LANES), jnp.int32)],
        scalars=1,
        mib=6,
    )(edge, *fields, base_in)

    link_tile = base
    for round_index in range(3):
        gathered = exchange(send)
        h_l, h_r = ring(f_l, f_r)
        rad, link_tile = call(
            functools.partial(response_kernel, first=round_index == 0), [tile, tile]
        )(gathered, base, link_tile)
        rad_l, rad_r = ring(rad, rad)
        parts = (h_l, f_l, f_r, h_r)
        if round_index < 2:
            rows = WIDE if round_index == 0 else MID
            f_l, f_r, send = call(
                functools.partial(two_steps_kernel, n_rows=rows),
                [populations(MID), populations(MID), sends],
                [
                    ((19, 8, rows + 2 * PAD, LANES), F32),
                    ((19, 8, MID + 2 * PAD, LANES), F32),
                ],
                mib=8,
            )(*parts, *fields, bits, links, rad, rad_l, rad_r)
    density_out, velocity_out = call(
        last_kernel,
        [((4, TILE, LANES), F32), ((3, 4, TILE, LANES), F32)],
        [((19, 8, MID + 2 * PAD, LANES), F32)],
        mib=4,
    )(*parts, *fields, bits, rad, rad_l, rad_r)
    own_radius = lax.dynamic_slice_in_dim(rad[1], place * UNIT_DEV, UNIT_DEV)
    return density_out, velocity_out, own_radius


def solution(mesh):
    finer = Mesh(mesh.devices.reshape(mesh.shape["gx"], 4, -1), ("gx", "gy_0", "gy_1"))
    placed = (P("gx", GY, None), P(None, "gx", GY, None), P("gx", GY, None), P("gx", GY), P(GX_GY))
    return jax.shard_map(
        per_device,
        mesh=finer,
        in_specs=placed,
        out_specs=(P("gx", GY, None), P(None, "gx", GY, None), P(GX_GY)),
        check_vma=False,
    )
```

```python
import functools

import jax
import jax.numpy as jnp
from jax import lax
from jax.experimental import pallas as pl
from jax.experimental.pallas import tpu as pltpu
from jax.sharding import Mesh
from jax.sharding import PartitionSpec as P


UNIT_DEV = 8
GX_GY = ("gx", "gy_0", "gy_1")
GY = ("gy_0", "gy_1")

LATTICE = (
    (0, 0, 0),
    (1, 0, 0),
    (-1, 0, 0),
    (0, 1, 0),
    (0, -1, 0),
    (0, 0, 1),
    (0, 0, -1),
    (1, 1, 0),
    (-1, -1, 0),
    (1, -1, 0),
    (-1, 1, 0),
    (1, 0, 1),
    (-1, 0, -1),
    (1, 0, -1),
    (-1, 0, 1),
    (0, 1, 1),
    (0, -1, -1),
    (0, 1, -1),
    (0, -1, 1),
)
PAIRS = tuple(range(1, 19, 2))
WEIGHTS = (1.0 / 3.0,) + (1.0 / 18.0,) * 6 + (1.0 / 36.0,) * 12
RELAX_RATE = 1.25
DRIVE_SCALE = 0.002
F32 = jnp.float32

TILE = 8
LANES = 128
PAD = 8
WIDE = 24
MID = 16


def opposite(direction):
    if direction == 0:
        return 0
    return direction + 1 if direction % 2 == 1 else direction - 1


def dot_c(direction, vector):
    total = None
    for c, v in zip(LATTICE[direction], vector):
        if c != 0:
            term = v if c > 0 else -v
            total = term if total is None else total + term
    return total


def moments(f, fluid):
    rho = f[0]
    momentum = [None, None, None]
    for i in PAIRS:
        rho = rho + (f[i] + f[i + 1])
        diff = f[i] - f[i + 1]
        for k in range(3):
            c = LATTICE[i][k]
            if c != 0:
                term = diff if c > 0 else -diff
                momentum[k] = term if momentum[k] is None else momentum[k] + term
    inverse = jnp.where(fluid, 1.0 / rho, 0.0)
    return jnp.where(fluid, rho, 0.0), [m * inverse for m in momentum]


def square(u):
    return u[0] * u[0] + u[1] * u[1] + u[2] * u[2]


def relaxed(f, rho, u, speed_sq, drive):
    rate = 1.0 if f is None else RELAX_RATE
    scaled = rate * rho
    even_base = scaled * (1.0 - 1.5 * speed_sq)
    force = drive * rho
    post = [None] * 19
    rest = WEIGHTS[0] * even_base
    post[0] = rest if f is None else rest + (1.0 - RELAX_RATE) * f[0]
    per_weight = {}
    for w in (WEIGHTS[1], WEIGHTS[7]):
        per_weight[w] = (w * even_base, (4.5 * w) * scaled, (3.0 * w) * scaled, (3.0 * w) * force)
    for i in PAIRS:
        base, quadratic, linear, push = per_weight[WEIGHTS[i]]
        cu = dot_c(i, u)
        even = base + quadratic * (cu * cu)
        odd = linear * cu
        if LATTICE[i][2] > 0:
            odd = odd + push
        elif LATTICE[i][2] < 0:
            odd = odd - push
        post[i] = even + odd
        post[i + 1] = even - odd
        if f is not None:
            post[i] = post[i] + (1.0 - RELAX_RATE) * f[i]
            post[i + 1] = post[i + 1] + (1.0 - RELAX_RATE) * f[i + 1]
    return post


def rolled(x, step):
    if step == 0:
        return x
    return pltpu.roll(x, step % LANES, axis=1)


def pulled(post_ref, column, row, bits):
    f = [post_ref[0, column, pl.ds(row, TILE), :]]
    for i in range(1, 19):
        cx, cy, cz = LATTICE[i]
        source = rolled(post_ref[i, column - cx, pl.ds(row - cy, TILE), :], cz)
        bounced = post_ref[opposite(i), column, pl.ds(row, TILE), :]
        f.append(jnp.where((bits & (1 << i)) != 0, source, bounced))
    return f


def drive_of(radius_row, unit):
    radius = jnp.take_along_axis(radius_row, unit.astype(jnp.int32), axis=1)
    return DRIVE_SCALE * radius * radius


def shear(links, speed_sq):
    return jnp.where(links > 0.0, links * speed_sq, 0.0)


def by_unit(column_values, unit):
    total = jnp.sum(column_values, axis=1, keepdims=True)
    lane = lax.broadcasted_iota(jnp.int32, (TILE, LANES), 1)
    return jnp.where(unit.astype(jnp.int32) == lane, total, 0.0)


def sublane_total(x):
    return jnp.broadcast_to(jnp.sum(x, axis=0, keepdims=True), (TILE, LANES))


def row_pick(rows):
    sub = lax.broadcasted_iota(jnp.int32, (TILE, LANES), 0)
    out = jnp.zeros((TILE, LANES), F32)
    for k, value in enumerate(rows):
        out = jnp.where(sub == k, value, out)
    return out


def every(tile, k):
    return jnp.broadcast_to(tile[k : k + 1, :], (TILE, LANES))


def send_all(ref, tile):
    for j in range(ref.shape[0]):
        ref[j] = tile


def sum_of(ref):
    parts = [ref[j] for j in range(ref.shape[0])]
    while len(parts) > 1:
        parts = [a + b for a, b in zip(parts[::2], parts[1::2])] + (
            [parts[-1]] if len(parts) % 2 else []
        )
    return parts[0]


def gather_kernel(place_ref, density, velocity, mask, unit, radius, out, placed):
    lane = lax.broadcasted_iota(jnp.int32, (TILE, LANES), 1)
    narrow = (TILE, TILE)
    diagonal = lax.broadcasted_iota(jnp.int32, narrow, 0) == lax.broadcasted_iota(jnp.int32, narrow, 1)
    for x in range(4):
        out[0, x] = jnp.where(mask[x] != 0, density[x], 0.0)
        for k in range(3):
            out[1 + k, x] = velocity[k, x]
        units = jnp.broadcast_to(unit[x : x + 1, :].astype(F32), narrow)
        column = jnp.sum(jnp.where(diagonal, units, 0.0), axis=1, keepdims=True)
        out[4, x] = jnp.broadcast_to(column, (TILE, LANES))
    radii = jnp.broadcast_to(radius[...], narrow)
    column = jnp.sum(jnp.where(diagonal, radii, 0.0), axis=1, keepdims=True)
    sub = lax.broadcasted_iota(jnp.int32, (TILE, LANES), 0)
    spread = jnp.where(lane == place_ref[0] * UNIT_DEV + sub, column, 0.0)
    placed[...] = sublane_total(spread)


def rows_kernel(low, own, high, left_out, right_out):
    for half, out in ((0, left_out), (1, right_out)):
        for k in range(5):
            for x in range(2):
                for part, ref in enumerate((low, own, high)):
                    out[k, x, pl.ds(part * TILE, TILE), :] = ref[k, 2 * half + x]


def base_kernel(own, left, right, out):
    sub = lax.broadcasted_iota(jnp.int32, (TILE, LANES), 0)
    tile = jnp.where(sub == 0, own[...], jnp.where(sub == 1, left[...], right[...]))
    send_all(out, jnp.where(sub < 3, tile, 0.0))


def first_kernel(
    edge_ref, halo_l, left, right, halo_r, base_in, f_l, f_r, bits_out, links_out, send, base_out, post, open_
):
    fields = (halo_l, left, right, halo_r)
    base = sum_of(base_in)
    base_out[...] = base
    radius = [every(base, 1), every(base, 0), every(base, 0), every(base, 2)]
    lane = lax.broadcasted_iota(jnp.int32, (TILE, LANES), 1)
    for part in range(4):
        inside = None
        if part == 0:
            inside = edge_ref[0]
        elif part == 3:
            inside = edge_ref[1]
        for x in range(2):
            column = 2 * part + x
            zero = jnp.zeros((TILE, LANES), jnp.int32)
            for k in range(3):
                open_[k, column, pl.ds(0, TILE), :] = zero
                open_[k, column, pl.ds(PAD + WIDE, TILE), :] = zero
            for t in range(WIDE // TILE):
                here = (fields[part][0, x, pl.ds(t * TILE, TILE), :] > 0.0).astype(jnp.int32)
                if inside is not None:
                    here = here * inside
                rows = pl.ds(PAD + t * TILE, TILE)
                open_[0, column, rows, :] = here
                open_[1, column, rows, :] = jnp.where(lane == 0, 0, pltpu.roll(here, 1, axis=1))
                open_[2, column, rows, :] = jnp.where(
                    lane == LANES - 1, 0, pltpu.roll(here, LANES - 1, axis=1)
                )
    for column in range(1, 7):
        part, x = divmod(column, 2)
        for t in range(WIDE // TILE):
            rows = pl.ds(t * TILE, TILE)
            rho = fields[part][0, x, rows, :]
            u = [fields[part][1 + k, x, rows, :] for k in range(3)]
            drive = drive_of(radius[part], fields[part][4, x, rows, :])
            values = relaxed(None, rho, u, square(u), drive)
            for i in range(19):
                post[i, column, pl.ds(PAD + t * TILE, TILE), :] = values[i]
    link_sum = shear_0 = shear_1 = jnp.zeros((TILE, LANES), F32)
    for column in range(1, 7):
        part, x = divmod(column, 2)
        for t in range(WIDE // TILE):
            row = PAD + t * TILE
            rows = pl.ds(t * TILE, TILE)
            bits = jnp.zeros((TILE, LANES), jnp.int32)
            count = jnp.zeros((TILE, LANES), jnp.int32)
            for i in range(1, 19):
                cx, cy, cz = LATTICE[i]
                seen = open_[cz % 3, column - cx, pl.ds(row - cy, TILE), :]
                count = count + seen
                bits = bits | (seen << i)
            bits_out[column - 1, rows, :] = bits
            if part not in (1, 2):
                continue
            f = pulled(post, column, row, bits)
            out = f_l if part == 1 else f_r
            for i in range(19):
                out[i, x, rows, :] = f[i]
            if t != 1:
                links_out[column - 2, rows, :] = jnp.zeros((TILE, LANES), F32)
                continue
            fluid = fields[part][0, x, rows, :] > 0.0
            links = jnp.where(fluid, (18 - count).astype(F32), 0.0)
            links_out[column - 2, rows, :] = links
            unit = fields[part][4, x, rows, :]
            u = [fields[part][1 + k, x, rows, :] for k in range(3)]
            link_sum = link_sum + by_unit(links, unit)
            shear_0 = shear_0 + by_unit(links * square(u), unit)
            _, u = moments(f, fluid)
            shear_1 = shear_1 + by_unit(links * square(u), unit)
    send_all(send, row_pick([sublane_total(s) for s in (shear_0, shear_1, link_sum)]))


def response_kernel(gathered, base, links_in, radius_out, links_out=None):
    totals = sum_of(gathered)
    if links_out is None:
        links = links_in[...]
    else:
        links = every(totals, 2)
        links_out[...] = links
    mean = 100.0 * totals / jnp.maximum(links, 1.0)
    radius_out[...] = every(base[...], 0) * (0.6 + 0.8 * jnp.tanh(mean))


def collide_from(parts, fields, radius, row_in_fields, columns, n_rows, post):
    for column in columns:
        part, x = divmod(column, 2)
        for t in range(n_rows // TILE):
            rows = pl.ds(t * TILE, TILE)
            near = pl.ds(row_in_fields + t * TILE, TILE)
            f = [parts[part][i, x, rows, :] for i in range(19)]
            rho, u = moments(f, fields[part][0, x, near, :] > 0.0)
            drive = drive_of(radius[part], fields[part][4, x, near, :])
            values = relaxed(f, rho, u, square(u), drive)
            for i in range(19):
                post[i, column, pl.ds(PAD + t * TILE, TILE), :] = values[i]


def two_steps_kernel(
    h_l, a, b, h_r, g_hl, g_a, g_b, g_hr, bits_in, links_in, rad, rad_l, rad_r, f_l, f_r, send, post_a, post_b, *, n_rows
):
    parts, fields = (h_l, a, b, h_r), (g_hl, g_a, g_b, g_hr)
    top = (WIDE - n_rows) // 2
    first = [every(r[...], 0) for r in (rad_l, rad, rad, rad_r)]
    second = [every(r[...], 1) for r in (rad_l, rad, rad, rad_r)]
    collide_from(parts, fields, first, top, range(8), n_rows, post_a)
    shear_a = shear_b = jnp.zeros((TILE, LANES), F32)
    skip = (n_rows - MID) // 2
    for column in range(1, 7):
        part, x = divmod(column, 2)
        for t in range(MID // TILE):
            near = pl.ds((WIDE - MID) // 2 + t * TILE, TILE)
            f = pulled(post_a, column, PAD + skip + t * TILE, bits_in[column - 1, near, :])
            rho, u = moments(f, fields[part][0, x, near, :] > 0.0)
            speed_sq = square(u)
            unit = fields[part][4, x, near, :]
            if part in (1, 2):
                shear_a = shear_a + by_unit(shear(links_in[column - 2, near, :], speed_sq), unit)
            values = relaxed(f, rho, u, speed_sq, drive_of(second[part], unit))
            for i in range(19):
                post_b[i, column, pl.ds(PAD + t * TILE, TILE), :] = values[i]
    for column in range(2, 6):
        part, x = divmod(column, 2)
        out = f_l if part == 1 else f_r
        for t in range(MID // TILE):
            near = pl.ds((WIDE - MID) // 2 + t * TILE, TILE)
            f = pulled(post_b, column, PAD + t * TILE, bits_in[column - 1, near, :])
            for i in range(19):
                out[i, x, pl.ds(t * TILE, TILE), :] = f[i]
            _, u = moments(f, fields[part][0, x, near, :] > 0.0)
            shear_b = shear_b + by_unit(
                shear(links_in[column - 2, near, :], square(u)), fields[part][4, x, near, :]
            )
    send_all(send, row_pick([sublane_total(s) for s in (shear_a, shear_b)]))


def last_kernel(
    h_l, a, b, h_r, g_hl, g_a, g_b, g_hr, bits_in, rad, rad_l, rad_r, density, velocity, post
):
    parts, fields = (h_l, a, b, h_r), (g_hl, g_a, g_b, g_hr)
    radius = [every(r[...], 0) for r in (rad_l, rad, rad, rad_r)]
    collide_from(parts, fields, radius, (WIDE - MID) // 2, range(1, 7), MID, post)
    own = pl.ds(TILE, TILE)
    for column in range(2, 6):
        part, x = divmod(column, 2)
        f = pulled(post, column, PAD + (MID - TILE) // 2, bits_in[column - 1, own, :])
        rho, u = moments(f, fields[part][0, x, own, :] > 0.0)
        density[column - 2] = rho
        for k in range(3):
            velocity[k, column - 2] = u[k]


def call(kernel, outs, scratch=(), scalars=0, mib=1, plain_in=False, plain_out=False):
    vmem = pl.BlockSpec(memory_space=pltpu.VMEM)
    smem = pl.BlockSpec(memory_space=pltpu.SMEM)

    def run(*args):
        space = pltpu.HBM if plain_in else pltpu.VMEM
        args = args[:scalars] + tuple(
            pltpu.with_memory_space_constraint(a, space) for a in args[scalars:]
        )
        held = jax.ShapeDtypeStruct if plain_out else pltpu.VMEM
        return pl.pallas_call(
            kernel,
            out_shape=[held(shape, dtype) for shape, dtype in outs],
            in_specs=[smem] * scalars + [vmem] * (len(args) - scalars),
            out_specs=[vmem] * len(outs),
            scratch_shapes=[pltpu.VMEM(shape, dtype) for shape, dtype in scratch],
            compiler_params=pltpu.CompilerParams(vmem_limit_bytes=mib << 20),
        )(*args)

    return run


def step_all(density, velocity, fluid_mask, unit_of_column, radius_base):
    count = lax.axis_size(GY)
    place = lax.axis_index(GY)
    at_x = lax.axis_index("gx")
    edge = jnp.stack([at_x > 0, at_x < lax.axis_size("gx") - 1]).astype(jnp.int32)
    tile = ((TILE, LANES), F32)
    sends = ((count, TILE, LANES), F32)

    def ring(low, high):
        size = lax.axis_size("gx")
        up = [(i, (i + 1) % size) for i in range(size)]
        down = [(target, source) for source, target in up]
        return lax.ppermute(high, "gx", up), lax.ppermute(low, "gx", down)

    def exchange(blocks):
        return lax.all_to_all(blocks, GY, split_axis=0, concat_axis=0, tiled=True)

    own, placed = call(
        gather_kernel, [((5, 4, TILE, LANES), F32), tile], scalars=1, plain_in=True
    )(place.reshape(1), density, velocity, fluid_mask, unit_of_column, radius_base.reshape(1, -1))

    base_l, base_r = ring(placed, placed)
    (base_send,) = call(base_kernel, [sends])(placed, base_l, base_r)
    base_in = exchange(base_send)

    forward = [(i, i + 1) for i in range(count - 1)]
    backward = [(target, source) for source, target in forward]
    low = lax.ppermute(own, GY, forward)
    high = lax.ppermute(own, GY, backward)
    pair = ((5, 2, WIDE, LANES), F32)
    g_l, g_r = call(rows_kernel, [pair, pair])(low, own, high)
    g_hl, g_hr = ring(g_l, g_r)
    fields = (g_hl, g_l, g_r, g_hr)

    def populations(rows):
        return ((19, 2, rows, LANES), F32)

    f_l, f_r, bits, links, send, base = call(
        first_kernel,
        [
            populations(WIDE),
            populations(WIDE),
            ((6, WIDE, LANES), jnp.int32),
            ((4, WIDE, LANES), F32),
            sends,
            tile,
        ],
        [((19, 8, WIDE + 2 * PAD, LANES), F32), ((3, 8, WIDE + 2 * PAD, LANES), jnp.int32)],
        scalars=1,
        mib=6,
    )(edge, *fields, base_in)

    for turn in range(3):
        gathered = exchange(send)
        h_l, h_r = ring(f_l, f_r)
        if turn == 0:
            rad, link_tile = call(response_kernel, [tile, tile])(gathered, base, base)
        else:
            (rad,) = call(response_kernel, [tile])(gathered, base, link_tile)
        rad_l, rad_r = ring(rad, rad)
        parts = (h_l, f_l, f_r, h_r)
        if turn < 2:
            rows = WIDE if turn == 0 else MID
            f_l, f_r, send = call(
                functools.partial(two_steps_kernel, n_rows=rows),
                [populations(MID), populations(MID), sends],
                [
                    ((19, 8, rows + 2 * PAD, LANES), F32),
                    ((19, 8, MID + 2 * PAD, LANES), F32),
                ],
                mib=8,
            )(*parts, *fields, bits, links, rad, rad_l, rad_r)
    density_out, velocity_out = call(
        last_kernel,
        [((4, TILE, LANES), F32), ((3, 4, TILE, LANES), F32)],
        [((19, 8, MID + 2 * PAD, LANES), F32)],
        mib=4,
        plain_out=True,
    )(*parts, *fields, bits, rad, rad_l, rad_r)
    own_radius = lax.dynamic_slice_in_dim(rad[1], place * UNIT_DEV, UNIT_DEV)
    return density_out, velocity_out, own_radius


def solution(mesh):
    finer = Mesh(mesh.devices.reshape(mesh.shape["gx"], 4, -1), ("gx", "gy_0", "gy_1"))
    placed = (P("gx", GY, None), P(None, "gx", GY, None), P("gx", GY, None), P("gx", GY), P(GX_GY))
    return jax.shard_map(
        step_all,
        mesh=finer,
        in_specs=placed,
        out_specs=(P("gx", GY, None), P(None, "gx", GY, None), P(GX_GY)),
        check_vma=False,
    )
```

```python
import functools

import jax
import jax.numpy as jnp
from jax import lax
from jax.experimental import pallas as pl
from jax.experimental.pallas import tpu as pltpu
from jax.sharding import Mesh
from jax.sharding import PartitionSpec as P


UNIT_DEV = 8
GX_GY = ("gx", "gy_0", "gy_1")
GY = ("gy_0", "gy_1")

LATTICE = (
    (0, 0, 0),
    (1, 0, 0),
    (-1, 0, 0),
    (0, 1, 0),
    (0, -1, 0),
    (0, 0, 1),
    (0, 0, -1),
    (1, 1, 0),
    (-1, -1, 0),
    (1, -1, 0),
    (-1, 1, 0),
    (1, 0, 1),
    (-1, 0, -1),
    (1, 0, -1),
    (-1, 0, 1),
    (0, 1, 1),
    (0, -1, -1),
    (0, 1, -1),
    (0, -1, 1),
)
PAIRS = tuple(range(1, 19, 2))
WEIGHTS = (1.0 / 3.0,) + (1.0 / 18.0,) * 6 + (1.0 / 36.0,) * 12
RELAX_RATE = 1.25
DRIVE_SCALE = 0.002
F32 = jnp.float32

TILE = 8
LANES = 128
PAD = 8
WIDE = 24
MID = 16
BASE_ROW = 5 * 2 * WIDE
TOWARD = {side: tuple(i for i in range(19) if LATTICE[i][0] == side) for side in (-1, 1)}
FAR = 9


def opposite(direction):
    if direction == 0:
        return 0
    return direction + 1 if direction % 2 == 1 else direction - 1


def dot_c(direction, vector):
    total = None
    for c, v in zip(LATTICE[direction], vector):
        if c != 0:
            term = v if c > 0 else -v
            total = term if total is None else total + term
    return total


def moments(f, fluid):
    rho = f[0]
    momentum = [None, None, None]
    for i in PAIRS:
        rho = rho + (f[i] + f[i + 1])
        diff = f[i] - f[i + 1]
        for k in range(3):
            c = LATTICE[i][k]
            if c != 0:
                term = diff if c > 0 else -diff
                momentum[k] = term if momentum[k] is None else momentum[k] + term
    inverse = jnp.where(fluid, 1.0 / rho, 0.0)
    return jnp.where(fluid, rho, 0.0), [m * inverse for m in momentum]


def square(u):
    return u[0] * u[0] + u[1] * u[1] + u[2] * u[2]


def relaxed(f, rho, u, speed_sq, drive):
    rate = 1.0 if f is None else RELAX_RATE
    scaled = rate * rho
    even_base = scaled * (1.0 - 1.5 * speed_sq)
    force = drive * rho
    post = [None] * 19
    rest = WEIGHTS[0] * even_base
    post[0] = rest if f is None else rest + (1.0 - RELAX_RATE) * f[0]
    per_weight = {}
    for w in (WEIGHTS[1], WEIGHTS[7]):
        per_weight[w] = (w * even_base, (4.5 * w) * scaled, (3.0 * w) * scaled, (3.0 * w) * force)
    for i in PAIRS:
        base, quadratic, linear, push = per_weight[WEIGHTS[i]]
        cu = dot_c(i, u)
        even = base + quadratic * (cu * cu)
        odd = linear * cu
        if LATTICE[i][2] > 0:
            odd = odd + push
        elif LATTICE[i][2] < 0:
            odd = odd - push
        post[i] = even + odd
        post[i + 1] = even - odd
        if f is not None:
            post[i] = post[i] + (1.0 - RELAX_RATE) * f[i]
            post[i + 1] = post[i + 1] + (1.0 - RELAX_RATE) * f[i + 1]
    return post


def relaxed_some(directions, f, rho, u, drive):
    scaled = RELAX_RATE * rho
    base = scaled * (1.0 - 1.5 * square(u))
    force = drive * rho
    post = []
    for i, population in zip(directions, f):
        cu = dot_c(i, u)
        value = base + scaled * (4.5 * (cu * cu) + 3.0 * cu)
        if LATTICE[i][2] != 0:
            value = value + (3.0 * LATTICE[i][2]) * force
        post.append(WEIGHTS[i] * value + (1.0 - RELAX_RATE) * population)
    return post


def field(ref, k, x, row):
    return ref[pl.ds((2 * k + x) * WIDE + row, TILE), :]


def put_all(out, rows, f):
    for i in range(19):
        out[i, rows, :] = f[i]


def put_far(out, first, rows, side, f, rho, u):
    values = [f[i] for i in TOWARD[side]] + [rho] + list(u)
    for n, value in enumerate(values):
        out[first + n, rows, :] = value


def collide_far(halo, first, side, field_ref, x, row_in_fields, radius, column, n_rows, post):
    for t in range(n_rows // TILE):
        rows = pl.ds(t * TILE, TILE)
        f = [halo[first + n, rows, :] for n in range(5)]
        rho = halo[first + 5, rows, :]
        u = [halo[first + 6 + k, rows, :] for k in range(3)]
        drive = drive_of(radius, field(field_ref, 4, x, row_in_fields + t * TILE))
        values = relaxed_some(TOWARD[side], f, rho, u, drive)
        for i, value in zip(TOWARD[side], values):
            post[i, column, pl.ds(PAD + t * TILE, TILE), :] = value


def rolled(x, step):
    if step == 0:
        return x
    return pltpu.roll(x, step % LANES, axis=1)


def pulled(post_ref, column, row, bits):
    f = [post_ref[0, column, pl.ds(row, TILE), :]]
    for i in range(1, 19):
        cx, cy, cz = LATTICE[i]
        source = rolled(post_ref[i, column - cx, pl.ds(row - cy, TILE), :], cz)
        bounced = post_ref[opposite(i), column, pl.ds(row, TILE), :]
        f.append(jnp.where((bits & (1 << i)) != 0, source, bounced))
    return f


def drive_of(radius_row, unit):
    radius = jnp.take_along_axis(radius_row, unit.astype(jnp.int32), axis=1)
    return DRIVE_SCALE * radius * radius


def shear(links, speed_sq):
    return jnp.where(links > 0.0, links * speed_sq, 0.0)


def by_unit(column_values, unit):
    total = jnp.sum(column_values, axis=1, keepdims=True)
    lane = lax.broadcasted_iota(jnp.int32, (TILE, LANES), 1)
    return jnp.where(unit.astype(jnp.int32) == lane, total, 0.0)


def sublane_total(x):
    return jnp.broadcast_to(jnp.sum(x, axis=0, keepdims=True), (TILE, LANES))


def row_pick(rows):
    sub = lax.broadcasted_iota(jnp.int32, (TILE, LANES), 0)
    out = jnp.zeros((TILE, LANES), F32)
    for k, value in enumerate(rows):
        out = jnp.where(sub == k, value, out)
    return out


def every(tile, k):
    return jnp.broadcast_to(tile[k : k + 1, :], (TILE, LANES))


def send_all(ref, tile):
    for j in range(ref.shape[0]):
        ref[j] = tile


def sum_of(ref):
    parts = [ref[j] for j in range(ref.shape[0])]
    while len(parts) > 1:
        parts = [a + b for a, b in zip(parts[::2], parts[1::2])] + (
            [parts[-1]] if len(parts) % 2 else []
        )
    return parts[0]


def gather_kernel(place_ref, density, velocity, mask, unit, radius, out, send):
    lane = lax.broadcasted_iota(jnp.int32, (TILE, LANES), 1)
    narrow = (TILE, TILE)
    diagonal = lax.broadcasted_iota(jnp.int32, narrow, 0) == lax.broadcasted_iota(jnp.int32, narrow, 1)
    for x in range(4):
        out[0, x] = jnp.where(mask[x] != 0, density[x], 0.0)
        for k in range(3):
            out[1 + k, x] = velocity[k, x]
        units = jnp.broadcast_to(unit[x : x + 1, :].astype(F32), narrow)
        column = jnp.sum(jnp.where(diagonal, units, 0.0), axis=1, keepdims=True)
        out[4, x] = jnp.broadcast_to(column, (TILE, LANES))
    radii = jnp.broadcast_to(radius[...], narrow)
    column = jnp.sum(jnp.where(diagonal, radii, 0.0), axis=1, keepdims=True)
    sub = lax.broadcasted_iota(jnp.int32, (TILE, LANES), 0)
    spread = jnp.where(lane == place_ref[0] * UNIT_DEV + sub, column, 0.0)
    send_all(send, sublane_total(spread))


def rows_kernel(low, own, high, base_in, left_out, right_out):
    base = sum_of(base_in)
    for half, out in ((0, left_out), (1, right_out)):
        for k in range(5):
            for x in range(2):
                for part, ref in enumerate((low, own, high)):
                    row = (2 * k + x) * WIDE + part * TILE
                    out[pl.ds(row, TILE), :] = ref[k, 2 * half + x]
        out[pl.ds(BASE_ROW, TILE), :] = base


def first_kernel(
    edge_ref, halo_l, left, right, halo_r, f_l, f_r, send_l, send_r, bits_out, links_out, send, base_out, post, open_
):
    fields = (halo_l, left, right, halo_r)
    radius = [ref[pl.ds(BASE_ROW, TILE), :] for ref in fields]
    base_out[...] = radius[1]
    lane = lax.broadcasted_iota(jnp.int32, (TILE, LANES), 1)
    for part in range(4):
        inside = None
        if part == 0:
            inside = edge_ref[0]
        elif part == 3:
            inside = edge_ref[1]
        for x in range(2):
            column = 2 * part + x
            zero = jnp.zeros((TILE, LANES), jnp.int32)
            for k in range(3):
                open_[k, column, pl.ds(0, TILE), :] = zero
                open_[k, column, pl.ds(PAD + WIDE, TILE), :] = zero
            for t in range(WIDE // TILE):
                here = (field(fields[part], 0, x, t * TILE) > 0.0).astype(jnp.int32)
                if inside is not None:
                    here = here * inside
                rows = pl.ds(PAD + t * TILE, TILE)
                open_[0, column, rows, :] = here
                open_[1, column, rows, :] = jnp.where(lane == 0, 0, pltpu.roll(here, 1, axis=1))
                open_[2, column, rows, :] = jnp.where(
                    lane == LANES - 1, 0, pltpu.roll(here, LANES - 1, axis=1)
                )
    for column in range(1, 7):
        part, x = divmod(column, 2)
        for t in range(WIDE // TILE):
            rho = field(fields[part], 0, x, t * TILE)
            u = [field(fields[part], 1 + k, x, t * TILE) for k in range(3)]
            drive = drive_of(radius[part], field(fields[part], 4, x, t * TILE))
            values = relaxed(None, rho, u, square(u), drive)
            for i in range(19):
                post[i, column, pl.ds(PAD + t * TILE, TILE), :] = values[i]
    link_sum = shear_0 = shear_1 = jnp.zeros((TILE, LANES), F32)
    for column in range(1, 7):
        part, x = divmod(column, 2)
        for t in range(WIDE // TILE):
            row = PAD + t * TILE
            rows = pl.ds(t * TILE, TILE)
            bits = jnp.zeros((TILE, LANES), jnp.int32)
            count = jnp.zeros((TILE, LANES), jnp.int32)
            for i in range(1, 19):
                cx, cy, cz = LATTICE[i]
                seen = open_[cz % 3, column - cx, pl.ds(row - cy, TILE), :]
                count = count + seen
                bits = bits | (seen << i)
            bits_out[column - 1, rows, :] = bits
            if part not in (1, 2):
                continue
            f = pulled(post, column, row, bits)
            out = f_l if part == 1 else f_r
            for i in range(19):
                out[i, x, rows, :] = f[i]
            fluid = field(fields[part], 0, x, t * TILE) > 0.0
            if t == 1 or column in (3, 4):
                rho, u = moments(f, fluid)
            if column == 2:
                put_all(send_l, rows, f)
            elif column == 3:
                put_far(send_l, 19, rows, -1, f, rho, u)
            elif column == 4:
                put_far(send_r, 19, rows, 1, f, rho, u)
            else:
                put_all(send_r, rows, f)
            if t != 1:
                links_out[column - 2, rows, :] = jnp.zeros((TILE, LANES), F32)
                continue
            links = jnp.where(fluid, (18 - count).astype(F32), 0.0)
            links_out[column - 2, rows, :] = links
            unit = field(fields[part], 4, x, t * TILE)
            start = [field(fields[part], 1 + k, x, t * TILE) for k in range(3)]
            link_sum = link_sum + by_unit(links, unit)
            shear_0 = shear_0 + by_unit(links * square(start), unit)
            shear_1 = shear_1 + by_unit(links * square(u), unit)
    send_all(send, row_pick([sublane_total(s) for s in (shear_0, shear_1, link_sum)]))


def response_kernel(gathered, base, links_in, radius_out, links_out=None):
    totals = sum_of(gathered)
    if links_out is None:
        links = links_in[...]
    else:
        links = every(totals, 2)
        links_out[...] = links
    mean = 100.0 * totals / jnp.maximum(links, 1.0)
    radius_out[...] = every(base[...], 0) * (0.6 + 0.8 * jnp.tanh(mean))


def collide_all(populations, column, fields, radius, row_in_fields, n_rows, post):
    part, x = divmod(column, 2)
    for t in range(n_rows // TILE):
        rows = pl.ds(t * TILE, TILE)
        near = row_in_fields + t * TILE
        f = [populations(i, rows) for i in range(19)]
        rho, u = moments(f, field(fields[part], 0, x, near) > 0.0)
        drive = drive_of(radius[part], field(fields[part], 4, x, near))
        values = relaxed(f, rho, u, square(u), drive)
        for i in range(19):
            post[i, column, pl.ds(PAD + t * TILE, TILE), :] = values[i]


def in_pair(ref, x):
    return lambda i, rows: ref[i, x, rows, :]


def in_halo(ref):
    return lambda i, rows: ref[i, rows, :]


def two_steps_kernel(
    h_l, a, b, h_r, g_hl, g_a, g_b, g_hr, bits_in, links_in, rad, rad_l, rad_r,
    f_l, f_r, send_l, send_r, send, post_a, post_b, *, n_rows, last_halo,
):
    fields = (g_hl, g_a, g_b, g_hr)
    top = (WIDE - n_rows) // 2
    first = [every(r[...], 0) for r in (rad_l, rad, rad, rad_r)]
    second = [every(r[...], 1) for r in (rad_l, rad, rad, rad_r)]
    for column in range(2, 6):
        source = in_pair(a if column < 4 else b, column % 2)
        collide_all(source, column, fields, first, top, n_rows, post_a)
    collide_all(in_halo(h_l), 1, fields, first, top, n_rows, post_a)
    collide_all(in_halo(h_r), 6, fields, first, top, n_rows, post_a)
    collide_far(h_l, 19, 1, g_hl, 0, top, first[0], 0, n_rows, post_a)
    collide_far(h_r, 19, -1, g_hr, 1, top, first[3], 7, n_rows, post_a)
    shear_a = shear_b = jnp.zeros((TILE, LANES), F32)
    skip = (n_rows - MID) // 2
    for column in range(1, 7):
        part, x = divmod(column, 2)
        for t in range(MID // TILE):
            row = (WIDE - MID) // 2 + t * TILE
            near = pl.ds(row, TILE)
            f = pulled(post_a, column, PAD + skip + t * TILE, bits_in[column - 1, near, :])
            rho, u = moments(f, field(fields[part], 0, x, row) > 0.0)
            speed_sq = square(u)
            unit = field(fields[part], 4, x, row)
            if part in (1, 2):
                shear_a = shear_a + by_unit(shear(links_in[column - 2, near, :], speed_sq), unit)
            values = relaxed(f, rho, u, speed_sq, drive_of(second[part], unit))
            for i in range(19):
                post_b[i, column, pl.ds(PAD + t * TILE, TILE), :] = values[i]
    for column in range(2, 6):
        part, x = divmod(column, 2)
        out = f_l if part == 1 else f_r
        for t in range(MID // TILE):
            row = (WIDE - MID) // 2 + t * TILE
            near = pl.ds(row, TILE)
            rows = pl.ds(t * TILE, TILE)
            f = pulled(post_b, column, PAD + t * TILE, bits_in[column - 1, near, :])
            for i in range(19):
                out[i, x, rows, :] = f[i]
            rho, u = moments(f, field(fields[part], 0, x, row) > 0.0)
            if last_halo:
                if column == 2:
                    put_far(send_l, 0, rows, -1, f, rho, u)
                elif column == 5:
                    put_far(send_r, 0, rows, 1, f, rho, u)
            elif column == 2:
                put_all(send_l, rows, f)
            elif column == 3:
                put_far(send_l, 19, rows, -1, f, rho, u)
            elif column == 4:
                put_far(send_r, 19, rows, 1, f, rho, u)
            else:
                put_all(send_r, rows, f)
            shear_b = shear_b + by_unit(
                shear(links_in[column - 2, near, :], square(u)), field(fields[part], 4, x, row)
            )
    send_all(send, row_pick([sublane_total(s) for s in (shear_a, shear_b)]))


def last_kernel(
    h_l, a, b, h_r, g_hl, g_a, g_b, g_hr, bits_in, rad, rad_l, rad_r, density, velocity, post
):
    fields = (g_hl, g_a, g_b, g_hr)
    radius = [every(r[...], 0) for r in (rad_l, rad, rad, rad_r)]
    top = (WIDE - MID) // 2
    for column in range(2, 6):
        source = in_pair(a if column < 4 else b, column % 2)
        collide_all(source, column, fields, radius, top, MID, post)
    collide_far(h_l, 0, 1, g_hl, 1, top, radius[0], 1, MID, post)
    collide_far(h_r, 0, -1, g_hr, 0, top, radius[3], 6, MID, post)
    own = pl.ds(TILE, TILE)
    for column in range(2, 6):
        part, x = divmod(column, 2)
        f = pulled(post, column, PAD + (MID - TILE) // 2, bits_in[column - 1, own, :])
        rho, u = moments(f, field(fields[part], 0, x, TILE) > 0.0)
        density[column - 2] = rho
        for k in range(3):
            velocity[k, column - 2] = u[k]


def call(kernel, outs, scratch=(), scalars=0, mib=1, plain_in=False, plain_out=False):
    vmem = pl.BlockSpec(memory_space=pltpu.VMEM)
    smem = pl.BlockSpec(memory_space=pltpu.SMEM)

    def run(*args):
        space = pltpu.HBM if plain_in else pltpu.VMEM
        args = args[:scalars] + tuple(
            pltpu.with_memory_space_constraint(a, space) for a in args[scalars:]
        )
        held = jax.ShapeDtypeStruct if plain_out else pltpu.VMEM
        return pl.pallas_call(
            kernel,
            out_shape=[held(shape, dtype) for shape, dtype in outs],
            in_specs=[smem] * scalars + [vmem] * (len(args) - scalars),
            out_specs=[vmem] * len(outs),
            scratch_shapes=[pltpu.VMEM(shape, dtype) for shape, dtype in scratch],
            compiler_params=pltpu.CompilerParams(vmem_limit_bytes=mib << 20),
        )(*args)

    return run


def step_all(density, velocity, fluid_mask, unit_of_column, radius_base):
    count = lax.axis_size(GY)
    place = lax.axis_index(GY)
    at_x = lax.axis_index("gx")
    edge = jnp.stack([at_x > 0, at_x < lax.axis_size("gx") - 1]).astype(jnp.int32)
    tile = ((TILE, LANES), F32)
    sends = ((count, TILE, LANES), F32)

    def ring(low, high):
        size = lax.axis_size("gx")
        up = [(i, (i + 1) % size) for i in range(size)]
        down = [(target, source) for source, target in up]
        return lax.ppermute(high, "gx", up), lax.ppermute(low, "gx", down)

    def exchange(blocks):
        return lax.all_to_all(blocks, GY, split_axis=0, concat_axis=0, tiled=True)

    own, base_send = call(
        gather_kernel, [((5, 4, TILE, LANES), F32), sends], scalars=1, plain_in=True
    )(place.reshape(1), density, velocity, fluid_mask, unit_of_column, radius_base.reshape(1, -1))
    base_in = exchange(base_send)

    forward = [(i, i + 1) for i in range(count - 1)]
    backward = [(target, source) for source, target in forward]
    low = lax.ppermute(own, GY, forward)
    high = lax.ppermute(own, GY, backward)
    pair = ((BASE_ROW + TILE, LANES), F32)
    g_l, g_r = call(rows_kernel, [pair, pair])(low, own, high, base_in)
    g_hl, g_hr = ring(g_l, g_r)
    fields = (g_hl, g_l, g_r, g_hr)

    def populations(rows):
        return [((19, 2, rows, LANES), F32)] * 2

    def halos(rows, last=False):
        return [((FAR if last else 19 + FAR, rows, LANES), F32)] * 2

    f_l, f_r, send_l, send_r, bits, links, send, base = call(
        first_kernel,
        [
            *populations(WIDE),
            *halos(WIDE),
            ((6, WIDE, LANES), jnp.int32),
            ((4, WIDE, LANES), F32),
            sends,
            tile,
        ],
        [((19, 8, WIDE + 2 * PAD, LANES), F32), ((3, 8, WIDE + 2 * PAD, LANES), jnp.int32)],
        scalars=1,
        mib=6,
    )(edge, *fields)

    for turn in range(3):
        gathered = exchange(send)
        h_l, h_r = ring(send_l, send_r)
        if turn == 0:
            rad, link_tile = call(response_kernel, [tile, tile])(gathered, base, base)
        else:
            (rad,) = call(response_kernel, [tile])(gathered, base, link_tile)
        rad_l, rad_r = ring(rad, rad)
        parts = (h_l, f_l, f_r, h_r)
        if turn < 2:
            rows = WIDE if turn == 0 else MID
            f_l, f_r, send_l, send_r, send = call(
                functools.partial(two_steps_kernel, n_rows=rows, last_halo=turn == 1),
                [*populations(MID), *halos(MID, last=turn == 1), sends],
                [
                    ((19, 8, rows + 2 * PAD, LANES), F32),
                    ((19, 8, MID + 2 * PAD, LANES), F32),
                ],
                mib=8,
            )(*parts, *fields, bits, links, rad, rad_l, rad_r)
    density_out, velocity_out = call(
        last_kernel,
        [((4, TILE, LANES), F32), ((3, 4, TILE, LANES), F32)],
        [((19, 8, MID + 2 * PAD, LANES), F32)],
        mib=4,
        plain_out=True,
    )(*parts, *fields, bits, rad, rad_l, rad_r)
    own_radius = lax.dynamic_slice_in_dim(rad[1], place * UNIT_DEV, UNIT_DEV)
    return density_out, velocity_out, own_radius


def solution(mesh):
    finer = Mesh(mesh.devices.reshape(mesh.shape["gx"], 4, -1), ("gx", "gy_0", "gy_1"))
    placed = (P("gx", GY, None), P(None, "gx", GY, None), P("gx", GY, None), P("gx", GY), P(GX_GY))
    return jax.shard_map(
        step_all,
        mesh=finer,
        in_specs=placed,
        out_specs=(P("gx", GY, None), P(None, "gx", GY, None), P(GX_GY)),
        check_vma=False,
    )
```

```python
import functools

import jax
import jax.numpy as jnp
from jax import lax
from jax.experimental import pallas as pl
from jax.experimental.pallas import tpu as pltpu
from jax.sharding import Mesh
from jax.sharding import PartitionSpec as P


UNIT_DEV = 8
GX_GY = ("gx", "gy_0", "gy_1")
GY = ("gy_0", "gy_1")

LATTICE = (
    (0, 0, 0),
    (1, 0, 0),
    (-1, 0, 0),
    (0, 1, 0),
    (0, -1, 0),
    (0, 0, 1),
    (0, 0, -1),
    (1, 1, 0),
    (-1, -1, 0),
    (1, -1, 0),
    (-1, 1, 0),
    (1, 0, 1),
    (-1, 0, -1),
    (1, 0, -1),
    (-1, 0, 1),
    (0, 1, 1),
    (0, -1, -1),
    (0, 1, -1),
    (0, -1, 1),
)
PAIRS = tuple(range(1, 19, 2))
WEIGHTS = (1.0 / 3.0,) + (1.0 / 18.0,) * 6 + (1.0 / 36.0,) * 12
RELAX_RATE = 1.25
DRIVE_SCALE = 0.002
F32 = jnp.float32

TILE = 8
LANES = 128
PAD = 8
WIDE = 24
MID = 16
BASE_ROW = 5 * 2 * WIDE
TOWARD = {side: tuple(i for i in range(19) if LATTICE[i][0] == side) for side in (-1, 1)}
FAR = 9


def opposite(direction):
    if direction == 0:
        return 0
    return direction + 1 if direction % 2 == 1 else direction - 1


def dot_c(direction, vector):
    total = None
    for c, v in zip(LATTICE[direction], vector):
        if c != 0:
            term = v if c > 0 else -v
            total = term if total is None else total + term
    return total


def moments(f, fluid):
    rho = f[0]
    momentum = [None, None, None]
    for i in PAIRS:
        rho = rho + (f[i] + f[i + 1])
        diff = f[i] - f[i + 1]
        for k in range(3):
            c = LATTICE[i][k]
            if c != 0:
                term = diff if c > 0 else -diff
                momentum[k] = term if momentum[k] is None else momentum[k] + term
    inverse = jnp.where(fluid, 1.0 / rho, 0.0)
    return jnp.where(fluid, rho, 0.0), [m * inverse for m in momentum]


def square(u):
    return u[0] * u[0] + u[1] * u[1] + u[2] * u[2]


def relaxed(f, rho, u, speed_sq, drive):
    rate = 1.0 if f is None else RELAX_RATE
    scaled = rate * rho
    even_base = scaled * (1.0 - 1.5 * speed_sq)
    force = drive * rho
    post = [None] * 19
    rest = WEIGHTS[0] * even_base
    post[0] = rest if f is None else rest + (1.0 - RELAX_RATE) * f[0]
    per_weight = {}
    for w in (WEIGHTS[1], WEIGHTS[7]):
        per_weight[w] = (w * even_base, (4.5 * w) * scaled, (3.0 * w) * scaled, (3.0 * w) * force)
    for i in PAIRS:
        base, quadratic, linear, push = per_weight[WEIGHTS[i]]
        cu = dot_c(i, u)
        even = base + quadratic * (cu * cu)
        odd = linear * cu
        if LATTICE[i][2] > 0:
            odd = odd + push
        elif LATTICE[i][2] < 0:
            odd = odd - push
        post[i] = even + odd
        post[i + 1] = even - odd
        if f is not None:
            post[i] = post[i] + (1.0 - RELAX_RATE) * f[i]
            post[i + 1] = post[i + 1] + (1.0 - RELAX_RATE) * f[i + 1]
    return post


def relaxed_some(directions, f, rho, u, drive):
    scaled = RELAX_RATE * rho
    base = scaled * (1.0 - 1.5 * square(u))
    force = drive * rho
    post = []
    for i, population in zip(directions, f):
        cu = dot_c(i, u)
        value = base + scaled * (4.5 * (cu * cu) + 3.0 * cu)
        if LATTICE[i][2] != 0:
            value = value + (3.0 * LATTICE[i][2]) * force
        post.append(WEIGHTS[i] * value + (1.0 - RELAX_RATE) * population)
    return post


def field(ref, k, x, row):
    return ref[pl.ds((2 * k + x) * WIDE + row, TILE), :]


def put_all(out, rows, f):
    for i in range(19):
        out[i, rows, :] = f[i]


def put_far(out, first, rows, side, f, rho, u):
    values = [f[i] for i in TOWARD[side]] + [rho] + list(u)
    for n, value in enumerate(values):
        out[first + n, rows, :] = value


def collide_far(halo, first, side, field_ref, x, row_in_fields, radius, n_rows, post, slot):
    for t in range(n_rows // TILE):
        rows = pl.ds(t * TILE, TILE)
        f = [halo[first + n, rows, :] for n in range(5)]
        rho = halo[first + 5, rows, :]
        u = [halo[first + 6 + k, rows, :] for k in range(3)]
        drive = drive_of(radius, field(field_ref, 4, x, row_in_fields + t * TILE))
        values = relaxed_some(TOWARD[side], f, rho, u, drive)
        for i, value in zip(TOWARD[side], values):
            post[i, slot, pl.ds(PAD + t * TILE, TILE), :] = value


def rolled(x, step):
    if step == 0:
        return x
    return pltpu.roll(x, step % LANES, axis=1)


def pulled(held, column, row, bits):
    def load(i, at_column, at_row):
        ref, slot = held[at_column]
        return ref[i, slot, pl.ds(at_row, TILE), :]

    f = [load(0, column, row)]
    for i in range(1, 19):
        cx, cy, cz = LATTICE[i]
        source = rolled(load(i, column - cx, row - cy), cz)
        bounced = load(opposite(i), column, row)
        f.append(jnp.where((bits & (1 << i)) != 0, source, bounced))
    return f


def drive_of(radius_row, unit):
    radius = jnp.take_along_axis(radius_row, unit.astype(jnp.int32), axis=1)
    return DRIVE_SCALE * radius * radius


def shear(links, speed_sq):
    return jnp.where(links > 0.0, links * speed_sq, 0.0)


def by_unit(column_values, unit):
    total = jnp.sum(column_values, axis=1, keepdims=True)
    lane = lax.broadcasted_iota(jnp.int32, (TILE, LANES), 1)
    return jnp.where(unit.astype(jnp.int32) == lane, total, 0.0)


def sublane_total(x):
    return jnp.broadcast_to(jnp.sum(x, axis=0, keepdims=True), (TILE, LANES))


def row_pick(rows):
    sub = lax.broadcasted_iota(jnp.int32, (TILE, LANES), 0)
    out = jnp.zeros((TILE, LANES), F32)
    for k, value in enumerate(rows):
        out = jnp.where(sub == k, value, out)
    return out


def every(tile, k):
    return jnp.broadcast_to(tile[k : k + 1, :], (TILE, LANES))


def send_all(ref, tile):
    for j in range(ref.shape[0]):
        ref[j] = tile


def sum_of(ref):
    parts = [ref[j] for j in range(ref.shape[0])]
    while len(parts) > 1:
        parts = [a + b for a, b in zip(parts[::2], parts[1::2])] + (
            [parts[-1]] if len(parts) % 2 else []
        )
    return parts[0]


def gather_kernel(
    place_ref, density, velocity, mask, unit, radius, out, send, density_v, velocity_v, mask_v, unit_v, radius_v, send_v, sems
):
    pairs = ((radius, radius_v), (density, density_v), (velocity, velocity_v), (mask, mask_v), (unit, unit_v))
    loads = [pltpu.make_async_copy(a, b, sems.at[n]) for n, (a, b) in enumerate(pairs)]
    for load in loads:
        load.start()
    lane = lax.broadcasted_iota(jnp.int32, (TILE, LANES), 1)
    narrow = (TILE, TILE)
    diagonal = lax.broadcasted_iota(jnp.int32, narrow, 0) == lax.broadcasted_iota(jnp.int32, narrow, 1)
    loads[0].wait()
    radii = jnp.broadcast_to(radius_v[...], narrow)
    column = jnp.sum(jnp.where(diagonal, radii, 0.0), axis=1, keepdims=True)
    sub = lax.broadcasted_iota(jnp.int32, (TILE, LANES), 0)
    spread = jnp.where(lane == place_ref[0] * UNIT_DEV + sub, column, 0.0)
    send_all(send_v, sublane_total(spread))
    store = pltpu.make_async_copy(send_v, send, sems.at[5])
    store.start()
    for load in loads[1:]:
        load.wait()
    for x in range(4):
        out[0, x] = jnp.where(mask_v[x] != 0, density_v[x], 0.0)
        for k in range(3):
            out[1 + k, x] = velocity_v[k, x]
        units = jnp.broadcast_to(unit_v[x : x + 1, :].astype(F32), narrow)
        column = jnp.sum(jnp.where(diagonal, units, 0.0), axis=1, keepdims=True)
        out[4, x] = jnp.broadcast_to(column, (TILE, LANES))
    store.wait()


def rows_kernel(low, own, high, base_in, left_out, right_out):
    base = sum_of(base_in)
    for half, out in ((0, left_out), (1, right_out)):
        for k in range(5):
            for x in range(2):
                for part, ref in enumerate((low, own, high)):
                    row = (2 * k + x) * WIDE + part * TILE
                    out[pl.ds(row, TILE), :] = ref[k, 2 * half + x]
        out[pl.ds(BASE_ROW, TILE), :] = base


def mark_open(open_, slot, column_fields, x, inside):
    lane = lax.broadcasted_iota(jnp.int32, (TILE, LANES), 1)
    zero = jnp.zeros((TILE, LANES), jnp.int32)
    for k in range(3):
        open_[k, slot, pl.ds(0, TILE), :] = zero
        open_[k, slot, pl.ds(PAD + WIDE, TILE), :] = zero
    for t in range(WIDE // TILE):
        here = (field(column_fields, 0, x, t * TILE) > 0.0).astype(jnp.int32)
        if inside is not None:
            here = here * inside
        rows = pl.ds(PAD + t * TILE, TILE)
        open_[0, slot, rows, :] = here
        open_[1, slot, rows, :] = jnp.where(lane == 0, 0, pltpu.roll(here, 1, axis=1))
        open_[2, slot, rows, :] = jnp.where(lane == LANES - 1, 0, pltpu.roll(here, LANES - 1, axis=1))


def start_column(post, slot, column_fields, x, radius, directions):
    for t in range(WIDE // TILE):
        rho = field(column_fields, 0, x, t * TILE)
        u = [field(column_fields, 1 + k, x, t * TILE) for k in range(3)]
        drive = drive_of(radius, field(column_fields, 4, x, t * TILE))
        values = relaxed(None, rho, u, square(u), drive)
        for i in directions:
            post[i, slot, pl.ds(PAD + t * TILE, TILE), :] = values[i]


def first_own_kernel(left, right, post, open_):
    for column in range(4):
        part, x = divmod(column, 2)
        ref = (left, right)[part]
        start_column(post, column, ref, x, ref[pl.ds(BASE_ROW, TILE), :], range(19))
        mark_open(open_, column, ref, x, None)


def first_kernel(
    edge_ref, halo_l, left, right, halo_r, post_own, open_own,
    f_l, f_r, send_l, send_r, bits_out, links_out, send, base_out, post_halo, open_halo,
):
    fields = (halo_l, left, right, halo_r)
    base_out[...] = left[pl.ds(BASE_ROW, TILE), :]
    post = {1: (post_halo, 0), 6: (post_halo, 1)} | {2 + k: (post_own, k) for k in range(4)}
    open_ = {0: (open_halo, 0), 1: (open_halo, 1), 6: (open_halo, 2), 7: (open_halo, 3)}
    open_ |= {2 + k: (open_own, k) for k in range(4)}
    for x in range(2):
        mark_open(open_halo, x, halo_l, x, edge_ref[0])
        mark_open(open_halo, 2 + x, halo_r, x, edge_ref[1])
    start_column(post_halo, 0, halo_l, 1, halo_l[pl.ds(BASE_ROW, TILE), :], TOWARD[1])
    start_column(post_halo, 1, halo_r, 0, halo_r[pl.ds(BASE_ROW, TILE), :], TOWARD[-1])
    link_sum = shear_0 = shear_1 = jnp.zeros((TILE, LANES), F32)
    for column in range(1, 7):
        part, x = divmod(column, 2)
        for t in range(WIDE // TILE):
            row = PAD + t * TILE
            rows = pl.ds(t * TILE, TILE)
            bits = jnp.zeros((TILE, LANES), jnp.int32)
            count = jnp.zeros((TILE, LANES), jnp.int32)
            for i in range(1, 19):
                cx, cy, cz = LATTICE[i]
                ref, slot = open_[column - cx]
                seen = ref[cz % 3, slot, pl.ds(row - cy, TILE), :]
                count = count + seen
                bits = bits | (seen << i)
            bits_out[column - 1, rows, :] = bits
            if part not in (1, 2):
                continue
            f = pulled(post, column, row, bits)
            out = f_l if part == 1 else f_r
            for i in range(19):
                out[i, x, rows, :] = f[i]
            fluid = field(fields[part], 0, x, t * TILE) > 0.0
            if t == 1 or column in (3, 4):
                rho, u = moments(f, fluid)
            if column == 2:
                put_all(send_l, rows, f)
            elif column == 3:
                put_far(send_l, 19, rows, -1, f, rho, u)
            elif column == 4:
                put_far(send_r, 19, rows, 1, f, rho, u)
            else:
                put_all(send_r, rows, f)
            if t != 1:
                links_out[column - 2, rows, :] = jnp.zeros((TILE, LANES), F32)
                continue
            links = jnp.where(fluid, (18 - count).astype(F32), 0.0)
            links_out[column - 2, rows, :] = links
            unit = field(fields[part], 4, x, t * TILE)
            start = [field(fields[part], 1 + k, x, t * TILE) for k in range(3)]
            link_sum = link_sum + by_unit(links, unit)
            shear_0 = shear_0 + by_unit(links * square(start), unit)
            shear_1 = shear_1 + by_unit(links * square(u), unit)
    send_all(send, row_pick([sublane_total(s) for s in (shear_0, shear_1, link_sum)]))


def response_kernel(gathered, base, links_in, radius_out, links_out=None):
    totals = sum_of(gathered)
    if links_out is None:
        links = links_in[...]
    else:
        links = every(totals, 2)
        links_out[...] = links
    mean = 100.0 * totals / jnp.maximum(links, 1.0)
    radius_out[...] = every(base[...], 0) * (0.6 + 0.8 * jnp.tanh(mean))


def collide_all(populations, field_ref, x, radius, row_in_fields, n_rows, post, slot):
    for t in range(n_rows // TILE):
        rows = pl.ds(t * TILE, TILE)
        near = row_in_fields + t * TILE
        f = [populations(i, rows) for i in range(19)]
        rho, u = moments(f, field(field_ref, 0, x, near) > 0.0)
        drive = drive_of(radius, field(field_ref, 4, x, near))
        values = relaxed(f, rho, u, square(u), drive)
        for i in range(19):
            post[i, slot, pl.ds(PAD + t * TILE, TILE), :] = values[i]


def in_pair(ref, x):
    return lambda i, rows: ref[i, x, rows, :]


def in_halo(ref):
    return lambda i, rows: ref[i, rows, :]


def own_kernel(a, b, g_a, g_b, rad, post, *, n_rows, row):
    radius = every(rad[...], row)
    for column in range(4):
        part, x = divmod(column, 2)
        collide_all(
            in_pair((a, b)[part], x), (g_a, g_b)[part], x, radius, (WIDE - n_rows) // 2, n_rows, post, column
        )


def advance(held, column, field_ref, x, links, bits_in, radius, skip, side, post, slot):
    sums = jnp.zeros((TILE, LANES), F32)
    for t in range(MID // TILE):
        row = (WIDE - MID) // 2 + t * TILE
        near = pl.ds(row, TILE)
        rows = pl.ds(PAD + t * TILE, TILE)
        f = pulled(held, column, PAD + skip + t * TILE, bits_in[column - 1, near, :])
        rho, u = moments(f, field(field_ref, 0, x, row) > 0.0)
        unit = field(field_ref, 4, x, row)
        drive = drive_of(radius, unit)
        if side is not None:
            chosen = TOWARD[side]
            values = relaxed_some(chosen, [f[i] for i in chosen], rho, u, drive)
        else:
            chosen = range(19)
            speed_sq = square(u)
            sums = sums + by_unit(shear(links[column - 2, near, :], speed_sq), unit)
            values = relaxed(f, rho, u, speed_sq, drive)
        for i, value in zip(chosen, values):
            post[i, slot, rows, :] = value
    return sums


def two_own_kernel(a, b, g_a, g_b, bits_in, links_in, rad, post_a, post_b, shear_out, *, n_rows):
    own_kernel(a, b, g_a, g_b, rad, post_a, n_rows=n_rows, row=0)
    held = {2 + k: (post_a, k) for k in range(4)}
    second = every(rad[...], 1)
    skip = (n_rows - MID) // 2
    shear_out[...] = advance(
        held, 3, g_a, 1, links_in, bits_in, second, skip, None, post_b, 0
    ) + advance(held, 4, g_b, 0, links_in, bits_in, second, skip, None, post_b, 1)


def two_steps_kernel(
    h_l, h_r, g_hl, g_a, g_b, g_hr, bits_in, links_in, rad, rad_l, rad_r, own_a, own_b, shear_in,
    f_l, f_r, send_l, send_r, send, post_a, post_b, *, n_rows, last_halo,
):
    fields = (g_hl, g_a, g_b, g_hr)
    top = (WIDE - n_rows) // 2
    skip = (n_rows - MID) // 2
    collide_all(in_halo(h_l), g_hl, 1, every(rad_l[...], 0), top, n_rows, post_a, 1)
    collide_all(in_halo(h_r), g_hr, 0, every(rad_r[...], 0), top, n_rows, post_a, 2)
    collide_far(h_l, 19, 1, g_hl, 0, top, every(rad_l[...], 0), n_rows, post_a, 0)
    collide_far(h_r, 19, -1, g_hr, 1, top, every(rad_r[...], 0), n_rows, post_a, 3)
    held = {0: (post_a, 0), 1: (post_a, 1), 6: (post_a, 2), 7: (post_a, 3)}
    held |= {2 + k: (own_a, k) for k in range(4)}
    own = every(rad[...], 1)
    shear_a = shear_in[...]
    shear_b = jnp.zeros((TILE, LANES), F32)
    advance(held, 1, g_hl, 1, links_in, bits_in, every(rad_l[...], 1), skip, 1, post_b, 0)
    advance(held, 6, g_hr, 0, links_in, bits_in, every(rad_r[...], 1), skip, -1, post_b, 3)
    shear_a += advance(held, 2, g_a, 0, links_in, bits_in, own, skip, None, post_b, 1)
    shear_a += advance(held, 5, g_b, 1, links_in, bits_in, own, skip, None, post_b, 2)
    held = {1: (post_b, 0), 2: (post_b, 1), 3: (own_b, 0), 4: (own_b, 1), 5: (post_b, 2), 6: (post_b, 3)}
    for column in range(2, 6):
        part, x = divmod(column, 2)
        out = f_l if part == 1 else f_r
        for t in range(MID // TILE):
            row = (WIDE - MID) // 2 + t * TILE
            near = pl.ds(row, TILE)
            rows = pl.ds(t * TILE, TILE)
            f = pulled(held, column, PAD + t * TILE, bits_in[column - 1, near, :])
            for i in range(19):
                out[i, x, rows, :] = f[i]
            rho, u = moments(f, field(fields[part], 0, x, row) > 0.0)
            if last_halo:
                if column == 2:
                    put_far(send_l, 0, rows, -1, f, rho, u)
                elif column == 5:
                    put_far(send_r, 0, rows, 1, f, rho, u)
            elif column == 2:
                put_all(send_l, rows, f)
            elif column == 3:
                put_far(send_l, 19, rows, -1, f, rho, u)
            elif column == 4:
                put_far(send_r, 19, rows, 1, f, rho, u)
            else:
                put_all(send_r, rows, f)
            shear_b = shear_b + by_unit(
                shear(links_in[column - 2, near, :], square(u)), field(fields[part], 4, x, row)
            )
    send_all(send, row_pick([sublane_total(s) for s in (shear_a, shear_b)]))


def last_kernel(h_l, h_r, g_hl, g_a, g_b, g_hr, bits_in, rad_l, rad_r, own_post, density, velocity, post):
    fields = (g_hl, g_a, g_b, g_hr)
    top = (WIDE - MID) // 2
    collide_far(h_l, 0, 1, g_hl, 1, top, every(rad_l[...], 0), MID, post, 0)
    collide_far(h_r, 0, -1, g_hr, 0, top, every(rad_r[...], 0), MID, post, 1)
    held = {1: (post, 0), 6: (post, 1)} | {2 + k: (own_post, k) for k in range(4)}
    own = pl.ds(TILE, TILE)
    for column in range(2, 6):
        part, x = divmod(column, 2)
        f = pulled(held, column, PAD + (MID - TILE) // 2, bits_in[column - 1, own, :])
        rho, u = moments(f, field(fields[part], 0, x, TILE) > 0.0)
        density[column - 2] = rho
        for k in range(3):
            velocity[k, column - 2] = u[k]


def call(kernel, outs, scratch=(), scalars=0, mib=1, plain_out=False):
    vmem = pl.BlockSpec(memory_space=pltpu.VMEM)
    smem = pl.BlockSpec(memory_space=pltpu.SMEM)

    def run(*args):
        args = args[:scalars] + tuple(
            pltpu.with_memory_space_constraint(a, pltpu.VMEM) for a in args[scalars:]
        )
        held = jax.ShapeDtypeStruct if plain_out else pltpu.VMEM
        return pl.pallas_call(
            kernel,
            out_shape=[held(shape, dtype) for shape, dtype in outs],
            in_specs=[smem] * scalars + [vmem] * (len(args) - scalars),
            out_specs=[vmem] * len(outs),
            scratch_shapes=[pltpu.VMEM(shape, dtype) for shape, dtype in scratch],
            compiler_params=pltpu.CompilerParams(vmem_limit_bytes=mib << 20),
        )(*args)

    return run


def step_all(density, velocity, fluid_mask, unit_of_column, radius_base):
    count = lax.axis_size(GY)
    place = lax.axis_index(GY)
    at_x = lax.axis_index("gx")
    edge = jnp.stack([at_x > 0, at_x < lax.axis_size("gx") - 1]).astype(jnp.int32)
    tile = ((TILE, LANES), F32)
    sends = ((count, TILE, LANES), F32)

    def ring(low, high):
        size = lax.axis_size("gx")
        up = [(i, (i + 1) % size) for i in range(size)]
        down = [(target, source) for source, target in up]
        return lax.ppermute(high, "gx", up), lax.ppermute(low, "gx", down)

    def exchange(blocks):
        return lax.all_to_all(blocks, GY, split_axis=0, concat_axis=0, tiled=True)

    arrays = (density, velocity, fluid_mask, unit_of_column, radius_base.reshape(1, -1))
    anywhere = pl.BlockSpec(memory_space=pl.ANY)
    own, base_send = pl.pallas_call(
        gather_kernel,
        out_shape=[pltpu.VMEM((5, 4, TILE, LANES), F32), jax.ShapeDtypeStruct(*sends)],
        in_specs=[pl.BlockSpec(memory_space=pltpu.SMEM)] + [anywhere] * 5,
        out_specs=[pl.BlockSpec(memory_space=pltpu.VMEM), anywhere],
        scratch_shapes=[pltpu.VMEM(a.shape, a.dtype) for a in arrays]
        + [pltpu.VMEM(*sends), pltpu.SemaphoreType.DMA((6,))],
        compiler_params=pltpu.CompilerParams(vmem_limit_bytes=1 << 20),
    )(place.reshape(1), *(pltpu.with_memory_space_constraint(a, pltpu.HBM) for a in arrays))
    base_in = exchange(base_send)

    forward = [(i, i + 1) for i in range(count - 1)]
    backward = [(target, source) for source, target in forward]
    low = lax.ppermute(own, GY, forward)
    high = lax.ppermute(own, GY, backward)
    pair = ((BASE_ROW + TILE, LANES), F32)
    g_l, g_r = call(rows_kernel, [pair, pair])(low, own, high, base_in)
    g_hl, g_hr = ring(g_l, g_r)
    fields = (g_hl, g_l, g_r, g_hr)

    def posts(columns, rows):
        return ((19, columns, rows + 2 * PAD, LANES), F32)

    def opens(columns):
        return ((3, columns, WIDE + 2 * PAD, LANES), jnp.int32)

    post_own, open_own = call(first_own_kernel, [posts(4, WIDE), opens(4)])(g_l, g_r)

    def populations(rows):
        return [((19, 2, rows, LANES), F32)] * 2

    def halos(rows, last=False):
        return [((FAR if last else 19 + FAR, rows, LANES), F32)] * 2

    f_l, f_r, send_l, send_r, bits, links, send, base = call(
        first_kernel,
        [
            *populations(WIDE),
            *halos(WIDE),
            ((6, WIDE, LANES), jnp.int32),
            ((4, WIDE, LANES), F32),
            sends,
            tile,
        ],
        [posts(2, WIDE), opens(4)],
        scalars=1,
        mib=3,
    )(edge, *fields, post_own, open_own)

    for turn in range(3):
        gathered = exchange(send)
        h_l, h_r = ring(send_l, send_r)
        if turn == 0:
            rad, link_tile = call(response_kernel, [tile, tile])(gathered, base, base)
        else:
            (rad,) = call(response_kernel, [tile])(gathered, base, link_tile)
        rad_l, rad_r = ring(rad, rad)
        if turn < 2:
            rows = WIDE if turn == 0 else MID
            own_part = call(
                functools.partial(two_own_kernel, n_rows=rows), [posts(4, rows), posts(2, MID), tile]
            )(f_l, f_r, g_l, g_r, bits, links, rad)
            f_l, f_r, send_l, send_r, send = call(
                functools.partial(two_steps_kernel, n_rows=rows, last_halo=turn == 1),
                [*populations(MID), *halos(MID, last=turn == 1), sends],
                [posts(4, rows), posts(4, MID)],
                mib=4,
            )(h_l, h_r, *fields, bits, links, rad, rad_l, rad_r, *own_part)
    (own_post,) = call(functools.partial(own_kernel, n_rows=MID, row=0), [posts(4, MID)])(
        f_l, f_r, g_l, g_r, rad
    )
    density_out, velocity_out = call(
        last_kernel,
        [((4, TILE, LANES), F32), ((3, 4, TILE, LANES), F32)],
        [posts(2, MID)],
        mib=2,
        plain_out=True,
    )(h_l, h_r, *fields, bits, rad_l, rad_r, own_post)
    own_radius = lax.dynamic_slice_in_dim(rad[1], place * UNIT_DEV, UNIT_DEV)
    return density_out, velocity_out, own_radius


def solution(mesh):
    finer = Mesh(mesh.devices.reshape(mesh.shape["gx"], 4, -1), ("gx", "gy_0", "gy_1"))
    placed = (P("gx", GY, None), P(None, "gx", GY, None), P("gx", GY, None), P("gx", GY), P(GX_GY))
    return jax.shard_map(
        step_all,
        mesh=finer,
        in_specs=placed,
        out_specs=(P("gx", GY, None), P(None, "gx", GY, None), P(GX_GY)),
        check_vma=False,
    )
```

```python
import functools

import jax
import jax.numpy as jnp
from jax import lax
from jax.experimental import pallas as pl
from jax.experimental.pallas import tpu as pltpu
from jax.sharding import Mesh
from jax.sharding import PartitionSpec as P


UNIT_DEV = 8
GX_GY = ("gx", "gy_0", "gy_1")
GY = ("gy_0", "gy_1")

LATTICE = (
    (0, 0, 0),
    (1, 0, 0),
    (-1, 0, 0),
    (0, 1, 0),
    (0, -1, 0),
    (0, 0, 1),
    (0, 0, -1),
    (1, 1, 0),
    (-1, -1, 0),
    (1, -1, 0),
    (-1, 1, 0),
    (1, 0, 1),
    (-1, 0, -1),
    (1, 0, -1),
    (-1, 0, 1),
    (0, 1, 1),
    (0, -1, -1),
    (0, 1, -1),
    (0, -1, 1),
)
PAIRS = tuple(range(1, 19, 2))
WEIGHTS = (1.0 / 3.0,) + (1.0 / 18.0,) * 6 + (1.0 / 36.0,) * 12
RELAX_RATE = 1.25
DRIVE_SCALE = 0.002
F32 = jnp.float32

TILE = 8
LANES = 128
PAD = 8
WIDE = 24
MID = 16
OWN_PLANES = {(k, x): 2 * k + x for k in range(5) for x in range(2)}
NEAR_FAR = {(k, 0): k for k in range(5)} | {(0, 1): 5, (4, 1): 6}
LEFT_PLANES = {(k, 1 - x): plane for (k, x), plane in NEAR_FAR.items()}
TOWARD = {side: tuple(i for i in range(19) if LATTICE[i][0] == side) for side in (-1, 1)}
FAR = 9


def opposite(direction):
    if direction == 0:
        return 0
    return direction + 1 if direction % 2 == 1 else direction - 1


def dot_c(direction, vector):
    total = None
    for c, v in zip(LATTICE[direction], vector):
        if c != 0:
            term = v if c > 0 else -v
            total = term if total is None else total + term
    return total


def moments(f, fluid):
    rho = f[0]
    momentum = [None, None, None]
    for i in PAIRS:
        rho = rho + (f[i] + f[i + 1])
        diff = f[i] - f[i + 1]
        for k in range(3):
            c = LATTICE[i][k]
            if c != 0:
                term = diff if c > 0 else -diff
                momentum[k] = term if momentum[k] is None else momentum[k] + term
    inverse = jnp.where(fluid, 1.0 / rho, 0.0)
    return jnp.where(fluid, rho, 0.0), [m * inverse for m in momentum]


def square(u):
    return u[0] * u[0] + u[1] * u[1] + u[2] * u[2]


def relaxed(f, rho, u, speed_sq, drive):
    rate = 1.0 if f is None else RELAX_RATE
    scaled = rate * rho
    even_base = scaled * (1.0 - 1.5 * speed_sq)
    force = drive * rho
    post = [None] * 19
    rest = WEIGHTS[0] * even_base
    post[0] = rest if f is None else rest + (1.0 - RELAX_RATE) * f[0]
    per_weight = {}
    for w in (WEIGHTS[1], WEIGHTS[7]):
        per_weight[w] = (w * even_base, (4.5 * w) * scaled, (3.0 * w) * scaled, (3.0 * w) * force)
    for i in PAIRS:
        base, quadratic, linear, push = per_weight[WEIGHTS[i]]
        cu = dot_c(i, u)
        even = base + quadratic * (cu * cu)
        odd = linear * cu
        if LATTICE[i][2] > 0:
            odd = odd + push
        elif LATTICE[i][2] < 0:
            odd = odd - push
        post[i] = even + odd
        post[i + 1] = even - odd
        if f is not None:
            post[i] = post[i] + (1.0 - RELAX_RATE) * f[i]
            post[i + 1] = post[i + 1] + (1.0 - RELAX_RATE) * f[i + 1]
    return post


def relaxed_some(directions, f, rho, u, drive):
    scaled = RELAX_RATE * rho
    base = scaled * (1.0 - 1.5 * square(u))
    force = drive * rho
    post = []
    for i, population in zip(directions, f):
        cu = dot_c(i, u)
        value = base + scaled * (4.5 * (cu * cu) + 3.0 * cu)
        if LATTICE[i][2] != 0:
            value = value + (3.0 * LATTICE[i][2]) * force
        post.append(WEIGHTS[i] * value + (1.0 - RELAX_RATE) * population)
    return post


def field(held, k, x, row):
    ref, planes = held
    return ref[pl.ds(planes[k, x] * WIDE + row, TILE), :]


def base_of(held):
    ref, planes = held
    return ref[pl.ds(len(planes) * WIDE, TILE), :]


def fields_of(halo_l, left, right, halo_r):
    return ((halo_l, LEFT_PLANES), (left, OWN_PLANES), (right, OWN_PLANES), (halo_r, NEAR_FAR))


def put_all(out, rows, f):
    for i in range(19):
        out[i, rows, :] = f[i]


def put_far(out, first, rows, side, f, rho, u):
    values = [f[i] for i in TOWARD[side]] + [rho] + list(u)
    for n, value in enumerate(values):
        out[first + n, rows, :] = value


def collide_far(halo, first, side, field_ref, x, row_in_fields, radius, n_rows, post, slot):
    for t in range(n_rows // TILE):
        rows = pl.ds(t * TILE, TILE)
        f = [halo[first + n, rows, :] for n in range(5)]
        rho = halo[first + 5, rows, :]
        u = [halo[first + 6 + k, rows, :] for k in range(3)]
        drive = drive_of(radius, field(field_ref, 4, x, row_in_fields + t * TILE))
        values = relaxed_some(TOWARD[side], f, rho, u, drive)
        for i, value in zip(TOWARD[side], values):
            post[i, slot, pl.ds(PAD + t * TILE, TILE), :] = value


def rolled(x, step):
    if step == 0:
        return x
    return pltpu.roll(x, step % LANES, axis=1)


def pulled(held, column, row, bits):
    def load(i, at_column, at_row):
        ref, slot = held[at_column]
        return ref[i, slot, pl.ds(at_row, TILE), :]

    f = [load(0, column, row)]
    for i in range(1, 19):
        cx, cy, cz = LATTICE[i]
        source = rolled(load(i, column - cx, row - cy), cz)
        bounced = load(opposite(i), column, row)
        f.append(jnp.where((bits & (1 << i)) != 0, source, bounced))
    return f


def drive_of(radius_row, unit):
    radius = jnp.take_along_axis(radius_row, unit.astype(jnp.int32), axis=1)
    return DRIVE_SCALE * radius * radius


def shear(links, speed_sq):
    return jnp.where(links > 0.0, links * speed_sq, 0.0)


def by_unit(column_values, unit):
    total = jnp.sum(column_values, axis=1, keepdims=True)
    lane = lax.broadcasted_iota(jnp.int32, (TILE, LANES), 1)
    return jnp.where(unit.astype(jnp.int32) == lane, total, 0.0)


def sublane_total(x):
    return jnp.broadcast_to(jnp.sum(x, axis=0, keepdims=True), (TILE, LANES))


def row_pick(rows):
    sub = lax.broadcasted_iota(jnp.int32, (TILE, LANES), 0)
    out = jnp.zeros((TILE, LANES), F32)
    for k, value in enumerate(rows):
        out = jnp.where(sub == k, value, out)
    return out


def every(tile, k):
    return jnp.broadcast_to(tile[k : k + 1, :], (TILE, LANES))


def send_all(ref, tile):
    for j in range(ref.shape[0]):
        ref[j] = tile


def sum_of(ref):
    parts = [ref[j] for j in range(ref.shape[0])]
    while len(parts) > 1:
        parts = [a + b for a, b in zip(parts[::2], parts[1::2])] + (
            [parts[-1]] if len(parts) % 2 else []
        )
    return parts[0]


def gather_kernel(
    place_ref, density, velocity, mask, unit, radius, out, send, density_v, velocity_v, mask_v, unit_v, radius_v, send_v, sems
):
    pairs = ((radius, radius_v), (density, density_v), (velocity, velocity_v), (mask, mask_v), (unit, unit_v))
    loads = [pltpu.make_async_copy(a, b, sems.at[n]) for n, (a, b) in enumerate(pairs)]
    for load in loads:
        load.start()
    lane = lax.broadcasted_iota(jnp.int32, (TILE, LANES), 1)
    narrow = (TILE, TILE)
    diagonal = lax.broadcasted_iota(jnp.int32, narrow, 0) == lax.broadcasted_iota(jnp.int32, narrow, 1)
    loads[0].wait()
    radii = jnp.broadcast_to(radius_v[...], narrow)
    column = jnp.sum(jnp.where(diagonal, radii, 0.0), axis=1, keepdims=True)
    sub = lax.broadcasted_iota(jnp.int32, (TILE, LANES), 0)
    spread = jnp.where(lane == place_ref[0] * UNIT_DEV + sub, column, 0.0)
    send_all(send_v, sublane_total(spread))
    store = pltpu.make_async_copy(send_v, send, sems.at[5])
    store.start()
    for load in loads[1:]:
        load.wait()
    for x in range(4):
        out[0, x] = jnp.where(mask_v[x] != 0, density_v[x], 0.0)
        for k in range(3):
            out[1 + k, x] = velocity_v[k, x]
        units = jnp.broadcast_to(unit_v[x : x + 1, :].astype(F32), narrow)
        column = jnp.sum(jnp.where(diagonal, units, 0.0), axis=1, keepdims=True)
        out[4, x] = jnp.broadcast_to(column, (TILE, LANES))
    store.wait()


def rows_kernel(low, own, high, base_in, left_out, right_out, left_send, right_send):
    base = sum_of(base_in)
    for half, out, send, planes in (
        (0, left_out, left_send, NEAR_FAR),
        (1, right_out, right_send, LEFT_PLANES),
    ):
        for (k, x), plane in OWN_PLANES.items():
            for part, ref in enumerate((low, own, high)):
                value = ref[k, 2 * half + x]
                out[pl.ds(plane * WIDE + part * TILE, TILE), :] = value
                if (k, x) in planes:
                    send[pl.ds(planes[k, x] * WIDE + part * TILE, TILE), :] = value
        out[pl.ds(len(OWN_PLANES) * WIDE, TILE), :] = base
        send[pl.ds(len(planes) * WIDE, TILE), :] = base


def mark_open(open_, slot, column_fields, x, inside):
    lane = lax.broadcasted_iota(jnp.int32, (TILE, LANES), 1)
    zero = jnp.zeros((TILE, LANES), jnp.int32)
    for k in range(3):
        open_[k, slot, pl.ds(0, TILE), :] = zero
        open_[k, slot, pl.ds(PAD + WIDE, TILE), :] = zero
    for t in range(WIDE // TILE):
        here = (field(column_fields, 0, x, t * TILE) > 0.0).astype(jnp.int32)
        if inside is not None:
            here = here * inside
        rows = pl.ds(PAD + t * TILE, TILE)
        open_[0, slot, rows, :] = here
        open_[1, slot, rows, :] = jnp.where(lane == 0, 0, pltpu.roll(here, 1, axis=1))
        open_[2, slot, rows, :] = jnp.where(lane == LANES - 1, 0, pltpu.roll(here, LANES - 1, axis=1))


def start_column(post, slot, column_fields, x, radius, directions):
    for t in range(WIDE // TILE):
        rho = field(column_fields, 0, x, t * TILE)
        u = [field(column_fields, 1 + k, x, t * TILE) for k in range(3)]
        drive = drive_of(radius, field(column_fields, 4, x, t * TILE))
        values = relaxed(None, rho, u, square(u), drive)
        for i in directions:
            post[i, slot, pl.ds(PAD + t * TILE, TILE), :] = values[i]


def stream_first(post, open_, column, held, x, f_out, send_near, send_far, side, links_out):
    sums = None
    bits_of = []
    for t in range(WIDE // TILE):
        row = PAD + t * TILE
        rows = pl.ds(t * TILE, TILE)
        bits, count = open_bits(open_, column, row)
        bits_of.append(bits)
        f = pulled(post, column, row, bits)
        put_all(f_out.at[:, x], rows, f)
        fluid = field(held, 0, x, t * TILE) > 0.0
        if t == 1 or send_far is not None:
            rho, u = moments(f, fluid)
        if send_far is not None:
            put_far(send_far, 19, rows, side, f, rho, u)
        else:
            put_all(send_near, rows, f)
        if t != 1:
            links_out[column - 2, rows, :] = jnp.zeros((TILE, LANES), F32)
            continue
        links = jnp.where(fluid, (18 - count).astype(F32), 0.0)
        links_out[column - 2, rows, :] = links
        unit = field(held, 4, x, t * TILE)
        start = [field(held, 1 + k, x, t * TILE) for k in range(3)]
        sums = [by_unit(v, unit) for v in (links * square(start), links * square(u), links)]
    return bits_of, sums


def open_bits(open_, column, row):
    bits = count = jnp.zeros((TILE, LANES), jnp.int32)
    for i in range(1, 19):
        cx, cy, cz = LATTICE[i]
        ref, slot = open_[column - cx]
        seen = ref[cz % 3, slot, pl.ds(row - cy, TILE), :]
        count = count + seen
        bits = bits | (seen << i)
    return bits, count


def put_bits(bits_out, column, bits_of):
    for t, bits in enumerate(bits_of):
        bits_out[column - 1, pl.ds(t * TILE, TILE), :] = bits


def first_own_kernel(left, right, post, open_, f_l, f_r, send_l, send_r, bits_out, links_out, sums_out):
    pairs = ((left, OWN_PLANES), (right, OWN_PLANES))
    for column in range(4):
        part, x = divmod(column, 2)
        start_column(post, column, pairs[part], x, base_of(pairs[part]), range(19))
        mark_open(open_, column, pairs[part], x, None)
    held = {2 + k: (post, k) for k in range(4)}
    seen = {2 + k: (open_, k) for k in range(4)}
    bits, sums_a = stream_first(held, seen, 3, pairs[0], 1, f_l, None, send_l, -1, links_out)
    put_bits(bits_out, 3, bits)
    bits, sums_b = stream_first(held, seen, 4, pairs[1], 0, f_r, None, send_r, 1, links_out)
    put_bits(bits_out, 4, bits)
    for k in range(3):
        sums_out[k] = sums_a[k] + sums_b[k]


def first_kernel(
    edge_ref, halo_l, left, right, halo_r, post_own, open_own, sums_in, *rest
):
    f_l, f_r, send_l, send_r, bits_out, links_out, send, base_out, post_halo, open_halo = rest[6:]
    fields = fields_of(halo_l, left, right, halo_r)
    base_out[...] = base_of(fields[1])
    post = {1: (post_halo, 0), 6: (post_halo, 1)} | {2 + k: (post_own, k) for k in range(4)}
    open_ = {0: (open_halo, 0), 1: (open_halo, 1), 6: (open_halo, 2), 7: (open_halo, 3)}
    open_ |= {2 + k: (open_own, k) for k in range(4)}
    for x in range(2):
        mark_open(open_halo, x, fields[0], x, edge_ref[0])
        mark_open(open_halo, 2 + x, fields[3], x, edge_ref[1])
    start_column(post_halo, 0, fields[0], 1, base_of(fields[0]), TOWARD[1])
    start_column(post_halo, 1, fields[3], 0, base_of(fields[3]), TOWARD[-1])
    for column in (1, 6):
        put_bits(bits_out, column, [open_bits(open_, column, PAD + t * TILE)[0] for t in range(WIDE // TILE)])
    bits, sums_a = stream_first(post, open_, 2, fields[1], 0, f_l, send_l, None, None, links_out)
    put_bits(bits_out, 2, bits)
    bits, sums_b = stream_first(post, open_, 5, fields[2], 1, f_r, send_r, None, None, links_out)
    put_bits(bits_out, 5, bits)
    send_all(send, row_pick([sublane_total(sums_in[k] + sums_a[k] + sums_b[k]) for k in range(3)]))


def response_kernel(gathered, base, links_in, radius_out, links_out=None):
    totals = sum_of(gathered)
    if links_out is None:
        links = links_in[...]
    else:
        links = every(totals, 2)
        links_out[...] = links
    mean = 100.0 * totals / jnp.maximum(links, 1.0)
    radius_out[...] = every(base[...], 0) * (0.6 + 0.8 * jnp.tanh(mean))


def collide_all(populations, field_ref, x, radius, row_in_fields, n_rows, post, slot):
    for t in range(n_rows // TILE):
        rows = pl.ds(t * TILE, TILE)
        near = row_in_fields + t * TILE
        f = [populations(i, rows) for i in range(19)]
        rho, u = moments(f, field(field_ref, 0, x, near) > 0.0)
        drive = drive_of(radius, field(field_ref, 4, x, near))
        values = relaxed(f, rho, u, square(u), drive)
        for i in range(19):
            post[i, slot, pl.ds(PAD + t * TILE, TILE), :] = values[i]


def in_pair(ref, x):
    return lambda i, rows: ref[i, x, rows, :]


def in_halo(ref):
    return lambda i, rows: ref[i, rows, :]


def own_kernel(a, b, g_a, g_b, rad, post, *, n_rows, row):
    radius = every(rad[...], row)
    for column in range(4):
        part, x = divmod(column, 2)
        collide_all(
            in_pair((a, b)[part], x), ((g_a, g_b)[part], OWN_PLANES), x, radius, (WIDE - n_rows) // 2, n_rows, post, column
        )


def advance(held, column, field_ref, x, links, bits_in, radius, skip, side, post, slot):
    sums = jnp.zeros((TILE, LANES), F32)
    for t in range(MID // TILE):
        row = (WIDE - MID) // 2 + t * TILE
        near = pl.ds(row, TILE)
        rows = pl.ds(PAD + t * TILE, TILE)
        f = pulled(held, column, PAD + skip + t * TILE, bits_in[column - 1, near, :])
        rho, u = moments(f, field(field_ref, 0, x, row) > 0.0)
        unit = field(field_ref, 4, x, row)
        drive = drive_of(radius, unit)
        if side is not None:
            chosen = TOWARD[side]
            values = relaxed_some(chosen, [f[i] for i in chosen], rho, u, drive)
        else:
            chosen = range(19)
            speed_sq = square(u)
            sums = sums + by_unit(shear(links[column - 2, near, :], speed_sq), unit)
            values = relaxed(f, rho, u, speed_sq, drive)
        for i, value in zip(chosen, values):
            post[i, slot, rows, :] = value
    return sums


def two_own_kernel(a, b, g_a, g_b, bits_in, links_in, rad, post_a, post_b, shear_out, *, n_rows):
    own_kernel(a, b, g_a, g_b, rad, post_a, n_rows=n_rows, row=0)
    held = {2 + k: (post_a, k) for k in range(4)}
    second = every(rad[...], 1)
    skip = (n_rows - MID) // 2
    shear_out[...] = advance(
        held, 3, (g_a, OWN_PLANES), 1, links_in, bits_in, second, skip, None, post_b, 0
    ) + advance(held, 4, (g_b, OWN_PLANES), 0, links_in, bits_in, second, skip, None, post_b, 1)


def two_steps_kernel(
    h_l, h_r, g_hl, g_a, g_b, g_hr, bits_in, links_in, rad, rad_l, rad_r, own_a, own_b, shear_in,
    f_l, f_r, send_l, send_r, send, post_a, post_b, *, n_rows, last_halo,
):
    fields = g_hl, g_a, g_b, g_hr = fields_of(g_hl, g_a, g_b, g_hr)
    top = (WIDE - n_rows) // 2
    skip = (n_rows - MID) // 2
    collide_all(in_halo(h_l), g_hl, 1, every(rad_l[...], 0), top, n_rows, post_a, 1)
    collide_all(in_halo(h_r), g_hr, 0, every(rad_r[...], 0), top, n_rows, post_a, 2)
    collide_far(h_l, 19, 1, g_hl, 0, top, every(rad_l[...], 0), n_rows, post_a, 0)
    collide_far(h_r, 19, -1, g_hr, 1, top, every(rad_r[...], 0), n_rows, post_a, 3)
    held = {0: (post_a, 0), 1: (post_a, 1), 6: (post_a, 2), 7: (post_a, 3)}
    held |= {2 + k: (own_a, k) for k in range(4)}
    own = every(rad[...], 1)
    shear_a = shear_in[...]
    shear_b = jnp.zeros((TILE, LANES), F32)
    advance(held, 1, g_hl, 1, links_in, bits_in, every(rad_l[...], 1), skip, 1, post_b, 0)
    advance(held, 6, g_hr, 0, links_in, bits_in, every(rad_r[...], 1), skip, -1, post_b, 3)
    shear_a += advance(held, 2, g_a, 0, links_in, bits_in, own, skip, None, post_b, 1)
    shear_a += advance(held, 5, g_b, 1, links_in, bits_in, own, skip, None, post_b, 2)
    held = {1: (post_b, 0), 2: (post_b, 1), 3: (own_b, 0), 4: (own_b, 1), 5: (post_b, 2), 6: (post_b, 3)}
    for column in range(2, 6):
        part, x = divmod(column, 2)
        out = f_l if part == 1 else f_r
        for t in range(MID // TILE):
            row = (WIDE - MID) // 2 + t * TILE
            near = pl.ds(row, TILE)
            rows = pl.ds(t * TILE, TILE)
            f = pulled(held, column, PAD + t * TILE, bits_in[column - 1, near, :])
            for i in range(19):
                out[i, x, rows, :] = f[i]
            rho, u = moments(f, field(fields[part], 0, x, row) > 0.0)
            if last_halo:
                if column == 2:
                    put_far(send_l, 0, rows, -1, f, rho, u)
                elif column == 5:
                    put_far(send_r, 0, rows, 1, f, rho, u)
            elif column == 2:
                put_all(send_l, rows, f)
            elif column == 3:
                put_far(send_l, 19, rows, -1, f, rho, u)
            elif column == 4:
                put_far(send_r, 19, rows, 1, f, rho, u)
            else:
                put_all(send_r, rows, f)
            shear_b = shear_b + by_unit(
                shear(links_in[column - 2, near, :], square(u)), field(fields[part], 4, x, row)
            )
    send_all(send, row_pick([sublane_total(s) for s in (shear_a, shear_b)]))


def last_kernel(h_l, h_r, g_hl, g_a, g_b, g_hr, bits_in, rad_l, rad_r, own_post, density, velocity, post):
    fields = g_hl, g_a, g_b, g_hr = fields_of(g_hl, g_a, g_b, g_hr)
    top = (WIDE - MID) // 2
    collide_far(h_l, 0, 1, g_hl, 1, top, every(rad_l[...], 0), MID, post, 0)
    collide_far(h_r, 0, -1, g_hr, 0, top, every(rad_r[...], 0), MID, post, 1)
    held = {1: (post, 0), 6: (post, 1)} | {2 + k: (own_post, k) for k in range(4)}
    own = pl.ds(TILE, TILE)
    for column in range(2, 6):
        part, x = divmod(column, 2)
        f = pulled(held, column, PAD + (MID - TILE) // 2, bits_in[column - 1, own, :])
        rho, u = moments(f, field(fields[part], 0, x, TILE) > 0.0)
        density[column - 2] = rho
        for k in range(3):
            velocity[k, column - 2] = u[k]


def call(kernel, outs, scratch=(), scalars=0, mib=1, plain_out=False, aliases=()):
    vmem = pl.BlockSpec(memory_space=pltpu.VMEM)
    smem = pl.BlockSpec(memory_space=pltpu.SMEM)

    def run(*args):
        args = args[:scalars] + tuple(
            pltpu.with_memory_space_constraint(a, pltpu.VMEM) for a in args[scalars:]
        )
        held = jax.ShapeDtypeStruct if plain_out else pltpu.VMEM
        return pl.pallas_call(
            kernel,
            out_shape=[held(shape, dtype) for shape, dtype in outs],
            in_specs=[smem] * scalars + [vmem] * (len(args) - scalars),
            out_specs=[vmem] * len(outs),
            scratch_shapes=[pltpu.VMEM(shape, dtype) for shape, dtype in scratch],
            input_output_aliases=dict(aliases),
            compiler_params=pltpu.CompilerParams(vmem_limit_bytes=mib << 20),
        )(*args)

    return run


def step_all(density, velocity, fluid_mask, unit_of_column, radius_base):
    count = lax.axis_size(GY)
    place = lax.axis_index(GY)
    at_x = lax.axis_index("gx")
    edge = jnp.stack([at_x > 0, at_x < lax.axis_size("gx") - 1]).astype(jnp.int32)
    tile = ((TILE, LANES), F32)
    sends = ((count, TILE, LANES), F32)

    def ring(low, high):
        size = lax.axis_size("gx")
        up = [(i, (i + 1) % size) for i in range(size)]
        down = [(target, source) for source, target in up]
        before = lax.ppermute(high, "gx", up)
        after = lax.ppermute(low, "gx", down)
        return before, after

    def exchange(blocks):
        return lax.all_to_all(blocks, GY, split_axis=0, concat_axis=0, tiled=True)

    arrays = (density, velocity, fluid_mask, unit_of_column, radius_base.reshape(1, -1))
    anywhere = pl.BlockSpec(memory_space=pl.ANY)
    own, base_send = pl.pallas_call(
        gather_kernel,
        out_shape=[pltpu.VMEM((5, 4, TILE, LANES), F32), jax.ShapeDtypeStruct(*sends)],
        in_specs=[pl.BlockSpec(memory_space=pltpu.SMEM)] + [anywhere] * 5,
        out_specs=[pl.BlockSpec(memory_space=pltpu.VMEM), anywhere],
        scratch_shapes=[pltpu.VMEM(a.shape, a.dtype) for a in arrays]
        + [pltpu.VMEM(*sends), pltpu.SemaphoreType.DMA((6,))],
        compiler_params=pltpu.CompilerParams(vmem_limit_bytes=1 << 20),
    )(place.reshape(1), *(pltpu.with_memory_space_constraint(a, pltpu.HBM) for a in arrays))
    base_in = exchange(base_send)

    forward = [(i, i + 1) for i in range(count - 1)]
    backward = [(target, source) for source, target in forward]
    low = lax.ppermute(own, GY, forward)
    high = lax.ppermute(own, GY, backward)
    pair = ((len(OWN_PLANES) * WIDE + TILE, LANES), F32)
    near_far = ((len(NEAR_FAR) * WIDE + TILE, LANES), F32)
    g_l, g_r, go_l, go_r = call(rows_kernel, [pair, pair, near_far, near_far])(low, own, high, base_in)
    g_hl, g_hr = ring(go_l, go_r)
    fields = (g_hl, g_l, g_r, g_hr)

    def posts(columns, rows):
        return ((19, columns, rows + 2 * PAD, LANES), F32)

    def opens(columns):
        return ((3, columns, WIDE + 2 * PAD, LANES), jnp.int32)

    def populations(rows):
        return [((19, 2, rows, LANES), F32)] * 2

    def halos(rows, last=False):
        return [((FAR if last else 19 + FAR, rows, LANES), F32)] * 2

    shared = [
        *populations(WIDE),
        *halos(WIDE),
        ((6, WIDE, LANES), jnp.int32),
        ((4, WIDE, LANES), F32),
    ]
    post_own, open_own, *begun, sums = call(
        first_own_kernel, [posts(4, WIDE), opens(4), *shared, ((3, TILE, LANES), F32)]
    )(g_l, g_r)
    f_l, f_r, send_l, send_r, bits, links, send, base = call(
        first_kernel,
        [*shared, sends, tile],
        [posts(2, WIDE), opens(4)],
        scalars=1,
        mib=3,
        aliases=[(8 + k, k) for k in range(6)],
    )(edge, *fields, post_own, open_own, sums, *begun)

    for turn in range(3):
        gathered = exchange(send)
        h_l, h_r = ring(send_l, send_r)
        if turn == 0:
            rad, link_tile = call(response_kernel, [tile, tile])(gathered, base, base)
        else:
            (rad,) = call(response_kernel, [tile])(gathered, base, link_tile)
        rad_l, rad_r = ring(rad, rad)
        if turn < 2:
            rows = WIDE if turn == 0 else MID
            own_part = call(
                functools.partial(two_own_kernel, n_rows=rows), [posts(4, rows), posts(2, MID), tile]
            )(f_l, f_r, g_l, g_r, bits, links, rad)
            f_l, f_r, send_l, send_r, send = call(
                functools.partial(two_steps_kernel, n_rows=rows, last_halo=turn == 1),
                [*populations(MID), *halos(MID, last=turn == 1), sends],
                [posts(4, rows), posts(4, MID)],
                mib=4,
            )(h_l, h_r, *fields, bits, links, rad, rad_l, rad_r, *own_part)
    (own_post,) = call(functools.partial(own_kernel, n_rows=MID, row=0), [posts(4, MID)])(
        f_l, f_r, g_l, g_r, rad
    )
    density_out, velocity_out = call(
        last_kernel,
        [((4, TILE, LANES), F32), ((3, 4, TILE, LANES), F32)],
        [posts(2, MID)],
        mib=2,
        plain_out=True,
    )(h_l, h_r, *fields, bits, rad_l, rad_r, own_post)
    own_radius = lax.dynamic_slice_in_dim(rad[1], place * UNIT_DEV, UNIT_DEV)
    return density_out, velocity_out, own_radius


def solution(mesh):
    finer = Mesh(mesh.devices.reshape(mesh.shape["gx"], 4, -1), ("gx", "gy_0", "gy_1"))
    placed = (P("gx", GY, None), P(None, "gx", GY, None), P("gx", GY, None), P("gx", GY), P(GX_GY))
    return jax.shard_map(
        step_all,
        mesh=finer,
        in_specs=placed,
        out_specs=(P("gx", GY, None), P(None, "gx", GY, None), P(GX_GY)),
        check_vma=False,
    )
```

```python
import functools

import jax
import jax.numpy as jnp
from jax import lax
from jax.experimental import pallas as pl
from jax.experimental.pallas import tpu as pltpu
from jax.sharding import Mesh
from jax.sharding import PartitionSpec as P


UNIT_DEV = 8
GX_GY = ("gx", "gy_0", "gy_1")
GY = ("gy_0", "gy_1")

LATTICE = (
    (0, 0, 0),
    (1, 0, 0),
    (-1, 0, 0),
    (0, 1, 0),
    (0, -1, 0),
    (0, 0, 1),
    (0, 0, -1),
    (1, 1, 0),
    (-1, -1, 0),
    (1, -1, 0),
    (-1, 1, 0),
    (1, 0, 1),
    (-1, 0, -1),
    (1, 0, -1),
    (-1, 0, 1),
    (0, 1, 1),
    (0, -1, -1),
    (0, 1, -1),
    (0, -1, 1),
)
PAIRS = tuple(range(1, 19, 2))
WEIGHTS = (1.0 / 3.0,) + (1.0 / 18.0,) * 6 + (1.0 / 36.0,) * 12
RELAX_RATE = 1.25
DRIVE_SCALE = 0.002
F32 = jnp.float32

TILE = 8
LANES = 128
PAD = 8
WIDE = 24
MID = 16
OWN_PLANES = {(k, x): 2 * k + x for k in range(5) for x in range(2)}
NEAR_FAR = {(k, 0): k for k in range(5)} | {(0, 1): 5, (4, 1): 6}
LEFT_PLANES = {(k, 1 - x): plane for (k, x), plane in NEAR_FAR.items()}
TOWARD = {side: tuple(i for i in range(19) if LATTICE[i][0] == side) for side in (-1, 1)}
FAR = 9


def opposite(direction):
    if direction == 0:
        return 0
    return direction + 1 if direction % 2 == 1 else direction - 1


def dot_c(direction, vector):
    total = None
    for c, v in zip(LATTICE[direction], vector):
        if c != 0:
            term = v if c > 0 else -v
            total = term if total is None else total + term
    return total


def moments(f, fluid):
    rho = f[0]
    momentum = [None, None, None]
    for i in PAIRS:
        rho = rho + (f[i] + f[i + 1])
        diff = f[i] - f[i + 1]
        for k in range(3):
            c = LATTICE[i][k]
            if c != 0:
                term = diff if c > 0 else -diff
                momentum[k] = term if momentum[k] is None else momentum[k] + term
    inverse = jnp.where(fluid, 1.0 / rho, 0.0)
    return jnp.where(fluid, rho, 0.0), [m * inverse for m in momentum]


def square(u):
    return u[0] * u[0] + u[1] * u[1] + u[2] * u[2]


def relaxed(f, rho, u, speed_sq, drive):
    rate = 1.0 if f is None else RELAX_RATE
    scaled = rate * rho
    even_base = scaled * (1.0 - 1.5 * speed_sq)
    force = drive * rho
    post = [None] * 19
    rest = WEIGHTS[0] * even_base
    post[0] = rest if f is None else rest + (1.0 - RELAX_RATE) * f[0]
    per_weight = {}
    for w in (WEIGHTS[1], WEIGHTS[7]):
        per_weight[w] = (w * even_base, (4.5 * w) * scaled, (3.0 * w) * scaled, (3.0 * w) * force)
    for i in PAIRS:
        base, quadratic, linear, push = per_weight[WEIGHTS[i]]
        cu = dot_c(i, u)
        even = base + quadratic * (cu * cu)
        odd = linear * cu
        if LATTICE[i][2] > 0:
            odd = odd + push
        elif LATTICE[i][2] < 0:
            odd = odd - push
        post[i] = even + odd
        post[i + 1] = even - odd
        if f is not None:
            post[i] = post[i] + (1.0 - RELAX_RATE) * f[i]
            post[i + 1] = post[i + 1] + (1.0 - RELAX_RATE) * f[i + 1]
    return post


def relaxed_some(directions, f, rho, u, drive):
    scaled = RELAX_RATE * rho
    base = scaled * (1.0 - 1.5 * square(u))
    force = drive * rho
    post = []
    for i, population in zip(directions, f):
        cu = dot_c(i, u)
        value = base + scaled * (4.5 * (cu * cu) + 3.0 * cu)
        if LATTICE[i][2] != 0:
            value = value + (3.0 * LATTICE[i][2]) * force
        post.append(WEIGHTS[i] * value + (1.0 - RELAX_RATE) * population)
    return post


def field(held, k, x, row):
    ref, planes = held
    return ref[pl.ds(planes[k, x] * WIDE + row, TILE), :]


def base_of(held):
    ref, planes = held
    return ref[pl.ds(len(planes) * WIDE, TILE), :]


def fields_of(halo_l, left, right, halo_r):
    return ((halo_l, LEFT_PLANES), (left, OWN_PLANES), (right, OWN_PLANES), (halo_r, NEAR_FAR))


def put_all(out, rows, f):
    for i in range(19):
        out[i, rows, :] = f[i]


def put_far(out, first, rows, side, f, rho, u):
    values = [f[i] for i in TOWARD[side]] + [rho] + list(u)
    for n, value in enumerate(values):
        out[first + n, rows, :] = value


def collide_far(halo, first, side, field_ref, x, row_in_fields, radius, n_rows, post, slot):
    for t in range(n_rows // TILE):
        rows = pl.ds(t * TILE, TILE)
        f = [halo[first + n, rows, :] for n in range(5)]
        rho = halo[first + 5, rows, :]
        u = [halo[first + 6 + k, rows, :] for k in range(3)]
        drive = drive_of(radius, field(field_ref, 4, x, row_in_fields + t * TILE))
        values = relaxed_some(TOWARD[side], f, rho, u, drive)
        for i, value in zip(TOWARD[side], values):
            post[i, slot, pl.ds(PAD + t * TILE, TILE), :] = value


def rolled(x, step):
    if step == 0:
        return x
    return pltpu.roll(x, step % LANES, axis=1)


def pulled(held, column, row, bits):
    def load(i, at_column, at_row):
        ref, slot = held[at_column]
        return ref[i, slot, pl.ds(at_row, TILE), :]

    f = [load(0, column, row)]
    for i in range(1, 19):
        cx, cy, cz = LATTICE[i]
        source = rolled(load(i, column - cx, row - cy), cz)
        bounced = load(opposite(i), column, row)
        f.append(jnp.where((bits & (1 << i)) != 0, source, bounced))
    return f


def drive_of(radius_row, unit):
    radius = jnp.take_along_axis(radius_row, unit.astype(jnp.int32), axis=1)
    return DRIVE_SCALE * radius * radius


def shear(links, speed_sq):
    return jnp.where(links > 0.0, links * speed_sq, 0.0)


def by_unit(column_values, unit):
    total = jnp.sum(column_values, axis=1, keepdims=True)
    lane = lax.broadcasted_iota(jnp.int32, (TILE, LANES), 1)
    return jnp.where(unit.astype(jnp.int32) == lane, total, 0.0)


def sublane_total(x):
    return jnp.broadcast_to(jnp.sum(x, axis=0, keepdims=True), (TILE, LANES))


def row_pick(rows):
    sub = lax.broadcasted_iota(jnp.int32, (TILE, LANES), 0)
    out = jnp.zeros((TILE, LANES), F32)
    for k, value in enumerate(rows):
        out = jnp.where(sub == k, value, out)
    return out


def every(tile, k):
    return jnp.broadcast_to(tile[k : k + 1, :], (TILE, LANES))


def send_all(ref, tile):
    for j in range(ref.shape[0]):
        ref[j] = tile


def send_off(send, send_v, sem, sums):
    send_all(send_v, row_pick([sublane_total(v) for v in sums]))
    store = pltpu.make_async_copy(send_v, send, sem)
    store.start()
    return store


def sum_of(ref):
    parts = [ref[j] for j in range(ref.shape[0])]
    while len(parts) > 1:
        parts = [a + b for a, b in zip(parts[::2], parts[1::2])] + (
            [parts[-1]] if len(parts) % 2 else []
        )
    return parts[0]


def gather_kernel(
    place_ref, density, velocity, mask, unit, radius, out, send, density_v, velocity_v, mask_v, unit_v, radius_v, send_v, sems
):
    pairs = ((radius, radius_v), (density, density_v), (velocity, velocity_v), (mask, mask_v), (unit, unit_v))
    loads = [pltpu.make_async_copy(a, b, sems.at[n]) for n, (a, b) in enumerate(pairs)]
    for load in loads:
        load.start()
    lane = lax.broadcasted_iota(jnp.int32, (TILE, LANES), 1)
    narrow = (TILE, TILE)
    diagonal = lax.broadcasted_iota(jnp.int32, narrow, 0) == lax.broadcasted_iota(jnp.int32, narrow, 1)
    loads[0].wait()
    radii = jnp.broadcast_to(radius_v[...], narrow)
    column = jnp.sum(jnp.where(diagonal, radii, 0.0), axis=1, keepdims=True)
    sub = lax.broadcasted_iota(jnp.int32, (TILE, LANES), 0)
    spread = jnp.where(lane == place_ref[0] * UNIT_DEV + sub, column, 0.0)
    send_all(send_v, sublane_total(spread))
    store = pltpu.make_async_copy(send_v, send, sems.at[5])
    store.start()
    for load in loads[1:]:
        load.wait()
    for x in range(4):
        out[0, x] = jnp.where(mask_v[x] != 0, density_v[x], 0.0)
        for k in range(3):
            out[1 + k, x] = velocity_v[k, x]
        units = jnp.broadcast_to(unit_v[x : x + 1, :].astype(F32), narrow)
        column = jnp.sum(jnp.where(diagonal, units, 0.0), axis=1, keepdims=True)
        out[4, x] = jnp.broadcast_to(column, (TILE, LANES))
    store.wait()


def rows_kernel(odd_ref, first, own, second, base_in, left_out, right_out, left_send, right_send):
    base = sum_of(base_in)
    odd = odd_ref[0] == 1
    for half, out, send, planes in (
        (0, left_out, left_send, NEAR_FAR),
        (1, right_out, right_send, LEFT_PLANES),
    ):
        for (k, x), plane in OWN_PLANES.items():
            here, a, b = (ref[k, 2 * half + x] for ref in (own, first, second))
            for part, value in enumerate((jnp.where(odd, a, b), here, jnp.where(odd, b, a))):
                out[pl.ds(plane * WIDE + part * TILE, TILE), :] = value
                if (k, x) in planes:
                    send[pl.ds(planes[k, x] * WIDE + part * TILE, TILE), :] = value
        out[pl.ds(len(OWN_PLANES) * WIDE, TILE), :] = base
        send[pl.ds(len(planes) * WIDE, TILE), :] = base


def mark_open(open_, slot, column_fields, x, inside):
    lane = lax.broadcasted_iota(jnp.int32, (TILE, LANES), 1)
    zero = jnp.zeros((TILE, LANES), jnp.int32)
    for k in range(3):
        open_[k, slot, pl.ds(0, TILE), :] = zero
        open_[k, slot, pl.ds(PAD + WIDE, TILE), :] = zero
    for t in range(WIDE // TILE):
        here = (field(column_fields, 0, x, t * TILE) > 0.0).astype(jnp.int32)
        if inside is not None:
            here = here * inside
        rows = pl.ds(PAD + t * TILE, TILE)
        open_[0, slot, rows, :] = here
        open_[1, slot, rows, :] = jnp.where(lane == 0, 0, pltpu.roll(here, 1, axis=1))
        open_[2, slot, rows, :] = jnp.where(lane == LANES - 1, 0, pltpu.roll(here, LANES - 1, axis=1))


def start_column(post, slot, column_fields, x, radius, directions):
    for t in range(WIDE // TILE):
        rho = field(column_fields, 0, x, t * TILE)
        u = [field(column_fields, 1 + k, x, t * TILE) for k in range(3)]
        drive = drive_of(radius, field(column_fields, 4, x, t * TILE))
        values = relaxed(None, rho, u, square(u), drive)
        for i in directions:
            post[i, slot, pl.ds(PAD + t * TILE, TILE), :] = values[i]


def stream_first(post, open_, column, held, x, f_out, send_near, send_far, side, links_out, bits_out, tiles):
    sums = None
    for t in tiles:
        row = PAD + t * TILE
        rows = pl.ds(t * TILE, TILE)
        bits, count = open_bits(open_, column, row)
        bits_out[column - 1, rows, :] = bits
        f = pulled(post, column, row, bits)
        put_all(f_out.at[:, x], rows, f)
        fluid = field(held, 0, x, t * TILE) > 0.0
        if t == 1 or send_far is not None:
            rho, u = moments(f, fluid)
        if send_far is not None:
            put_far(send_far, 19, rows, side, f, rho, u)
        else:
            put_all(send_near, rows, f)
        if t != 1:
            links_out[column - 2, rows, :] = jnp.zeros((TILE, LANES), F32)
            continue
        links = jnp.where(fluid, (18 - count).astype(F32), 0.0)
        links_out[column - 2, rows, :] = links
        unit = field(held, 4, x, t * TILE)
        start = [field(held, 1 + k, x, t * TILE) for k in range(3)]
        sums = [by_unit(v, unit) for v in (links * square(start), links * square(u), links)]
    return sums


def open_bits(open_, column, row):
    bits = count = jnp.zeros((TILE, LANES), jnp.int32)
    for i in range(1, 19):
        cx, cy, cz = LATTICE[i]
        ref, slot = open_[column - cx]
        seen = ref[cz % 3, slot, pl.ds(row - cy, TILE), :]
        count = count + seen
        bits = bits | (seen << i)
    return bits, count


def first_own_kernel(left, right, post, open_, f_l, f_r, send_l, send_r, bits_out, links_out, sums_out):
    pairs = ((left, OWN_PLANES), (right, OWN_PLANES))
    for column in range(4):
        part, x = divmod(column, 2)
        start_column(post, column, pairs[part], x, base_of(pairs[part]), range(19))
        mark_open(open_, column, pairs[part], x, None)
    held = {2 + k: (post, k) for k in range(4)}
    seen = {2 + k: (open_, k) for k in range(4)}
    tiles = range(WIDE // TILE)
    sums_a = stream_first(held, seen, 3, pairs[0], 1, f_l, None, send_l, -1, links_out, bits_out, tiles)
    sums_b = stream_first(held, seen, 4, pairs[1], 0, f_r, None, send_r, 1, links_out, bits_out, tiles)
    for k in range(3):
        sums_out[k] = sums_a[k] + sums_b[k]


def first_kernel(
    edge_ref, halo_l, left, right, halo_r, post_own, open_own, sums_in, *rest
):
    f_l, f_r, send_l, send_r, bits_out, links_out, send, base_out, post_halo, open_halo, send_v, sem = rest[6:]
    fields = fields_of(halo_l, left, right, halo_r)
    base_out[...] = base_of(fields[1])
    post = {1: (post_halo, 0), 6: (post_halo, 1)} | {2 + k: (post_own, k) for k in range(4)}
    open_ = {0: (open_halo, 0), 1: (open_halo, 1), 6: (open_halo, 2), 7: (open_halo, 3)}
    open_ |= {2 + k: (open_own, k) for k in range(4)}
    for x in range(2):
        mark_open(open_halo, x, fields[0], x, edge_ref[0])
        mark_open(open_halo, 2 + x, fields[3], x, edge_ref[1])
    start_column(post_halo, 0, fields[0], 1, base_of(fields[0]), TOWARD[1])
    start_column(post_halo, 1, fields[3], 0, base_of(fields[3]), TOWARD[-1])
    outer = ((2, fields[1], 0, f_l, send_l), (5, fields[2], 1, f_r, send_r))
    sums = [sums_in[k] for k in range(3)]
    for column, held, x, f_out, near in outer:
        part = stream_first(post, open_, column, held, x, f_out, near, None, None, links_out, bits_out, (1,))
        sums = [a + b for a, b in zip(sums, part)]
    store = send_off(send, send_v, sem, sums)
    for column, held, x, f_out, near in outer:
        stream_first(post, open_, column, held, x, f_out, near, None, None, links_out, bits_out, (0, 2))
    for column in (1, 6):
        for t in range(WIDE // TILE):
            bits_out[column - 1, pl.ds(t * TILE, TILE), :] = open_bits(open_, column, PAD + t * TILE)[0]
    store.wait()


def response_kernel(gathered, base, links_in, radius_out, links_out=None):
    totals = sum_of(gathered)
    if links_out is None:
        links = links_in[...]
    else:
        links = every(totals, 2)
        links_out[...] = links
    mean = 100.0 * totals / jnp.maximum(links, 1.0)
    radius_out[...] = every(base[...], 0) * (0.6 + 0.8 * jnp.tanh(mean))


def collide_all(populations, field_ref, x, radius, row_in_fields, n_rows, post, slot):
    for t in range(n_rows // TILE):
        rows = pl.ds(t * TILE, TILE)
        near = row_in_fields + t * TILE
        f = [populations(i, rows) for i in range(19)]
        rho, u = moments(f, field(field_ref, 0, x, near) > 0.0)
        drive = drive_of(radius, field(field_ref, 4, x, near))
        values = relaxed(f, rho, u, square(u), drive)
        for i in range(19):
            post[i, slot, pl.ds(PAD + t * TILE, TILE), :] = values[i]


def in_pair(ref, x):
    return lambda i, rows: ref[i, x, rows, :]


def in_halo(ref):
    return lambda i, rows: ref[i, rows, :]


def own_kernel(a, b, g_a, g_b, rad, post, *, n_rows, row):
    radius = every(rad[...], row)
    for column in range(4):
        part, x = divmod(column, 2)
        collide_all(
            in_pair((a, b)[part], x), ((g_a, g_b)[part], OWN_PLANES), x, radius, (WIDE - n_rows) // 2, n_rows, post, column
        )


def advance(held, column, field_ref, x, links, bits_in, radius, skip, side, post, slot):
    sums = jnp.zeros((TILE, LANES), F32)
    for t in range(MID // TILE):
        row = (WIDE - MID) // 2 + t * TILE
        near = pl.ds(row, TILE)
        rows = pl.ds(PAD + t * TILE, TILE)
        f = pulled(held, column, PAD + skip + t * TILE, bits_in[column - 1, near, :])
        rho, u = moments(f, field(field_ref, 0, x, row) > 0.0)
        unit = field(field_ref, 4, x, row)
        drive = drive_of(radius, unit)
        if side is not None:
            chosen = TOWARD[side]
            values = relaxed_some(chosen, [f[i] for i in chosen], rho, u, drive)
        else:
            chosen = range(19)
            speed_sq = square(u)
            sums = sums + by_unit(shear(links[column - 2, near, :], speed_sq), unit)
            values = relaxed(f, rho, u, speed_sq, drive)
        for i, value in zip(chosen, values):
            post[i, slot, rows, :] = value
    return sums


def two_own_kernel(a, b, g_a, g_b, bits_in, links_in, rad, post_a, post_b, shear_out, *, n_rows):
    own_kernel(a, b, g_a, g_b, rad, post_a, n_rows=n_rows, row=0)
    held = {2 + k: (post_a, k) for k in range(4)}
    second = every(rad[...], 1)
    skip = (n_rows - MID) // 2
    shear_out[...] = advance(
        held, 3, (g_a, OWN_PLANES), 1, links_in, bits_in, second, skip, None, post_b, 0
    ) + advance(held, 4, (g_b, OWN_PLANES), 0, links_in, bits_in, second, skip, None, post_b, 1)


def two_steps_kernel(
    h_l, h_r, g_hl, g_a, g_b, g_hr, bits_in, links_in, rad, rad_l, rad_r, own_a, own_b, shear_in,
    f_l, f_r, send_l, send_r, send, post_a, post_b, send_v, sem, *, n_rows, last_halo,
):
    fields = g_hl, g_a, g_b, g_hr = fields_of(g_hl, g_a, g_b, g_hr)
    top = (WIDE - n_rows) // 2
    skip = (n_rows - MID) // 2
    collide_all(in_halo(h_l), g_hl, 1, every(rad_l[...], 0), top, n_rows, post_a, 1)
    collide_all(in_halo(h_r), g_hr, 0, every(rad_r[...], 0), top, n_rows, post_a, 2)
    collide_far(h_l, 19, 1, g_hl, 0, top, every(rad_l[...], 0), n_rows, post_a, 0)
    collide_far(h_r, 19, -1, g_hr, 1, top, every(rad_r[...], 0), n_rows, post_a, 3)
    held = {0: (post_a, 0), 1: (post_a, 1), 6: (post_a, 2), 7: (post_a, 3)}
    held |= {2 + k: (own_a, k) for k in range(4)}
    own = every(rad[...], 1)
    shear_a = shear_in[...]
    shear_b = jnp.zeros((TILE, LANES), F32)
    advance(held, 1, g_hl, 1, links_in, bits_in, every(rad_l[...], 1), skip, 1, post_b, 0)
    advance(held, 6, g_hr, 0, links_in, bits_in, every(rad_r[...], 1), skip, -1, post_b, 3)
    shear_a += advance(held, 2, g_a, 0, links_in, bits_in, own, skip, None, post_b, 1)
    shear_a += advance(held, 5, g_b, 1, links_in, bits_in, own, skip, None, post_b, 2)
    held = {1: (post_b, 0), 2: (post_b, 1), 3: (own_b, 0), 4: (own_b, 1), 5: (post_b, 2), 6: (post_b, 3)}
    own = pl.ds(TILE, TILE)
    for column in range(2, 6):
        part, x = divmod(column, 2)
        f = pulled(held, column, PAD + (MID - TILE) // 2, bits_in[column - 1, own, :])
        _, u = moments(f, field(fields[part], 0, x, TILE) > 0.0)
        shear_b += by_unit(links_in[column - 2, own, :] * square(u), field(fields[part], 4, x, TILE))
    store = send_off(send, send_v, sem, (shear_a, shear_b))
    for column in range(2, 6):
        part, x = divmod(column, 2)
        out = f_l if part == 1 else f_r
        for t in range(MID // TILE):
            row = (WIDE - MID) // 2 + t * TILE
            near = pl.ds(row, TILE)
            rows = pl.ds(t * TILE, TILE)
            f = pulled(held, column, PAD + t * TILE, bits_in[column - 1, near, :])
            for i in range(19):
                out[i, x, rows, :] = f[i]
            if column in ((2, 5) if last_halo else (3, 4)):
                rho, u = moments(f, field(fields[part], 0, x, row) > 0.0)
            if last_halo:
                if column == 2:
                    put_far(send_l, 0, rows, -1, f, rho, u)
                elif column == 5:
                    put_far(send_r, 0, rows, 1, f, rho, u)
            elif column == 2:
                put_all(send_l, rows, f)
            elif column == 3:
                put_far(send_l, 19, rows, -1, f, rho, u)
            elif column == 4:
                put_far(send_r, 19, rows, 1, f, rho, u)
            else:
                put_all(send_r, rows, f)
    store.wait()


def last_kernel(h_l, h_r, g_hl, g_a, g_b, g_hr, bits_in, rad_l, rad_r, own_post, density, velocity, post):
    fields = g_hl, g_a, g_b, g_hr = fields_of(g_hl, g_a, g_b, g_hr)
    top = (WIDE - MID) // 2
    collide_far(h_l, 0, 1, g_hl, 1, top, every(rad_l[...], 0), MID, post, 0)
    collide_far(h_r, 0, -1, g_hr, 0, top, every(rad_r[...], 0), MID, post, 1)
    held = {1: (post, 0), 6: (post, 1)} | {2 + k: (own_post, k) for k in range(4)}
    own = pl.ds(TILE, TILE)
    for column in range(2, 6):
        part, x = divmod(column, 2)
        f = pulled(held, column, PAD + (MID - TILE) // 2, bits_in[column - 1, own, :])
        rho, u = moments(f, field(fields[part], 0, x, TILE) > 0.0)
        density[column - 2] = rho
        for k in range(3):
            velocity[k, column - 2] = u[k]


def call(kernel, outs, scratch=(), scalars=0, mib=1, plain_out=False, aliases=(), hbm_out=None):
    vmem = pl.BlockSpec(memory_space=pltpu.VMEM)
    smem = pl.BlockSpec(memory_space=pltpu.SMEM)

    def run(*args):
        args = args[:scalars] + tuple(
            pltpu.with_memory_space_constraint(a, pltpu.VMEM) for a in args[scalars:]
        )
        held = jax.ShapeDtypeStruct if plain_out else pltpu.VMEM
        return pl.pallas_call(
            kernel,
            out_shape=[
                (jax.ShapeDtypeStruct if n == hbm_out else held)(shape, dtype) for n, (shape, dtype) in enumerate(outs)
            ],
            in_specs=[smem] * scalars + [vmem] * (len(args) - scalars),
            out_specs=[pl.BlockSpec(memory_space=pl.ANY) if n == hbm_out else vmem for n in range(len(outs))],
            scratch_shapes=[pltpu.VMEM(shape, dtype) for shape, dtype in scratch]
            + ([] if hbm_out is None else [pltpu.VMEM(*outs[hbm_out]), pltpu.SemaphoreType.DMA]),
            input_output_aliases=dict(aliases),
            compiler_params=pltpu.CompilerParams(vmem_limit_bytes=mib << 20),
        )(*args)

    return run


def step_all(density, velocity, fluid_mask, unit_of_column, radius_base):
    count = lax.axis_size(GY)
    place = lax.axis_index(GY)
    at_x = lax.axis_index("gx")
    edge = jnp.stack([at_x > 0, at_x < lax.axis_size("gx") - 1]).astype(jnp.int32)
    tile = ((TILE, LANES), F32)
    sends = ((count, TILE, LANES), F32)

    def ring(low, high):
        size = lax.axis_size("gx")
        up = [(i, (i + 1) % size) for i in range(size)]
        down = [(target, source) for source, target in up]
        before = lax.ppermute(high, "gx", up)
        after = lax.ppermute(low, "gx", down)
        return before, after

    def exchange(blocks):
        return lax.all_to_all(blocks, GY, split_axis=0, concat_axis=0, tiled=True)

    arrays = (density, velocity, fluid_mask, unit_of_column, radius_base.reshape(1, -1))
    anywhere = pl.BlockSpec(memory_space=pl.ANY)
    own, base_send = pl.pallas_call(
        gather_kernel,
        out_shape=[pltpu.VMEM((5, 4, TILE, LANES), F32), jax.ShapeDtypeStruct(*sends)],
        in_specs=[pl.BlockSpec(memory_space=pltpu.SMEM)] + [anywhere] * 5,
        out_specs=[pl.BlockSpec(memory_space=pltpu.VMEM), anywhere],
        scratch_shapes=[pltpu.VMEM(a.shape, a.dtype) for a in arrays]
        + [pltpu.VMEM(*sends), pltpu.SemaphoreType.DMA((6,))],
        compiler_params=pltpu.CompilerParams(vmem_limit_bytes=1 << 20),
    )(place.reshape(1), *(pltpu.with_memory_space_constraint(a, pltpu.HBM) for a in arrays))
    base_in = exchange(base_send)

    def swap(start):
        pairs = [(i, i + 1) for i in range(start, count - 1, 2)]
        return lax.ppermute(own, GY, pairs + [(b, a) for a, b in pairs])

    swaps = swap(0), swap(1)
    pair = ((len(OWN_PLANES) * WIDE + TILE, LANES), F32)
    near_far = ((len(NEAR_FAR) * WIDE + TILE, LANES), F32)
    g_l, g_r, go_l, go_r = call(rows_kernel, [pair, pair, near_far, near_far], scalars=1)(
        (place % 2).reshape(1), swaps[0], own, swaps[1], base_in
    )
    g_hl, g_hr = ring(go_l, go_r)
    fields = (g_hl, g_l, g_r, g_hr)

    def posts(columns, rows):
        return ((19, columns, rows + 2 * PAD, LANES), F32)

    def opens(columns):
        return ((3, columns, WIDE + 2 * PAD, LANES), jnp.int32)

    def populations(rows):
        return [((19, 2, rows, LANES), F32)] * 2

    def halos(rows, last=False):
        return [((FAR if last else 19 + FAR, rows, LANES), F32)] * 2

    shared = [
        *populations(WIDE),
        *halos(WIDE),
        ((6, WIDE, LANES), jnp.int32),
        ((4, WIDE, LANES), F32),
    ]
    post_own, open_own, *begun, sums = call(
        first_own_kernel, [posts(4, WIDE), opens(4), *shared, ((3, TILE, LANES), F32)]
    )(g_l, g_r)
    f_l, f_r, send_l, send_r, bits, links, send, base = call(
        first_kernel,
        [*shared, sends, tile],
        [posts(2, WIDE), opens(4)],
        scalars=1,
        mib=3,
        hbm_out=6,
        aliases=[(8 + k, k) for k in range(6)],
    )(edge, *fields, post_own, open_own, sums, *begun)

    for turn in range(3):
        gathered = exchange(send)
        h_l, h_r = ring(send_l, send_r)
        if turn == 0:
            rad, link_tile = call(response_kernel, [tile, tile])(gathered, base, base)
        else:
            (rad,) = call(response_kernel, [tile])(gathered, base, link_tile)
        rad_l, rad_r = ring(rad, rad)
        if turn < 2:
            rows = WIDE if turn == 0 else MID
            own_part = call(
                functools.partial(two_own_kernel, n_rows=rows), [posts(4, rows), posts(2, MID), tile]
            )(f_l, f_r, g_l, g_r, bits, links, rad)
            f_l, f_r, send_l, send_r, send = call(
                functools.partial(two_steps_kernel, n_rows=rows, last_halo=turn == 1),
                [*populations(MID), *halos(MID, last=turn == 1), sends],
                [posts(4, rows), posts(4, MID)],
                mib=4,
                hbm_out=4,
            )(h_l, h_r, *fields, bits, links, rad, rad_l, rad_r, *own_part)
    (own_post,) = call(functools.partial(own_kernel, n_rows=MID, row=0), [posts(4, MID)])(
        f_l, f_r, g_l, g_r, rad
    )
    density_out, velocity_out = call(
        last_kernel,
        [((4, TILE, LANES), F32), ((3, 4, TILE, LANES), F32)],
        [posts(2, MID)],
        mib=2,
        plain_out=True,
    )(h_l, h_r, *fields, bits, rad_l, rad_r, own_post)
    own_radius = lax.dynamic_slice_in_dim(rad[1], place * UNIT_DEV, UNIT_DEV)
    return density_out, velocity_out, own_radius


def solution(mesh):
    finer = Mesh(mesh.devices.reshape(mesh.shape["gx"], 4, -1), ("gx", "gy_0", "gy_1"))
    placed = (P("gx", GY, None), P(None, "gx", GY, None), P("gx", GY, None), P("gx", GY), P(GX_GY))
    return jax.shard_map(
        step_all,
        mesh=finer,
        in_specs=placed,
        out_specs=(P("gx", GY, None), P(None, "gx", GY, None), P(GX_GY)),
        check_vma=False,
    )
```

```python
import functools

import jax
import jax.numpy as jnp
from jax import lax
from jax.experimental import pallas as pl
from jax.experimental.pallas import tpu as pltpu
from jax.sharding import Mesh
from jax.sharding import PartitionSpec as P


UNIT_DEV = 8
GX_GY = ("gx", "gy_0", "gy_1")
GY = ("gy_0", "gy_1")

LATTICE = (
    (0, 0, 0),
    (1, 0, 0),
    (-1, 0, 0),
    (0, 1, 0),
    (0, -1, 0),
    (0, 0, 1),
    (0, 0, -1),
    (1, 1, 0),
    (-1, -1, 0),
    (1, -1, 0),
    (-1, 1, 0),
    (1, 0, 1),
    (-1, 0, -1),
    (1, 0, -1),
    (-1, 0, 1),
    (0, 1, 1),
    (0, -1, -1),
    (0, 1, -1),
    (0, -1, 1),
)
PAIRS = tuple(range(1, 19, 2))
WEIGHTS = (1.0 / 3.0,) + (1.0 / 18.0,) * 6 + (1.0 / 36.0,) * 12
RELAX_RATE = 1.25
DRIVE_SCALE = 0.002
F32 = jnp.float32

TILE = 8
LANES = 128
HALO = 6
Y_ROWS = 16 * HALO + TILE
PAD = 8
WIDE = 24
MID = 16
OWN_PLANES = {(k, x): 2 * k + x for k in range(5) for x in range(2)}
NEAR_FAR = {(k, 0): k for k in range(5)} | {(0, 1): 5, (4, 1): 6}
LEFT_PLANES = {(k, 1 - x): plane for (k, x), plane in NEAR_FAR.items()}
TOWARD = {side: tuple(i for i in range(19) if LATTICE[i][0] == side) for side in (-1, 1)}
FAR = 9


def opposite(direction):
    if direction == 0:
        return 0
    return direction + 1 if direction % 2 == 1 else direction - 1


def dot_c(direction, vector):
    total = None
    for c, v in zip(LATTICE[direction], vector):
        if c != 0:
            term = v if c > 0 else -v
            total = term if total is None else total + term
    return total


def moments(f, fluid):
    rho = f[0]
    momentum = [None, None, None]
    for i in PAIRS:
        rho = rho + (f[i] + f[i + 1])
        diff = f[i] - f[i + 1]
        for k in range(3):
            c = LATTICE[i][k]
            if c != 0:
                term = diff if c > 0 else -diff
                momentum[k] = term if momentum[k] is None else momentum[k] + term
    inverse = jnp.where(fluid, 1.0 / rho, 0.0)
    return jnp.where(fluid, rho, 0.0), [m * inverse for m in momentum]


def square(u):
    return u[0] * u[0] + u[1] * u[1] + u[2] * u[2]


def relaxed(f, rho, u, speed_sq, drive):
    rate = 1.0 if f is None else RELAX_RATE
    scaled = rate * rho
    even_base = scaled * (1.0 - 1.5 * speed_sq)
    force = drive * rho
    post = [None] * 19
    rest = WEIGHTS[0] * even_base
    post[0] = rest if f is None else rest + (1.0 - RELAX_RATE) * f[0]
    per_weight = {}
    for w in (WEIGHTS[1], WEIGHTS[7]):
        per_weight[w] = (w * even_base, (4.5 * w) * scaled, (3.0 * w) * scaled, (3.0 * w) * force)
    for i in PAIRS:
        base, quadratic, linear, push = per_weight[WEIGHTS[i]]
        cu = dot_c(i, u)
        even = base + quadratic * (cu * cu)
        odd = linear * cu
        if LATTICE[i][2] > 0:
            odd = odd + push
        elif LATTICE[i][2] < 0:
            odd = odd - push
        post[i] = even + odd
        post[i + 1] = even - odd
        if f is not None:
            post[i] = post[i] + (1.0 - RELAX_RATE) * f[i]
            post[i + 1] = post[i + 1] + (1.0 - RELAX_RATE) * f[i + 1]
    return post


def relaxed_some(directions, f, rho, u, drive):
    scaled = RELAX_RATE * rho
    base = scaled * (1.0 - 1.5 * square(u))
    force = drive * rho
    post = []
    for i, population in zip(directions, f):
        cu = dot_c(i, u)
        value = base + scaled * (4.5 * (cu * cu) + 3.0 * cu)
        if LATTICE[i][2] != 0:
            value = value + (3.0 * LATTICE[i][2]) * force
        post.append(WEIGHTS[i] * value + (1.0 - RELAX_RATE) * population)
    return post


def field(held, k, x, row):
    ref, planes = held
    return ref[pl.ds(planes[k, x] * WIDE + row, TILE), :]


def base_of(held):
    ref, planes = held
    return ref[pl.ds(len(planes) * WIDE, TILE), :]


def fields_of(halo_l, left, right, halo_r):
    return ((halo_l, LEFT_PLANES), (left, OWN_PLANES), (right, OWN_PLANES), (halo_r, NEAR_FAR))


def put_all(out, rows, f):
    for i in range(19):
        out[i, rows, :] = f[i]


def put_far(out, first, rows, side, f, rho, u):
    values = [f[i] for i in TOWARD[side]] + [rho] + list(u)
    for n, value in enumerate(values):
        out[first + n, rows, :] = value


def collide_far(halo, first, side, field_ref, x, row_in_fields, radius, n_rows, post, slot):
    for t in range(n_rows // TILE):
        rows = pl.ds(t * TILE, TILE)
        f = [halo[first + n, rows, :] for n in range(5)]
        rho = halo[first + 5, rows, :]
        u = [halo[first + 6 + k, rows, :] for k in range(3)]
        drive = drive_of(radius, field(field_ref, 4, x, row_in_fields + t * TILE))
        values = relaxed_some(TOWARD[side], f, rho, u, drive)
        for i, value in zip(TOWARD[side], values):
            post[i, slot, pl.ds(PAD + t * TILE, TILE), :] = value


def rolled(x, step):
    if step == 0:
        return x
    return pltpu.roll(x, step % LANES, axis=1)


def pulled(held, column, row, bits):
    def load(i, at_column, at_row):
        ref, slot = held[at_column]
        return ref[i, slot, pl.ds(at_row, TILE), :]

    f = [load(0, column, row)]
    for i in range(1, 19):
        cx, cy, cz = LATTICE[i]
        source = rolled(load(i, column - cx, row - cy), cz)
        bounced = load(opposite(i), column, row)
        f.append(jnp.where((bits & (1 << i)) != 0, source, bounced))
    return f


def drive_of(radius_row, unit):
    radius = jnp.take_along_axis(radius_row, unit.astype(jnp.int32), axis=1)
    return DRIVE_SCALE * radius * radius


def shear(links, speed_sq):
    return jnp.where(links > 0.0, links * speed_sq, 0.0)


def by_unit(column_values, unit):
    total = jnp.sum(column_values, axis=1, keepdims=True)
    lane = lax.broadcasted_iota(jnp.int32, (TILE, LANES), 1)
    return jnp.where(unit.astype(jnp.int32) == lane, total, 0.0)


def sublane_total(x):
    return jnp.broadcast_to(jnp.sum(x, axis=0, keepdims=True), (TILE, LANES))


def row_pick(rows):
    sub = lax.broadcasted_iota(jnp.int32, (TILE, LANES), 0)
    out = jnp.zeros((TILE, LANES), F32)
    for k, value in enumerate(rows):
        out = jnp.where(sub == k, value, out)
    return out


def every(tile, k):
    return jnp.broadcast_to(tile[k : k + 1, :], (TILE, LANES))


def send_all(ref, tile):
    for j in range(ref.shape[0]):
        ref[j] = tile


def send_off(send, send_v, sem, sums):
    send_all(send_v, row_pick([sublane_total(v) for v in sums]))
    store = pltpu.make_async_copy(send_v, send, sem)
    store.start()
    return store


def sum_of(ref):
    parts = [ref[j] for j in range(ref.shape[0])]
    while len(parts) > 1:
        parts = [a + b for a, b in zip(parts[::2], parts[1::2])] + (
            [parts[-1]] if len(parts) % 2 else []
        )
    return parts[0]


def gather_kernel(
    place_ref, density, velocity, mask, unit, radius, out, first, second, send, density_v, velocity_v, mask_v, unit_v, radius_v, send_v, sems
):
    pairs = ((radius, radius_v), (density, density_v), (velocity, velocity_v), (mask, mask_v), (unit, unit_v))
    loads = [pltpu.make_async_copy(a, b, sems.at[n]) for n, (a, b) in enumerate(pairs)]
    for load in loads:
        load.start()
    lane = lax.broadcasted_iota(jnp.int32, (TILE, LANES), 1)
    narrow = (TILE, TILE)
    diagonal = lax.broadcasted_iota(jnp.int32, narrow, 0) == lax.broadcasted_iota(jnp.int32, narrow, 1)
    loads[0].wait()
    radii = jnp.broadcast_to(radius_v[...], narrow)
    column = jnp.sum(jnp.where(diagonal, radii, 0.0), axis=1, keepdims=True)
    sub = lax.broadcasted_iota(jnp.int32, (TILE, LANES), 0)
    spread = jnp.where(lane == place_ref[0] * UNIT_DEV + sub, column, 0.0)
    send_all(send_v, sublane_total(spread))
    store = pltpu.make_async_copy(send_v, send, sems.at[5])
    store.start()
    for load in loads[1:]:
        load.wait()
    odd = (place_ref[0] & 1) == 1
    unit_tile = jnp.zeros((TILE, LANES), F32)
    for x in range(4):
        out[0, x] = jnp.where(mask_v[x] != 0, density_v[x], 0.0)
        for k in range(3):
            out[1 + k, x] = velocity_v[k, x]
        units = jnp.broadcast_to(unit_v[x : x + 1, :].astype(F32), narrow)
        column = jnp.sum(jnp.where(diagonal, units, 0.0), axis=1, keepdims=True)
        out[4, x] = jnp.broadcast_to(column, (TILE, LANES))
        unit_tile = jnp.where(lane == x, column, unit_tile)
    for k in range(4):
        for x in range(4):
            to_before = out[k, x, pl.ds(0, HALO), :]
            to_after = out[k, x, pl.ds(TILE - HALO, HALO), :]
            rows = pl.ds((4 * k + x) * HALO, HALO)
            first[rows, :] = jnp.where(odd, to_before, to_after)
            second[rows, :] = jnp.where(odd, to_after, to_before)
    for ref in (first, second):
        ref[pl.ds(16 * HALO, TILE), :] = unit_tile
    store.wait()


def rows_kernel(odd_ref, first, own, second, base_in, left_out, right_out, left_send, right_send):
    base = sum_of(base_in)
    odd = odd_ref[0] == 1
    zero = jnp.zeros((TILE, LANES), F32)
    lane = lax.broadcasted_iota(jnp.int32, (TILE, LANES), 1)

    def unit_column(ref, column):
        picked = jnp.where(lane == column, ref[pl.ds(16 * HALO, TILE), :], 0.0)
        return jnp.broadcast_to(jnp.sum(picked, axis=1, keepdims=True), (TILE, LANES))

    for half, out, send, planes in (
        (0, left_out, left_send, NEAR_FAR),
        (1, right_out, right_send, LEFT_PLANES),
    ):
        for (k, x), plane in OWN_PLANES.items():
            column = 2 * half + x
            targets = [(out, plane)] + ([(send, planes[k, x])] if (k, x) in planes else [])
            if k < 4:
                rows = pl.ds((4 * k + column) * HALO, HALO)
                a, b = first[rows, :], second[rows, :]
            else:
                a, b = (unit_column(ref, column) for ref in (first, second))
            before, after = jnp.where(odd, a, b), jnp.where(odd, b, a)
            for ref, at in targets:
                at = at * WIDE
                if k < 4:
                    ref[pl.ds(at, TILE), :] = zero
                    ref[pl.ds(at + 2 * TILE, TILE), :] = zero
                ref[pl.ds(at + TILE - before.shape[0], before.shape[0]), :] = before
                ref[pl.ds(at + TILE, TILE), :] = own[k, column]
                ref[pl.ds(at + 2 * TILE, after.shape[0]), :] = after
        out[pl.ds(len(OWN_PLANES) * WIDE, TILE), :] = base
        send[pl.ds(len(planes) * WIDE, TILE), :] = base


def mark_open(open_, slot, column_fields, x, inside):
    lane = lax.broadcasted_iota(jnp.int32, (TILE, LANES), 1)
    zero = jnp.zeros((TILE, LANES), jnp.int32)
    for k in range(3):
        open_[k, slot, pl.ds(0, TILE), :] = zero
        open_[k, slot, pl.ds(PAD + WIDE, TILE), :] = zero
    for t in range(WIDE // TILE):
        here = (field(column_fields, 0, x, t * TILE) > 0.0).astype(jnp.int32)
        if inside is not None:
            here = here * inside
        rows = pl.ds(PAD + t * TILE, TILE)
        open_[0, slot, rows, :] = here
        open_[1, slot, rows, :] = jnp.where(lane == 0, 0, pltpu.roll(here, 1, axis=1))
        open_[2, slot, rows, :] = jnp.where(lane == LANES - 1, 0, pltpu.roll(here, LANES - 1, axis=1))


def start_column(post, slot, column_fields, x, radius, directions):
    for t in range(WIDE // TILE):
        rho = field(column_fields, 0, x, t * TILE)
        u = [field(column_fields, 1 + k, x, t * TILE) for k in range(3)]
        drive = drive_of(radius, field(column_fields, 4, x, t * TILE))
        values = relaxed(None, rho, u, square(u), drive)
        for i in directions:
            post[i, slot, pl.ds(PAD + t * TILE, TILE), :] = values[i]


def stream_first(post, open_, column, held, x, f_out, send_near, send_far, side, links_out, bits_out, tiles):
    sums = None
    for t in tiles:
        row = PAD + t * TILE
        rows = pl.ds(t * TILE, TILE)
        bits, count = open_bits(open_, column, row)
        bits_out[column - 1, rows, :] = bits
        f = pulled(post, column, row, bits)
        put_all(f_out.at[:, x], rows, f)
        fluid = field(held, 0, x, t * TILE) > 0.0
        if t == 1 or send_far is not None:
            rho, u = moments(f, fluid)
        if send_far is not None:
            put_far(send_far, 19, rows, side, f, rho, u)
        else:
            put_all(send_near, rows, f)
        if t != 1:
            links_out[column - 2, rows, :] = jnp.zeros((TILE, LANES), F32)
            continue
        links = jnp.where(fluid, (18 - count).astype(F32), 0.0)
        links_out[column - 2, rows, :] = links
        unit = field(held, 4, x, t * TILE)
        start = [field(held, 1 + k, x, t * TILE) for k in range(3)]
        sums = [by_unit(v, unit) for v in (links * square(start), links * square(u), links)]
    return sums


def open_bits(open_, column, row):
    bits = count = jnp.zeros((TILE, LANES), jnp.int32)
    for i in range(1, 19):
        cx, cy, cz = LATTICE[i]
        ref, slot = open_[column - cx]
        seen = ref[cz % 3, slot, pl.ds(row - cy, TILE), :]
        count = count + seen
        bits = bits | (seen << i)
    return bits, count


def first_own_kernel(left, right, post, open_, f_l, f_r, send_l, send_r, bits_out, links_out, sums_out):
    pairs = ((left, OWN_PLANES), (right, OWN_PLANES))
    for column in range(4):
        part, x = divmod(column, 2)
        start_column(post, column, pairs[part], x, base_of(pairs[part]), range(19))
        mark_open(open_, column, pairs[part], x, None)
    held = {2 + k: (post, k) for k in range(4)}
    seen = {2 + k: (open_, k) for k in range(4)}
    tiles = range(WIDE // TILE)
    sums_a = stream_first(held, seen, 3, pairs[0], 1, f_l, None, send_l, -1, links_out, bits_out, tiles)
    sums_b = stream_first(held, seen, 4, pairs[1], 0, f_r, None, send_r, 1, links_out, bits_out, tiles)
    for k in range(3):
        sums_out[k] = sums_a[k] + sums_b[k]


def first_kernel(
    edge_ref, halo_l, left, right, halo_r, post_own, open_own, sums_in, *rest
):
    f_l, f_r, send_l, send_r, bits_out, links_out, send, base_out, post_halo, open_halo, send_v, sem = rest[6:]
    fields = fields_of(halo_l, left, right, halo_r)
    base_out[...] = base_of(fields[1])
    post = {1: (post_halo, 0), 6: (post_halo, 1)} | {2 + k: (post_own, k) for k in range(4)}
    open_ = {0: (open_halo, 0), 1: (open_halo, 1), 6: (open_halo, 2), 7: (open_halo, 3)}
    open_ |= {2 + k: (open_own, k) for k in range(4)}
    for x in range(2):
        mark_open(open_halo, x, fields[0], x, edge_ref[0])
        mark_open(open_halo, 2 + x, fields[3], x, edge_ref[1])
    start_column(post_halo, 0, fields[0], 1, base_of(fields[0]), TOWARD[1])
    start_column(post_halo, 1, fields[3], 0, base_of(fields[3]), TOWARD[-1])
    outer = ((2, fields[1], 0, f_l, send_l), (5, fields[2], 1, f_r, send_r))
    sums = [sums_in[k] for k in range(3)]
    for column, held, x, f_out, near in outer:
        part = stream_first(post, open_, column, held, x, f_out, near, None, None, links_out, bits_out, (1,))
        sums = [a + b for a, b in zip(sums, part)]
    store = send_off(send, send_v, sem, sums)
    for column, held, x, f_out, near in outer:
        stream_first(post, open_, column, held, x, f_out, near, None, None, links_out, bits_out, (0, 2))
    for column in (1, 6):
        for t in range(WIDE // TILE):
            bits_out[column - 1, pl.ds(t * TILE, TILE), :] = open_bits(open_, column, PAD + t * TILE)[0]
    store.wait()


def response_kernel(gathered, base, links_in, radius_out, links_out=None):
    totals = sum_of(gathered)
    if links_out is None:
        links = links_in[...]
    else:
        links = every(totals, 2)
        links_out[...] = links
    mean = 100.0 * totals / jnp.maximum(links, 1.0)
    radius_out[...] = every(base[...], 0) * (0.6 + 0.8 * jnp.tanh(mean))


def collide_all(populations, field_ref, x, radius, row_in_fields, n_rows, post, slot):
    for t in range(n_rows // TILE):
        rows = pl.ds(t * TILE, TILE)
        near = row_in_fields + t * TILE
        f = [populations(i, rows) for i in range(19)]
        rho, u = moments(f, field(field_ref, 0, x, near) > 0.0)
        drive = drive_of(radius, field(field_ref, 4, x, near))
        values = relaxed(f, rho, u, square(u), drive)
        for i in range(19):
            post[i, slot, pl.ds(PAD + t * TILE, TILE), :] = values[i]


def in_pair(ref, x):
    return lambda i, rows: ref[i, x, rows, :]


def in_halo(ref):
    return lambda i, rows: ref[i, rows, :]


def own_kernel(a, b, g_a, g_b, rad, post, *, n_rows, row):
    radius = every(rad[...], row)
    for column in range(4):
        part, x = divmod(column, 2)
        collide_all(
            in_pair((a, b)[part], x), ((g_a, g_b)[part], OWN_PLANES), x, radius, (WIDE - n_rows) // 2, n_rows, post, column
        )


def advance(held, column, field_ref, x, links, bits_in, radius, skip, side, post, slot):
    sums = jnp.zeros((TILE, LANES), F32)
    for t in range(MID // TILE):
        row = (WIDE - MID) // 2 + t * TILE
        near = pl.ds(row, TILE)
        rows = pl.ds(PAD + t * TILE, TILE)
        f = pulled(held, column, PAD + skip + t * TILE, bits_in[column - 1, near, :])
        rho, u = moments(f, field(field_ref, 0, x, row) > 0.0)
        unit = field(field_ref, 4, x, row)
        drive = drive_of(radius, unit)
        if side is not None:
            chosen = TOWARD[side]
            values = relaxed_some(chosen, [f[i] for i in chosen], rho, u, drive)
        else:
            chosen = range(19)
            speed_sq = square(u)
            sums = sums + by_unit(shear(links[column - 2, near, :], speed_sq), unit)
            values = relaxed(f, rho, u, speed_sq, drive)
        for i, value in zip(chosen, values):
            post[i, slot, rows, :] = value
    return sums


def two_own_kernel(a, b, g_a, g_b, bits_in, links_in, rad, post_a, post_b, shear_out, *, n_rows):
    own_kernel(a, b, g_a, g_b, rad, post_a, n_rows=n_rows, row=0)
    held = {2 + k: (post_a, k) for k in range(4)}
    second = every(rad[...], 1)
    skip = (n_rows - MID) // 2
    shear_out[...] = advance(
        held, 3, (g_a, OWN_PLANES), 1, links_in, bits_in, second, skip, None, post_b, 0
    ) + advance(held, 4, (g_b, OWN_PLANES), 0, links_in, bits_in, second, skip, None, post_b, 1)


def two_steps_kernel(
    h_l, h_r, g_hl, g_a, g_b, g_hr, bits_in, links_in, rad, rad_l, rad_r, own_a, own_b, shear_in,
    f_l, f_r, send_l, send_r, send, post_a, post_b, send_v, sem, *, n_rows, last_halo,
):
    fields = g_hl, g_a, g_b, g_hr = fields_of(g_hl, g_a, g_b, g_hr)
    top = (WIDE - n_rows) // 2
    skip = (n_rows - MID) // 2
    collide_all(in_halo(h_l), g_hl, 1, every(rad_l[...], 0), top, n_rows, post_a, 1)
    collide_all(in_halo(h_r), g_hr, 0, every(rad_r[...], 0), top, n_rows, post_a, 2)
    collide_far(h_l, 19, 1, g_hl, 0, top, every(rad_l[...], 0), n_rows, post_a, 0)
    collide_far(h_r, 19, -1, g_hr, 1, top, every(rad_r[...], 0), n_rows, post_a, 3)
    held = {0: (post_a, 0), 1: (post_a, 1), 6: (post_a, 2), 7: (post_a, 3)}
    held |= {2 + k: (own_a, k) for k in range(4)}
    own = every(rad[...], 1)
    shear_a = shear_in[...]
    shear_b = jnp.zeros((TILE, LANES), F32)
    advance(held, 1, g_hl, 1, links_in, bits_in, every(rad_l[...], 1), skip, 1, post_b, 0)
    advance(held, 6, g_hr, 0, links_in, bits_in, every(rad_r[...], 1), skip, -1, post_b, 3)
    shear_a += advance(held, 2, g_a, 0, links_in, bits_in, own, skip, None, post_b, 1)
    shear_a += advance(held, 5, g_b, 1, links_in, bits_in, own, skip, None, post_b, 2)
    held = {1: (post_b, 0), 2: (post_b, 1), 3: (own_b, 0), 4: (own_b, 1), 5: (post_b, 2), 6: (post_b, 3)}
    own = pl.ds(TILE, TILE)
    for column in range(2, 6):
        part, x = divmod(column, 2)
        f = pulled(held, column, PAD + (MID - TILE) // 2, bits_in[column - 1, own, :])
        _, u = moments(f, field(fields[part], 0, x, TILE) > 0.0)
        shear_b += by_unit(links_in[column - 2, own, :] * square(u), field(fields[part], 4, x, TILE))
    store = send_off(send, send_v, sem, (shear_a, shear_b))
    for column in range(2, 6):
        part, x = divmod(column, 2)
        out = f_l if part == 1 else f_r
        for t in range(MID // TILE):
            row = (WIDE - MID) // 2 + t * TILE
            near = pl.ds(row, TILE)
            rows = pl.ds(t * TILE, TILE)
            f = pulled(held, column, PAD + t * TILE, bits_in[column - 1, near, :])
            for i in range(19):
                out[i, x, rows, :] = f[i]
            if column in ((2, 5) if last_halo else (3, 4)):
                rho, u = moments(f, field(fields[part], 0, x, row) > 0.0)
            if last_halo:
                if column == 2:
                    put_far(send_l, 0, rows, -1, f, rho, u)
                elif column == 5:
                    put_far(send_r, 0, rows, 1, f, rho, u)
            elif column == 2:
                put_all(send_l, rows, f)
            elif column == 3:
                put_far(send_l, 19, rows, -1, f, rho, u)
            elif column == 4:
                put_far(send_r, 19, rows, 1, f, rho, u)
            else:
                put_all(send_r, rows, f)
    store.wait()


def last_kernel(h_l, h_r, g_hl, g_a, g_b, g_hr, bits_in, rad_l, rad_r, own_post, density, velocity, post):
    fields = g_hl, g_a, g_b, g_hr = fields_of(g_hl, g_a, g_b, g_hr)
    top = (WIDE - MID) // 2
    collide_far(h_l, 0, 1, g_hl, 1, top, every(rad_l[...], 0), MID, post, 0)
    collide_far(h_r, 0, -1, g_hr, 0, top, every(rad_r[...], 0), MID, post, 1)
    held = {1: (post, 0), 6: (post, 1)} | {2 + k: (own_post, k) for k in range(4)}
    own = pl.ds(TILE, TILE)
    for column in range(2, 6):
        part, x = divmod(column, 2)
        f = pulled(held, column, PAD + (MID - TILE) // 2, bits_in[column - 1, own, :])
        rho, u = moments(f, field(fields[part], 0, x, TILE) > 0.0)
        density[column - 2] = rho
        for k in range(3):
            velocity[k, column - 2] = u[k]


def call(kernel, outs, scratch=(), scalars=0, mib=1, plain_out=False, aliases=(), hbm_out=None):
    vmem = pl.BlockSpec(memory_space=pltpu.VMEM)
    smem = pl.BlockSpec(memory_space=pltpu.SMEM)

    def run(*args):
        args = args[:scalars] + tuple(
            pltpu.with_memory_space_constraint(a, pltpu.VMEM) for a in args[scalars:]
        )
        held = jax.ShapeDtypeStruct if plain_out else pltpu.VMEM
        return pl.pallas_call(
            kernel,
            out_shape=[
                (jax.ShapeDtypeStruct if n == hbm_out else held)(shape, dtype) for n, (shape, dtype) in enumerate(outs)
            ],
            in_specs=[smem] * scalars + [vmem] * (len(args) - scalars),
            out_specs=[pl.BlockSpec(memory_space=pl.ANY) if n == hbm_out else vmem for n in range(len(outs))],
            scratch_shapes=[pltpu.VMEM(shape, dtype) for shape, dtype in scratch]
            + ([] if hbm_out is None else [pltpu.VMEM(*outs[hbm_out]), pltpu.SemaphoreType.DMA]),
            input_output_aliases=dict(aliases),
            compiler_params=pltpu.CompilerParams(vmem_limit_bytes=mib << 20),
        )(*args)

    return run


def step_all(density, velocity, fluid_mask, unit_of_column, radius_base):
    count = lax.axis_size(GY)
    place = lax.axis_index(GY)
    at_x = lax.axis_index("gx")
    edge = jnp.stack([at_x > 0, at_x < lax.axis_size("gx") - 1]).astype(jnp.int32)
    tile = ((TILE, LANES), F32)
    sends = ((count, TILE, LANES), F32)

    def ring(low, high):
        size = lax.axis_size("gx")
        up = [(i, (i + 1) % size) for i in range(size)]
        down = [(target, source) for source, target in up]
        before = lax.ppermute(high, "gx", up)
        after = lax.ppermute(low, "gx", down)
        return before, after

    def exchange(blocks):
        return lax.all_to_all(blocks, GY, split_axis=0, concat_axis=0, tiled=True)

    arrays = (density, velocity, fluid_mask, unit_of_column, radius_base.reshape(1, -1))
    anywhere = pl.BlockSpec(memory_space=pl.ANY)
    own, to_first, to_second, base_send = pl.pallas_call(
        gather_kernel,
        out_shape=[pltpu.VMEM((5, 4, TILE, LANES), F32)]
        + [pltpu.VMEM((Y_ROWS, LANES), F32)] * 2
        + [jax.ShapeDtypeStruct(*sends)],
        in_specs=[pl.BlockSpec(memory_space=pltpu.SMEM)] + [anywhere] * 5,
        out_specs=[pl.BlockSpec(memory_space=pltpu.VMEM)] * 3 + [anywhere],
        scratch_shapes=[pltpu.VMEM(a.shape, a.dtype) for a in arrays]
        + [pltpu.VMEM(*sends), pltpu.SemaphoreType.DMA((6,))],
        compiler_params=pltpu.CompilerParams(vmem_limit_bytes=1 << 20),
    )(place.reshape(1), *(pltpu.with_memory_space_constraint(a, pltpu.HBM) for a in arrays))
    base_in = exchange(base_send)

    def swap(start, rows):
        pairs = [(i, i + 1) for i in range(start, count - 1, 2)]
        return lax.ppermute(rows, GY, pairs + [(b, a) for a, b in pairs])

    swaps = swap(0, to_first), swap(1, to_second)
    pair = ((len(OWN_PLANES) * WIDE + TILE, LANES), F32)
    near_far = ((len(NEAR_FAR) * WIDE + TILE, LANES), F32)
    g_l, g_r, go_l, go_r = call(rows_kernel, [pair, pair, near_far, near_far], scalars=1)(
        (place & 1).reshape(1), swaps[0], own, swaps[1], base_in
    )
    g_hl, g_hr = ring(go_l, go_r)
    fields = (g_hl, g_l, g_r, g_hr)

    def posts(columns, rows):
        return ((19, columns, rows + 2 * PAD, LANES), F32)

    def opens(columns):
        return ((3, columns, WIDE + 2 * PAD, LANES), jnp.int32)

    def populations(rows):
        return [((19, 2, rows, LANES), F32)] * 2

    def halos(rows, last=False):
        return [((FAR if last else 19 + FAR, rows, LANES), F32)] * 2

    shared = [
        *populations(WIDE),
        *halos(WIDE),
        ((6, WIDE, LANES), jnp.int32),
        ((4, WIDE, LANES), F32),
    ]
    post_own, open_own, *begun, sums = call(
        first_own_kernel, [posts(4, WIDE), opens(4), *shared, ((3, TILE, LANES), F32)]
    )(g_l, g_r)
    f_l, f_r, send_l, send_r, bits, links, send, base = call(
        first_kernel,
        [*shared, sends, tile],
        [posts(2, WIDE), opens(4)],
        scalars=1,
        mib=3,
        hbm_out=6,
        aliases=[(8 + k, k) for k in range(6)],
    )(edge, *fields, post_own, open_own, sums, *begun)

    for turn in range(3):
        gathered = exchange(send)
        h_l, h_r = ring(send_l, send_r)
        if turn == 0:
            rad, link_tile = call(response_kernel, [tile, tile])(gathered, base, base)
        else:
            (rad,) = call(response_kernel, [tile])(gathered, base, link_tile)
        rad_l, rad_r = ring(rad, rad)
        if turn < 2:
            rows = WIDE if turn == 0 else MID
            own_part = call(
                functools.partial(two_own_kernel, n_rows=rows), [posts(4, rows), posts(2, MID), tile]
            )(f_l, f_r, g_l, g_r, bits, links, rad)
            f_l, f_r, send_l, send_r, send = call(
                functools.partial(two_steps_kernel, n_rows=rows, last_halo=turn == 1),
                [*populations(MID), *halos(MID, last=turn == 1), sends],
                [posts(4, rows), posts(4, MID)],
                mib=4,
                hbm_out=4,
            )(h_l, h_r, *fields, bits, links, rad, rad_l, rad_r, *own_part)
    (own_post,) = call(functools.partial(own_kernel, n_rows=MID, row=0), [posts(4, MID)])(
        f_l, f_r, g_l, g_r, rad
    )
    density_out, velocity_out = call(
        last_kernel,
        [((4, TILE, LANES), F32), ((3, 4, TILE, LANES), F32)],
        [posts(2, MID)],
        mib=2,
        plain_out=True,
    )(h_l, h_r, *fields, bits, rad_l, rad_r, own_post)
    own_radius = lax.dynamic_slice_in_dim(rad[1], place * UNIT_DEV, UNIT_DEV)
    return density_out, velocity_out, own_radius


def solution(mesh):
    finer = Mesh(mesh.devices.reshape(mesh.shape["gx"], 4, -1), ("gx", "gy_0", "gy_1"))
    placed = (P("gx", GY, None), P(None, "gx", GY, None), P("gx", GY, None), P("gx", GY), P(GX_GY))
    return jax.shard_map(
        step_all,
        mesh=finer,
        in_specs=placed,
        out_specs=(P("gx", GY, None), P(None, "gx", GY, None), P(GX_GY)),
        check_vma=False,
    )
```

```python
import functools

import jax
import jax.numpy as jnp
from jax import lax
from jax.experimental import pallas as pl
from jax.experimental.pallas import tpu as pltpu
from jax.sharding import Mesh
from jax.sharding import PartitionSpec as P


UNIT_DEV = 8
GX_GY = ("gx", "gy_0", "gy_1")
GY = ("gy_0", "gy_1")

LATTICE = (
    (0, 0, 0),
    (1, 0, 0),
    (-1, 0, 0),
    (0, 1, 0),
    (0, -1, 0),
    (0, 0, 1),
    (0, 0, -1),
    (1, 1, 0),
    (-1, -1, 0),
    (1, -1, 0),
    (-1, 1, 0),
    (1, 0, 1),
    (-1, 0, -1),
    (1, 0, -1),
    (-1, 0, 1),
    (0, 1, 1),
    (0, -1, -1),
    (0, 1, -1),
    (0, -1, 1),
)
PAIRS = tuple(range(1, 19, 2))
WEIGHTS = (1.0 / 3.0,) + (1.0 / 18.0,) * 6 + (1.0 / 36.0,) * 12
RELAX_RATE = 1.25
DRIVE_SCALE = 0.002
F32 = jnp.float32

TILE = 8
LANES = 128
HALO = 6
Y_ROWS = 16 * HALO + TILE
PAD = 8
WIDE = 24
MID = 16
OWN_PLANES = {(k, x): 2 * k + x for k in range(5) for x in range(2)}
NEAR_FAR = {(k, 0): k for k in range(5)} | {(0, 1): 5, (4, 1): 6}
LEFT_PLANES = {(k, 1 - x): plane for (k, x), plane in NEAR_FAR.items()}
TOWARD = {side: tuple(i for i in range(19) if LATTICE[i][0] == side) for side in (-1, 1)}
FAR = 9


def opposite(direction):
    if direction == 0:
        return 0
    return direction + 1 if direction % 2 == 1 else direction - 1


def dot_c(direction, vector):
    total = None
    for c, v in zip(LATTICE[direction], vector):
        if c != 0:
            term = v if c > 0 else -v
            total = term if total is None else total + term
    return total


def moments(f, fluid):
    rho = f[0]
    momentum = [None, None, None]
    for i in PAIRS:
        rho = rho + (f[i] + f[i + 1])
        diff = f[i] - f[i + 1]
        for k in range(3):
            c = LATTICE[i][k]
            if c != 0:
                term = diff if c > 0 else -diff
                momentum[k] = term if momentum[k] is None else momentum[k] + term
    inverse = jnp.where(fluid, 1.0 / rho, 0.0)
    return jnp.where(fluid, rho, 0.0), [m * inverse for m in momentum]


def square(u):
    return u[0] * u[0] + u[1] * u[1] + u[2] * u[2]


def relaxed(f, rho, u, speed_sq, drive):
    rate = 1.0 if f is None else RELAX_RATE
    scaled = rate * rho
    even_base = scaled * (1.0 - 1.5 * speed_sq)
    force = drive * rho
    post = [None] * 19
    rest = WEIGHTS[0] * even_base
    post[0] = rest if f is None else rest + (1.0 - RELAX_RATE) * f[0]
    per_weight = {}
    for w in (WEIGHTS[1], WEIGHTS[7]):
        per_weight[w] = (w * even_base, (4.5 * w) * scaled, (3.0 * w) * scaled, (3.0 * w) * force)
    for i in PAIRS:
        base, quadratic, linear, push = per_weight[WEIGHTS[i]]
        cu = dot_c(i, u)
        even = base + quadratic * (cu * cu)
        odd = linear * cu
        if LATTICE[i][2] > 0:
            odd = odd + push
        elif LATTICE[i][2] < 0:
            odd = odd - push
        post[i] = even + odd
        post[i + 1] = even - odd
        if f is not None:
            post[i] = post[i] + (1.0 - RELAX_RATE) * f[i]
            post[i + 1] = post[i + 1] + (1.0 - RELAX_RATE) * f[i + 1]
    return post


def relaxed_some(directions, f, rho, u, drive):
    scaled = RELAX_RATE * rho
    base = scaled * (1.0 - 1.5 * square(u))
    force = drive * rho
    post = []
    for i, population in zip(directions, f):
        cu = dot_c(i, u)
        value = base + scaled * (4.5 * (cu * cu) + 3.0 * cu)
        if LATTICE[i][2] != 0:
            value = value + (3.0 * LATTICE[i][2]) * force
        post.append(WEIGHTS[i] * value + (1.0 - RELAX_RATE) * population)
    return post


def field(held, k, x, row):
    ref, planes = held
    return ref[pl.ds(planes[k, x] * WIDE + row, TILE), :]


def base_of(held):
    ref, planes = held
    return ref[pl.ds(len(planes) * WIDE, TILE), :]


def fields_of(halo_l, left, right, halo_r):
    return ((halo_l, LEFT_PLANES), (left, OWN_PLANES), (right, OWN_PLANES), (halo_r, NEAR_FAR))


def put_all(out, rows, f):
    for i in range(19):
        out[i, rows, :] = f[i]


def put_far(out, first, rows, side, f, rho, u):
    values = [f[i] for i in TOWARD[side]] + [rho] + list(u)
    for n, value in enumerate(values):
        out[first + n, rows, :] = value


def collide_far(halo, first, side, field_ref, x, row_in_fields, radius, n_rows, post, slot):
    for t in range(n_rows // TILE):
        rows = pl.ds(t * TILE, TILE)
        f = [halo[first + n, rows, :] for n in range(5)]
        rho = halo[first + 5, rows, :]
        u = [halo[first + 6 + k, rows, :] for k in range(3)]
        drive = drive_of(radius, field(field_ref, 4, x, row_in_fields + t * TILE))
        values = relaxed_some(TOWARD[side], f, rho, u, drive)
        for i, value in zip(TOWARD[side], values):
            post[i, slot, pl.ds(PAD + t * TILE, TILE), :] = value


def rolled(x, step):
    if step == 0:
        return x
    return pltpu.roll(x, step % LANES, axis=1)


def pulled(held, column, row, bits):
    def load(i, at_column, at_row):
        ref, slot = held[at_column]
        return ref[i, slot, pl.ds(at_row, TILE), :]

    f = [load(0, column, row)]
    for i in range(1, 19):
        cx, cy, cz = LATTICE[i]
        source = rolled(load(i, column - cx, row - cy), cz)
        bounced = load(opposite(i), column, row)
        f.append(jnp.where((bits & (1 << i)) != 0, source, bounced))
    return f


def drive_of(radius_row, unit):
    radius = jnp.take_along_axis(radius_row, unit.astype(jnp.int32), axis=1)
    return DRIVE_SCALE * radius * radius


def shear(links, speed_sq):
    return jnp.where(links > 0.0, links * speed_sq, 0.0)


def by_unit(column_values, unit):
    total = jnp.sum(column_values, axis=1, keepdims=True)
    lane = lax.broadcasted_iota(jnp.int32, (TILE, LANES), 1)
    return jnp.where(unit.astype(jnp.int32) == lane, total, 0.0)


def sublane_total(x):
    return jnp.broadcast_to(jnp.sum(x, axis=0, keepdims=True), (TILE, LANES))


def row_pick(rows):
    sub = lax.broadcasted_iota(jnp.int32, (TILE, LANES), 0)
    out = jnp.zeros((TILE, LANES), F32)
    for k, value in enumerate(rows):
        out = jnp.where(sub == k, value, out)
    return out


def every(tile, k):
    return jnp.broadcast_to(tile[k : k + 1, :], (TILE, LANES))


def send_all(ref, tile):
    for j in range(ref.shape[0]):
        ref[j] = tile


def send_off(send, send_v, sem, sums):
    send_all(send_v, row_pick([sublane_total(v) for v in sums]))
    store = pltpu.make_async_copy(send_v, send, sem)
    store.start()
    return store


def sum_of(ref):
    parts = [ref[j] for j in range(ref.shape[0])]
    while len(parts) > 1:
        parts = [a + b for a, b in zip(parts[::2], parts[1::2])] + (
            [parts[-1]] if len(parts) % 2 else []
        )
    return parts[0]


def gather_kernel(
    place_ref, density, velocity, mask, unit, radius, out, first, second, send, density_v, velocity_v, mask_v, unit_v, radius_v, send_v, sems
):
    pairs = ((radius, radius_v), (density, density_v), (velocity, velocity_v), (mask, mask_v), (unit, unit_v))
    loads = [pltpu.make_async_copy(a, b, sems.at[n]) for n, (a, b) in enumerate(pairs)]
    for load in loads:
        load.start()
    lane = lax.broadcasted_iota(jnp.int32, (TILE, LANES), 1)
    narrow = (TILE, TILE)
    diagonal = lax.broadcasted_iota(jnp.int32, narrow, 0) == lax.broadcasted_iota(jnp.int32, narrow, 1)
    loads[0].wait()
    radii = jnp.broadcast_to(radius_v[...], narrow)
    column = jnp.sum(jnp.where(diagonal, radii, 0.0), axis=1, keepdims=True)
    sub = lax.broadcasted_iota(jnp.int32, (TILE, LANES), 0)
    spread = jnp.where(lane == place_ref[0] * UNIT_DEV + sub, column, 0.0)
    send_all(send_v, sublane_total(spread))
    store = pltpu.make_async_copy(send_v, send, sems.at[5])
    store.start()
    for load in loads[1:]:
        load.wait()
    odd = (place_ref[0] & 1) == 1
    unit_tile = jnp.zeros((TILE, LANES), F32)
    for x in range(4):
        out[0, x] = jnp.where(mask_v[x] != 0, density_v[x], 0.0)
        for k in range(3):
            out[1 + k, x] = velocity_v[k, x]
        units = jnp.broadcast_to(unit_v[x : x + 1, :].astype(F32), narrow)
        column = jnp.sum(jnp.where(diagonal, units, 0.0), axis=1, keepdims=True)
        out[4, x] = jnp.broadcast_to(column, (TILE, LANES))
        unit_tile = jnp.where(lane == x, column, unit_tile)
    for k in range(4):
        for x in range(4):
            to_before = out[k, x, pl.ds(0, HALO), :]
            to_after = out[k, x, pl.ds(TILE - HALO, HALO), :]
            rows = pl.ds((4 * k + x) * HALO, HALO)
            first[rows, :] = jnp.where(odd, to_before, to_after)
            second[rows, :] = jnp.where(odd, to_after, to_before)
    for ref in (first, second):
        ref[pl.ds(16 * HALO, TILE), :] = unit_tile
    store.wait()


def rows_kernel(odd_ref, first, own, second, base_in, left_out, right_out, left_send, right_send):
    base = sum_of(base_in)
    odd = odd_ref[0] == 1
    zero = jnp.zeros((TILE, LANES), F32)
    lane = lax.broadcasted_iota(jnp.int32, (TILE, LANES), 1)

    def unit_column(ref, column):
        picked = jnp.where(lane == column, ref[pl.ds(16 * HALO, TILE), :], 0.0)
        return jnp.broadcast_to(jnp.sum(picked, axis=1, keepdims=True), (TILE, LANES))

    for half, out, send, planes in (
        (0, left_out, left_send, NEAR_FAR),
        (1, right_out, right_send, LEFT_PLANES),
    ):
        for (k, x), plane in OWN_PLANES.items():
            column = 2 * half + x
            targets = [(out, plane)] + ([(send, planes[k, x])] if (k, x) in planes else [])
            if k < 4:
                rows = pl.ds((4 * k + column) * HALO, HALO)
                a, b = first[rows, :], second[rows, :]
            else:
                a, b = (unit_column(ref, column) for ref in (first, second))
            before, after = jnp.where(odd, a, b), jnp.where(odd, b, a)
            for ref, at in targets:
                at = at * WIDE
                if k < 4:
                    ref[pl.ds(at, TILE), :] = zero
                    ref[pl.ds(at + 2 * TILE, TILE), :] = zero
                ref[pl.ds(at + TILE - before.shape[0], before.shape[0]), :] = before
                ref[pl.ds(at + TILE, TILE), :] = own[k, column]
                ref[pl.ds(at + 2 * TILE, after.shape[0]), :] = after
        out[pl.ds(len(OWN_PLANES) * WIDE, TILE), :] = base
        send[pl.ds(len(planes) * WIDE, TILE), :] = base


def mark_open(open_, slot, column_fields, x, inside):
    lane = lax.broadcasted_iota(jnp.int32, (TILE, LANES), 1)
    zero = jnp.zeros((TILE, LANES), jnp.int32)
    for k in range(3):
        open_[k, slot, pl.ds(0, TILE), :] = zero
        open_[k, slot, pl.ds(PAD + WIDE, TILE), :] = zero
    for t in range(WIDE // TILE):
        here = (field(column_fields, 0, x, t * TILE) > 0.0).astype(jnp.int32)
        if inside is not None:
            here = here * inside
        rows = pl.ds(PAD + t * TILE, TILE)
        open_[0, slot, rows, :] = here
        open_[1, slot, rows, :] = jnp.where(lane == 0, 0, pltpu.roll(here, 1, axis=1))
        open_[2, slot, rows, :] = jnp.where(lane == LANES - 1, 0, pltpu.roll(here, LANES - 1, axis=1))


def start_column(post, slot, column_fields, x, radius, directions):
    for t in range(WIDE // TILE):
        rho = field(column_fields, 0, x, t * TILE)
        u = [field(column_fields, 1 + k, x, t * TILE) for k in range(3)]
        drive = drive_of(radius, field(column_fields, 4, x, t * TILE))
        values = relaxed(None, rho, u, square(u), drive)
        for i in directions:
            post[i, slot, pl.ds(PAD + t * TILE, TILE), :] = values[i]


def stream_first(post, open_, column, held, x, f_out, send_near, send_far, side, links_out, bits_out, tiles):
    sums = None
    for t in tiles:
        row = PAD + t * TILE
        rows = pl.ds(t * TILE, TILE)
        bits, count = open_bits(open_, column, row)
        bits_out[column - 1, rows, :] = bits
        f = pulled(post, column, row, bits)
        put_all(f_out.at[:, x], rows, f)
        fluid = field(held, 0, x, t * TILE) > 0.0
        if t == 1 or send_far is not None:
            rho, u = moments(f, fluid)
        if send_far is not None:
            put_far(send_far, 19, rows, side, f, rho, u)
        else:
            put_all(send_near, rows, f)
        if t != 1:
            links_out[column - 2, rows, :] = jnp.zeros((TILE, LANES), F32)
            continue
        links = jnp.where(fluid, (18 - count).astype(F32), 0.0)
        links_out[column - 2, rows, :] = links
        unit = field(held, 4, x, t * TILE)
        start = [field(held, 1 + k, x, t * TILE) for k in range(3)]
        sums = [by_unit(v, unit) for v in (links * square(start), links * square(u), links)]
    return sums


def open_bits(open_, column, row):
    bits = count = jnp.zeros((TILE, LANES), jnp.int32)
    for i in range(1, 19):
        cx, cy, cz = LATTICE[i]
        ref, slot = open_[column - cx]
        seen = ref[cz % 3, slot, pl.ds(row - cy, TILE), :]
        count = count + seen
        bits = bits | (seen << i)
    return bits, count


def first_own_kernel(left, right, post, open_, f_l, f_r, send_l, send_r, bits_out, links_out, sums_out):
    pairs = ((left, OWN_PLANES), (right, OWN_PLANES))
    for column in range(4):
        part, x = divmod(column, 2)
        start_column(post, column, pairs[part], x, base_of(pairs[part]), range(19))
        mark_open(open_, column, pairs[part], x, None)
    held = {2 + k: (post, k) for k in range(4)}
    seen = {2 + k: (open_, k) for k in range(4)}
    tiles = range(WIDE // TILE)
    sums_a = stream_first(held, seen, 3, pairs[0], 1, f_l, None, send_l, -1, links_out, bits_out, tiles)
    sums_b = stream_first(held, seen, 4, pairs[1], 0, f_r, None, send_r, 1, links_out, bits_out, tiles)
    for k in range(3):
        sums_out[k] = sums_a[k] + sums_b[k]


def first_kernel(
    edge_ref, halo_l, left, right, halo_r, post_own, open_own, sums_in, *rest
):
    f_l, f_r, send_l, send_r, bits_out, links_out, send, base_out, post_halo, open_halo, send_v, sem = rest[6:]
    fields = fields_of(halo_l, left, right, halo_r)
    base_out[...] = base_of(fields[1])
    post = {1: (post_halo, 0), 6: (post_halo, 1)} | {2 + k: (post_own, k) for k in range(4)}
    open_ = {0: (open_halo, 0), 1: (open_halo, 1), 6: (open_halo, 2), 7: (open_halo, 3)}
    open_ |= {2 + k: (open_own, k) for k in range(4)}
    for x in range(2):
        mark_open(open_halo, x, fields[0], x, edge_ref[0])
        mark_open(open_halo, 2 + x, fields[3], x, edge_ref[1])
    start_column(post_halo, 0, fields[0], 1, base_of(fields[0]), TOWARD[1])
    start_column(post_halo, 1, fields[3], 0, base_of(fields[3]), TOWARD[-1])
    outer = ((2, fields[1], 0, f_l, send_l), (5, fields[2], 1, f_r, send_r))
    sums = [sums_in[k] for k in range(3)]
    for column, held, x, f_out, near in outer:
        part = stream_first(post, open_, column, held, x, f_out, near, None, None, links_out, bits_out, (1,))
        sums = [a + b for a, b in zip(sums, part)]
    store = send_off(send, send_v, sem, sums)
    for column, held, x, f_out, near in outer:
        stream_first(post, open_, column, held, x, f_out, near, None, None, links_out, bits_out, (0, 2))
    for column in (1, 6):
        for t in range(WIDE // TILE):
            bits_out[column - 1, pl.ds(t * TILE, TILE), :] = open_bits(open_, column, PAD + t * TILE)[0]
    store.wait()


def response_kernel(gathered, base, links_in, radius_out, links_out=None):
    totals = sum_of(gathered)
    if links_out is None:
        links = links_in[...]
    else:
        links = every(totals, 2)
        links_out[...] = links
    mean = 100.0 * totals / jnp.maximum(links, 1.0)
    radius_out[...] = every(base[...], 0) * (0.6 + 0.8 * jnp.tanh(mean))


def collide_all(populations, field_ref, x, radius, row_in_fields, n_rows, post, slot):
    for t in range(n_rows // TILE):
        rows = pl.ds(t * TILE, TILE)
        near = row_in_fields + t * TILE
        f = [populations(i, rows) for i in range(19)]
        rho, u = moments(f, field(field_ref, 0, x, near) > 0.0)
        drive = drive_of(radius, field(field_ref, 4, x, near))
        values = relaxed(f, rho, u, square(u), drive)
        for i in range(19):
            post[i, slot, pl.ds(PAD + t * TILE, TILE), :] = values[i]


def in_pair(ref, x):
    return lambda i, rows: ref[i, x, rows, :]


def in_halo(ref):
    return lambda i, rows: ref[i, rows, :]


def own_kernel(a, b, g_a, g_b, rad, post, *, n_rows, row):
    radius = every(rad[...], row)
    for column in range(4):
        part, x = divmod(column, 2)
        collide_all(
            in_pair((a, b)[part], x), ((g_a, g_b)[part], OWN_PLANES), x, radius, (WIDE - n_rows) // 2, n_rows, post, column
        )


def advance(held, column, field_ref, x, links, bits_in, radius, skip, side, post, slot):
    sums = jnp.zeros((TILE, LANES), F32)
    for t in range(MID // TILE):
        row = (WIDE - MID) // 2 + t * TILE
        near = pl.ds(row, TILE)
        rows = pl.ds(PAD + t * TILE, TILE)
        f = pulled(held, column, PAD + skip + t * TILE, bits_in[column - 1, near, :])
        rho, u = moments(f, field(field_ref, 0, x, row) > 0.0)
        unit = field(field_ref, 4, x, row)
        drive = drive_of(radius, unit)
        if side is not None:
            chosen = TOWARD[side]
            values = relaxed_some(chosen, [f[i] for i in chosen], rho, u, drive)
        else:
            chosen = range(19)
            speed_sq = square(u)
            sums = sums + by_unit(shear(links[column - 2, near, :], speed_sq), unit)
            values = relaxed(f, rho, u, speed_sq, drive)
        for i, value in zip(chosen, values):
            post[i, slot, rows, :] = value
    return sums


def two_own_kernel(a, b, g_a, g_b, bits_in, links_in, rad, post_a, post_b, shear_out, *, n_rows):
    own_kernel(a, b, g_a, g_b, rad, post_a, n_rows=n_rows, row=0)
    held = {2 + k: (post_a, k) for k in range(4)}
    second = every(rad[...], 1)
    skip = (n_rows - MID) // 2
    shear_out[...] = advance(
        held, 3, (g_a, OWN_PLANES), 1, links_in, bits_in, second, skip, None, post_b, 0
    ) + advance(held, 4, (g_b, OWN_PLANES), 0, links_in, bits_in, second, skip, None, post_b, 1)


def two_steps_kernel(
    h_l, h_r, g_hl, g_a, g_b, g_hr, bits_in, links_in, rad, rad_l, rad_r, own_a, own_b, shear_in,
    f_l, f_r, send_l, send_r, send, post_a, post_b, send_v, sem, *, n_rows, last_halo,
):
    fields = g_hl, g_a, g_b, g_hr = fields_of(g_hl, g_a, g_b, g_hr)
    top = (WIDE - n_rows) // 2
    skip = (n_rows - MID) // 2
    collide_all(in_halo(h_l), g_hl, 1, every(rad_l[...], 0), top, n_rows, post_a, 1)
    collide_all(in_halo(h_r), g_hr, 0, every(rad_r[...], 0), top, n_rows, post_a, 2)
    collide_far(h_l, 19, 1, g_hl, 0, top, every(rad_l[...], 0), n_rows, post_a, 0)
    collide_far(h_r, 19, -1, g_hr, 1, top, every(rad_r[...], 0), n_rows, post_a, 3)
    held = {0: (post_a, 0), 1: (post_a, 1), 6: (post_a, 2), 7: (post_a, 3)}
    held |= {2 + k: (own_a, k) for k in range(4)}
    own = every(rad[...], 1)
    shear_a = shear_in[...]
    shear_b = jnp.zeros((TILE, LANES), F32)
    advance(held, 1, g_hl, 1, links_in, bits_in, every(rad_l[...], 1), skip, 1, post_b, 0)
    advance(held, 6, g_hr, 0, links_in, bits_in, every(rad_r[...], 1), skip, -1, post_b, 3)
    shear_a += advance(held, 2, g_a, 0, links_in, bits_in, own, skip, None, post_b, 1)
    shear_a += advance(held, 5, g_b, 1, links_in, bits_in, own, skip, None, post_b, 2)
    held = {1: (post_b, 0), 2: (post_b, 1), 3: (own_b, 0), 4: (own_b, 1), 5: (post_b, 2), 6: (post_b, 3)}
    own = pl.ds(TILE, TILE)
    for column in range(2, 6):
        part, x = divmod(column, 2)
        f = pulled(held, column, PAD + (MID - TILE) // 2, bits_in[column - 1, own, :])
        _, u = moments(f, field(fields[part], 0, x, TILE) > 0.0)
        shear_b += by_unit(links_in[column - 2, own, :] * square(u), field(fields[part], 4, x, TILE))
    store = send_off(send, send_v, sem, (shear_a, shear_b))
    for column in range(2, 6):
        part, x = divmod(column, 2)
        out = f_l if part == 1 else f_r
        for t in range(MID // TILE):
            row = (WIDE - MID) // 2 + t * TILE
            near = pl.ds(row, TILE)
            rows = pl.ds(t * TILE, TILE)
            f = pulled(held, column, PAD + t * TILE, bits_in[column - 1, near, :])
            for i in range(19):
                out[i, x, rows, :] = f[i]
            if column in ((2, 5) if last_halo else (3, 4)):
                rho, u = moments(f, field(fields[part], 0, x, row) > 0.0)
            if last_halo:
                if column == 2:
                    put_far(send_l, 0, rows, -1, f, rho, u)
                elif column == 5:
                    put_far(send_r, 0, rows, 1, f, rho, u)
            elif column == 2:
                put_all(send_l, rows, f)
            elif column == 3:
                put_far(send_l, 19, rows, -1, f, rho, u)
            elif column == 4:
                put_far(send_r, 19, rows, 1, f, rho, u)
            else:
                put_all(send_r, rows, f)
    store.wait()


def last_kernel(h_l, h_r, g_hl, g_a, g_b, g_hr, bits_in, rad_l, rad_r, own_post, density, velocity, post):
    fields = g_hl, g_a, g_b, g_hr = fields_of(g_hl, g_a, g_b, g_hr)
    top = (WIDE - MID) // 2
    collide_far(h_l, 0, 1, g_hl, 1, top, every(rad_l[...], 0), MID, post, 0)
    collide_far(h_r, 0, -1, g_hr, 0, top, every(rad_r[...], 0), MID, post, 1)
    held = {1: (post, 0), 6: (post, 1)} | {2 + k: (own_post, k) for k in range(4)}
    own = pl.ds(TILE, TILE)
    for column in range(2, 6):
        part, x = divmod(column, 2)
        f = pulled(held, column, PAD + (MID - TILE) // 2, bits_in[column - 1, own, :])
        rho, u = moments(f, field(fields[part], 0, x, TILE) > 0.0)
        density[column - 2] = rho
        for k in range(3):
            velocity[k, column - 2] = u[k]


def call(kernel, outs, scratch=(), scalars=0, mib=1, plain_out=False, aliases=(), hbm_out=None):
    vmem = pl.BlockSpec(memory_space=pltpu.VMEM)
    smem = pl.BlockSpec(memory_space=pltpu.SMEM)

    def run(*args):
        args = args[:scalars] + tuple(
            pltpu.with_memory_space_constraint(a, pltpu.VMEM) for a in args[scalars:]
        )
        held = jax.ShapeDtypeStruct if plain_out else pltpu.VMEM
        return pl.pallas_call(
            kernel,
            out_shape=[
                (jax.ShapeDtypeStruct if n == hbm_out else held)(shape, dtype) for n, (shape, dtype) in enumerate(outs)
            ],
            in_specs=[smem] * scalars + [vmem] * (len(args) - scalars),
            out_specs=[pl.BlockSpec(memory_space=pl.ANY) if n == hbm_out else vmem for n in range(len(outs))],
            scratch_shapes=[pltpu.VMEM(shape, dtype) for shape, dtype in scratch]
            + ([] if hbm_out is None else [pltpu.VMEM(*outs[hbm_out]), pltpu.SemaphoreType.DMA]),
            input_output_aliases=dict(aliases),
            compiler_params=pltpu.CompilerParams(vmem_limit_bytes=mib << 20),
        )(*args)

    return run


def step_all(density, velocity, fluid_mask, unit_of_column, radius_base):
    count = lax.axis_size(GY)
    place = lax.axis_index(GY)
    at_x = lax.axis_index("gx")
    edge = jnp.stack([at_x > 0, at_x < lax.axis_size("gx") - 1]).astype(jnp.int32)
    tile = ((TILE, LANES), F32)
    sends = ((count, TILE, LANES), F32)

    def ring(low, high):
        size = lax.axis_size("gx")
        up = [(i, (i + 1) % size) for i in range(size)]
        down = [(target, source) for source, target in up]
        before = lax.ppermute(high, "gx", up)
        after = lax.ppermute(low, "gx", down)
        return before, after

    def exchange(blocks):
        return lax.all_to_all(blocks, GY, split_axis=0, concat_axis=0, tiled=True)

    arrays = (density, velocity, fluid_mask, unit_of_column, radius_base.reshape(1, -1))
    anywhere = pl.BlockSpec(memory_space=pl.ANY)
    own, to_first, to_second, base_send = pl.pallas_call(
        gather_kernel,
        out_shape=[pltpu.VMEM((5, 4, TILE, LANES), F32)]
        + [pltpu.VMEM((Y_ROWS, LANES), F32)] * 2
        + [jax.ShapeDtypeStruct(*sends)],
        in_specs=[pl.BlockSpec(memory_space=pltpu.SMEM)] + [anywhere] * 5,
        out_specs=[pl.BlockSpec(memory_space=pltpu.VMEM)] * 3 + [anywhere],
        scratch_shapes=[pltpu.VMEM(a.shape, a.dtype) for a in arrays]
        + [pltpu.VMEM(*sends), pltpu.SemaphoreType.DMA((6,))],
        compiler_params=pltpu.CompilerParams(vmem_limit_bytes=1 << 20),
    )(place.reshape(1), *(pltpu.with_memory_space_constraint(a, pltpu.HBM) for a in arrays))
    base_in = exchange(base_send)

    def swap(start, rows):
        pairs = [(i, i + 1) for i in range(start, count - 1, 2)]
        return lax.ppermute(rows, GY, pairs + [(b, a) for a, b in pairs])

    by_first = swap(0, to_first)
    by_second = swap(1, to_second)
    pair = ((len(OWN_PLANES) * WIDE + TILE, LANES), F32)
    near_far = ((len(NEAR_FAR) * WIDE + TILE, LANES), F32)
    g_l, g_r, go_l, go_r = call(rows_kernel, [pair, pair, near_far, near_far], scalars=1)(
        (place & 1).reshape(1), by_first, own, by_second, base_in
    )
    g_hl, g_hr = ring(go_l, go_r)
    fields = (g_hl, g_l, g_r, g_hr)

    def posts(columns, rows):
        return ((19, columns, rows + 2 * PAD, LANES), F32)

    def opens(columns):
        return ((3, columns, WIDE + 2 * PAD, LANES), jnp.int32)

    def populations(rows):
        return [((19, 2, rows, LANES), F32)] * 2

    def halos(rows, last=False):
        return [((FAR if last else 19 + FAR, rows, LANES), F32)] * 2

    shared = [
        *populations(WIDE),
        *halos(WIDE),
        ((6, WIDE, LANES), jnp.int32),
        ((4, WIDE, LANES), F32),
    ]
    post_own, open_own, *begun, sums = call(
        first_own_kernel, [posts(4, WIDE), opens(4), *shared, ((3, TILE, LANES), F32)]
    )(g_l, g_r)
    f_l, f_r, send_l, send_r, bits, links, send, base = call(
        first_kernel,
        [*shared, sends, tile],
        [posts(2, WIDE), opens(4)],
        scalars=1,
        mib=3,
        hbm_out=6,
        aliases=[(8 + k, k) for k in range(6)],
    )(edge, *fields, post_own, open_own, sums, *begun)

    for turn in range(3):
        gathered = exchange(send)
        h_l, h_r = ring(send_l, send_r)
        if turn == 0:
            rad, link_tile = call(response_kernel, [tile, tile])(gathered, base, base)
        else:
            (rad,) = call(response_kernel, [tile])(gathered, base, link_tile)
        rad_l, rad_r = ring(rad, rad)
        if turn < 2:
            rows = WIDE if turn == 0 else MID
            own_part = call(
                functools.partial(two_own_kernel, n_rows=rows), [posts(4, rows), posts(2, MID), tile]
            )(f_l, f_r, g_l, g_r, bits, links, rad)
            f_l, f_r, send_l, send_r, send = call(
                functools.partial(two_steps_kernel, n_rows=rows, last_halo=turn == 1),
                [*populations(MID), *halos(MID, last=turn == 1), sends],
                [posts(4, rows), posts(4, MID)],
                mib=4,
                hbm_out=4,
            )(h_l, h_r, *fields, bits, links, rad, rad_l, rad_r, *own_part)
    (own_post,) = call(functools.partial(own_kernel, n_rows=MID, row=0), [posts(4, MID)])(
        f_l, f_r, g_l, g_r, rad
    )
    density_out, velocity_out = call(
        last_kernel,
        [((4, TILE, LANES), F32), ((3, 4, TILE, LANES), F32)],
        [posts(2, MID)],
        mib=2,
        plain_out=True,
    )(h_l, h_r, *fields, bits, rad_l, rad_r, own_post)
    own_radius = lax.dynamic_slice_in_dim(rad[1], place * UNIT_DEV, UNIT_DEV)
    return density_out, velocity_out, own_radius


def solution(mesh):
    finer = Mesh(mesh.devices.reshape(mesh.shape["gx"], 4, -1), ("gx", "gy_0", "gy_1"))
    placed = (P("gx", GY, None), P(None, "gx", GY, None), P("gx", GY, None), P("gx", GY), P(GX_GY))
    return jax.shard_map(
        step_all,
        mesh=finer,
        in_specs=placed,
        out_specs=(P("gx", GY, None), P(None, "gx", GY, None), P(GX_GY)),
        check_vma=False,
    )
```
